32 devices in a mesh: group: 16 (over z, y, core), tp: 2 (over x).
Axes of the slice: x: 2, y: 2, z: 4, core: 2. Of those that a mesh axis runs over, the one named last changes fastest.
Arguments:
- tokens: bfloat16 [8192, 3200], P('group', 'tp'), may hold values from -6 to 6
- norm_gain: bfloat16 [3200], P('tp'), may hold values from 0.25 to 1.75
- w_qkv: bfloat16 [3200, 3, 2048], P('group', None, 'tp'), may hold values from -1 to 1, as said below
- qk_gain: float32 [2, 2048], P(None, 'tp'), may hold values from 0.5 to 8
- w_out: bfloat16 [2048, 3200], P('tp', 'group'), may hold values from -0.125 to 0.125
- layer_scale: float32 [3200], P('tp'), may hold values from 0.3 to 1.5
- request: int32 [8192], P('group'), may hold values from 0 to 8191, as said below
- owner: int32 [8192, 1], P('group'), may hold values from 0 to 15; in each aligned block of 512 rows (0 to 511, 512 to 1023, ...) at most 64 rows name the same one
Outputs:
- routed: bfloat16 [16, 16, 64, 3200], P('group', None, None, 'tp')
The draws below stay inside these ranges and needn't reach their ends.
Inputs may be any that keep to these rules, and one draw needn't show every extreme that they name: Requests never cross a block of 1024 rows starting at a multiple of 1024, and blocks share none; in each such block exactly one request holds rows on both sides of its middle, at most 128 on each side, exactly 128 on each side in the first block; the first row's number is 0 and the last row's is 8191. Among one group's 512 rows at most 64 name the same owner; some owner is named by exactly 64 rows of some group. `w_qkv`: column scales of the projections vary across the columns.
All inputs are finite; a program needn't handle non-finite values.
Results may differ from the reference program's by a relative error of at most 0.0117.
The reference program's roundings to bfloat16 on the way count: a program that leaves them out, or rounds other values in their place, can miss the bound.
Values may be sent and summed in bfloat16 or wider, within the bound.
A program may use at most 128 MiB of HBM per device.

```python
import math
import jax
import jax.numpy as jnp
import numpy as np
from jax import lax

D = 3200
HD = 128
HEADS = 16
ROWS = 512
SHARE = 128
CAP = 64
TOKENS = 8192
N_GROUP = 16
N_TP = 2


def draw_w_qkv(key, part):
    width = HEADS * HD
    base = jax.random.truncated_normal(key, -6.0, 6.0, (D, 3, width), jnp.float32)
    column = jnp.arange(width, dtype=jnp.float32) / (width - 1)
    scale = 0.6 + 1.2 * column
    values = base * D ** (-0.5) * scale[None, None, :]
    return jnp.clip(values, -1.0, 1.0).astype(jnp.bfloat16)


def draw_qk_gain(key, part):
    width = HEADS * HD
    unit = jax.random.uniform(key, (2, width), jnp.float32)
    return 0.5 + unit


def draw_request(key, part):
    pairs = N_GROUP // 2
    block = 2 * ROWS
    gap = max(4, ROWS // 3)
    key_cut = jax.random.fold_in(key, 11)
    key_left = jax.random.fold_in(key, 12)
    key_right = jax.random.fold_in(key, 13)
    flags = (jax.random.randint(key_cut, (pairs, block), 0, gap) == 0).astype(jnp.int32)
    position = jnp.arange(block, dtype=jnp.int32)[None, :]
    left = jax.random.randint(key_left, (pairs, 1), 1, SHARE + 1)
    right = jax.random.randint(key_right, (pairs, 1), 1, SHARE + 1)
    left = left.at[0].set(SHARE)
    right = right.at[0].set(SHARE)
    lower = ROWS - left
    upper = ROWS + right
    flags = jnp.where((position > lower) & (position < upper), 0, flags)
    flags = jnp.where((position == lower) | (position == upper), 1, flags)
    flags = flags.at[:, 0].set(0)
    ordinal = jnp.cumsum(flags, axis=1)
    total = ordinal[:, -1:]
    backward = block - 1 - (total - ordinal)
    pair_index = jnp.arange(pairs, dtype=jnp.int32)[:, None]
    local_ids = jnp.where(pair_index == 0, ordinal, backward)
    ids = pair_index * block + local_ids
    return ids.reshape(-1).astype(jnp.int32)


def block_levels(stream_key, dims, split, smallest, top_value):
    factor_of, own = 1.0, jax.random.fold_in(stream_key, 6)
    for dim, parts in split:
        steps = jnp.exp(jax.random.uniform(jax.random.fold_in(own, dim), (parts,), jnp.float32, smallest / len(split), top_value / len(split)))
        factor_of = factor_of * jnp.repeat(steps, dims[dim] // parts).reshape([-1 if axis == dim else 1 for axis in range(len(dims))])
    return factor_of


def routed_block(key, own, number, rows, count, top, most, slope):
    order = jax.random.permutation(key, count)
    crowded, usual = shares(count, rows * top, most, slope, True), shares(count, rows * top, most, slope, False)
    places = jnp.arange(count)

    def named(tallies, offset_by):
        used = int((tallies > 0).sum())
        fixed = max(1, used // 4)
        shifted = fixed + (places - fixed + offset_by * (used - fixed)) % max(1, count - fixed)
        return jnp.zeros((count,), jnp.int32).at[order[jnp.where(places < fixed, places, shifted)]].set(jnp.asarray(tallies, jnp.int32))

    tallies = jnp.where(number % 4 == 0, named(crowded, number // 4), named(usual, number - number // 4 - 1))
    mixed = jax.random.permutation(jax.random.fold_in(own, 3), count)
    source_of, sink = mixed[0:count // 2 * 2:2], mixed[1:count // 2 * 2:2]
    room = jnp.minimum(tallies[source_of] - 1, most - tallies[sink]) // 2
    room = jnp.where((source_of == order[0]) | (sink == order[0]) | (tallies[sink] == 0), 0, jnp.maximum(room, 0))
    shifted = jax.random.randint(jax.random.fold_in(own, 4), (count // 2,), 0, 1 << 20) % (room + 1)
    tallies = tallies.at[source_of].add(-shifted).at[sink].add(shifted)
    labels = jnp.searchsorted(jnp.cumsum(tallies), jnp.arange(rows * top), side="right").astype(jnp.int32)
    grid = labels.reshape(top, rows).T
    grid = grid[jax.random.permutation(jax.random.fold_in(own, 1), rows)]
    offset_by = jax.random.randint(jax.random.fold_in(own, 2), (rows, 1), 0, top)
    return jnp.take_along_axis(grid, (jnp.arange(top)[None, :] + offset_by) % top, axis=1)


def shares(count, total, bound, slope, full):
    weights = [(1 << 20) // math.isqrt(grade ** slope) + 1 for grade in range(1, count + 1)]
    largest = bound if full else min(bound, max(-(-total // count), total * weights[0] // sum(weights)))
    least = 1 if total - largest >= count - 1 else 0
    counts, rest = [largest] + [least] * (count - 1), total - largest - least * (count - 1)
    while rest > 0:
        candidates = [i for i in range(1, count) if counts[i] < largest] or [i for i in range(1, count) if counts[i] < bound]
        mass, remaining = sum([weights[i] for i in candidates]), rest
        for i in candidates:
            extra = min(bound - counts[i], max(1, remaining * weights[i] // mass), rest)
            counts[i] = counts[i] + extra
            rest = rest - extra
    return np.array(counts)


def centred(rng, shape, deviation, most, shards=(), held_as=jnp.bfloat16):
    values = jax.random.normal(rng, shape, jnp.float32) * deviation
    if len(shards) > 0:
        values = block_levels(rng, shape, shards, -0.22, 0.18) * values
    return jnp.clip(values, min=-most, max=most).astype(held_as)


def setup_inputs(seed: int = 0) -> dict:
    keys = jax.random.split(jax.random.key(seed), 9)
    tokens = centred(keys[0], (TOKENS, D), 1.0, 6.0, ((0, 16), (1, 2)))
    norm_gain = jnp.clip(1.0 + 0.15 * jax.random.normal(keys[1], (D,), jnp.float32), 0.25, 1.75).astype(jnp.bfloat16)
    w_qkv = draw_w_qkv(jax.random.fold_in(keys[8], 71), 0)
    qk_gain = draw_qk_gain(jax.random.fold_in(keys[8], 71), 0)
    w_out = centred(keys[4], (HEADS * HD, D), (HEADS * HD) ** -0.5, 0.125, ((0, 2), (1, 16)))
    layer_scale = jnp.clip(jnp.exp(math.log(1.5) - 1.60943787 * jax.random.uniform(keys[5], (D,), jnp.float32) ** block_levels(keys[5], (D,), ((0, 2),), -0.2, 0.2)), 0.3, 1.5)
    request = draw_request(jax.random.fold_in(keys[8], 71), 0)
    owner_keys = jax.random.split(jax.random.fold_in(keys[7], 1), TOKENS // ROWS)
    owner_turns = jax.random.permutation(jax.random.fold_in(keys[7], 3), TOKENS // ROWS)
    owner = jax.vmap(lambda own, number: routed_block(jax.random.fold_in(keys[7], 2), own, number, ROWS, N_GROUP, 1, CAP, 2))(owner_keys, owner_turns).reshape((TOKENS, 1))
    return dict(tokens=tokens, norm_gain=norm_gain, w_qkv=w_qkv, qk_gain=qk_gain, w_out=w_out, layer_scale=layer_scale, request=request, owner=owner)


def pair_rows(start, tokens, norm_gain, w_qkv, qk_gain, w_out, layer_scale, request):
    width = HEADS * HD
    block = 2 * ROWS
    rows_in = lax.dynamic_slice_in_dim(tokens, start, block, 0)
    ids = lax.dynamic_slice_in_dim(request, start, block, 0)
    xf = rows_in.astype(jnp.float32)
    stat = lax.optimization_barrier(jnp.mean(xf * xf, axis=-1, keepdims=True))
    normed = (xf * lax.rsqrt(stat + 1e-06) * norm_gain.astype(jnp.float32)).astype(jnp.bfloat16)
    qkv = jnp.dot(normed, w_qkv.reshape(D, 3 * width), preferred_element_type=jnp.float32).reshape(block, 3, width)
    query = qkv[:, 0, :]
    key_rows = qkv[:, 1, :]
    value = qkv[:, 2, :].astype(jnp.bfloat16)
    qstat = lax.optimization_barrier(jnp.mean(query * query, axis=-1, keepdims=True))
    kstat = lax.optimization_barrier(jnp.mean(key_rows * key_rows, axis=-1, keepdims=True))
    qnorm = (query * lax.rsqrt(qstat + 1e-06) * qk_gain[0]).astype(jnp.bfloat16)
    knorm = (key_rows * lax.rsqrt(kstat + 1e-06) * qk_gain[1]).astype(jnp.bfloat16)
    qh = qnorm.reshape(block, HEADS, HD).astype(jnp.float32)
    kh = knorm.reshape(block, HEADS, HD).astype(jnp.float32)
    vh = value.reshape(block, HEADS, HD).astype(jnp.float32)
    scores = jnp.einsum('qhd,khd->hqk', qh, kh) / math.sqrt(HD)
    same = ids[:, None] == ids[None, :]
    scores = jnp.where(same[None], scores, -jnp.inf)
    top = lax.optimization_barrier(jnp.max(scores, axis=-1, keepdims=True))
    expo = jnp.exp(scores - top)
    probs = (expo / lax.optimization_barrier(jnp.sum(expo, axis=-1, keepdims=True))).astype(jnp.bfloat16)
    attended = jnp.einsum('hqk,khd->qhd', probs.astype(jnp.float32), vh).astype(jnp.bfloat16).reshape(block, width)
    local = width // N_TP
    branch = jnp.zeros((block, D), jnp.float32)
    for piece_index in range(N_TP):
        lo = piece_index * local
        part = jnp.dot(attended[:, lo:lo + local], w_out[lo:lo + local], preferred_element_type=jnp.float32).astype(jnp.bfloat16)
        part = lax.optimization_barrier(part)
        branch = branch + part.astype(jnp.float32)
    return (xf + layer_scale * branch).astype(jnp.bfloat16)

def reference(tokens, norm_gain, w_qkv, qk_gain, w_out, layer_scale, request, owner):
    pairs = N_GROUP // 2
    starts = jnp.arange(pairs, dtype=jnp.int32) * (2 * ROWS)
    mixed = lax.map(lambda s: pair_rows(s, tokens, norm_gain, w_qkv, qk_gain, w_out, layer_scale, request), starts)
    mixed = mixed.reshape(N_GROUP, ROWS, D)
    own = owner[:, 0].reshape(N_GROUP, ROWS)
    onehot = (own[:, :, None] == jnp.arange(N_GROUP, dtype=jnp.int32)[None, None, :]).astype(jnp.int32)
    slot = lax.optimization_barrier(jnp.sum((jnp.cumsum(onehot, axis=1) - onehot) * onehot, axis=-1))
    source = jnp.broadcast_to(jnp.arange(N_GROUP, dtype=jnp.int32)[:, None], (N_GROUP, ROWS))
    routed = jnp.zeros((N_GROUP, N_GROUP, CAP, D), jnp.bfloat16)
    routed = routed.at[source, own, slot].set(mixed)
    return jnp.transpose(routed, (1, 0, 2, 3))
```

```python
import math

import jax
import jax.numpy as jnp
from jax import lax
from jax.experimental import pallas as pl
from jax.experimental.pallas import tpu as pltpu
from jax.sharding import PartitionSpec as P

HD = 128
SHARE = 128


def swapped(value, axis, apart):
    mask = 2**apart
    pairs = [(source, source ^ mask) for source in range(lax.axis_size(axis))]
    return lax.ppermute(value, axis, pairs)


def from_next(value, axis):
    count = lax.axis_size(axis)
    return lax.ppermute(value, axis, [((i + 1) % count, i) for i in range(count)])


def attend_kernel(q_ref, k_ref, v_ref, kp_ref, vp_ref, row_ref, own_ref, pair_ref, out_ref):
    query = q_ref[...]
    over = (((1,), (1,)), ((), ()))
    scale = 1.0 / math.sqrt(HD)
    near = lax.dot_general(query, k_ref[...], over, preferred_element_type=jnp.float32) * scale
    far = lax.dot_general(query, kp_ref[...], over, preferred_element_type=jnp.float32) * scale
    near = jnp.where(row_ref[...] == own_ref[...], near, -jnp.inf)
    far = jnp.where(row_ref[...] == pair_ref[...], far, -jnp.inf)
    top = jnp.maximum(
        jnp.max(near, axis=-1, keepdims=True), jnp.max(far, axis=-1, keepdims=True)
    )
    near, far = jnp.exp(near - top), jnp.exp(far - top)
    share = 1.0 / (jnp.sum(near, axis=-1, keepdims=True) + jnp.sum(far, axis=-1, keepdims=True))
    near, far = (near * share).astype(jnp.bfloat16), (far * share).astype(jnp.bfloat16)
    total = jnp.dot(near, v_ref[...], preferred_element_type=jnp.float32)
    total += jnp.dot(far, vp_ref[...], preferred_element_type=jnp.float32)
    out_ref[...] = total.astype(jnp.bfloat16)


def attend(query, keys, values, paired_keys, paired_values, ids, paired_ids):
    rows, width = query.shape
    seam = paired_keys.shape[0]
    block = pl.BlockSpec((rows, HD), lambda h: (0, h))
    seam_block = pl.BlockSpec((seam, HD), lambda h: (0, h))
    fixed = lambda shape: pl.BlockSpec(shape, lambda h: (0, 0))
    return pl.pallas_call(
        attend_kernel,
        grid=(width // HD,),
        out_shape=jax.ShapeDtypeStruct((rows, width), jnp.bfloat16),
        in_specs=[
            block, block, block, seam_block, seam_block,
            fixed((rows, 1)), fixed((1, rows)), fixed((1, seam)),
        ],
        out_specs=block,
        compiler_params=pltpu.CompilerParams(vmem_limit_bytes=32 * 2**20),
        cost_estimate=pl.CostEstimate(
            flops=4 * rows * (rows + seam) * width,
            transcendentals=rows * (rows + seam) * width // HD,
            bytes_accessed=8 * rows * width,
        ),
    )(
        query, keys, values, paired_keys, paired_values,
        ids[:, None], ids[None, :], paired_ids[None, :],
    )


def route_kernel(count, place_ref, mixed_ref, out_ref, outbox, send_sem, recv_sem, keep_sem):
    me = lax.axis_index("group")
    capacity = outbox.shape[1]
    rows = mixed_ref.shape[0]
    barrier = pltpu.get_barrier_semaphore()

    @pl.loop(1, count)
    def _(step):
        pl.semaphore_signal(
            barrier, inc=1, device_id={"group": lax.rem(me + step, count)},
            device_id_type=pl.DeviceIdType.MESH,
        )

    pl.semaphore_wait(barrier, count - 1)

    def pick(owner):
        slots = lax.broadcasted_iota(jnp.int32, (capacity, rows), 0) + owner * capacity
        select = (slots == place_ref[...]).astype(jnp.float32).astype(jnp.bfloat16)
        return jnp.dot(select, mixed_ref[...], preferred_element_type=jnp.float32).astype(
            jnp.bfloat16
        )

    def sending(step):
        ahead = 1 + lax.rem(step - 1 + count // 2 - 1, count - 1)
        peer = lax.rem(me + ahead, count)
        return peer, pltpu.make_async_remote_copy(
            src_ref=outbox.at[step],
            dst_ref=out_ref.at[me],
            send_sem=send_sem.at[step],
            recv_sem=recv_sem.at[me],
            device_id={"group": peer},
            device_id_type=pl.DeviceIdType.MESH,
        )

    @pl.loop(1, count)
    def _(step):
        peer, copy = sending(step)
        outbox[step] = pick(peer)
        copy.start()

    outbox[0] = pick(me)
    keep = pltpu.make_async_copy(outbox.at[0], out_ref.at[me], keep_sem)
    keep.start()

    @pl.loop(1, count)
    def _(step):
        source = lax.rem(me + step, count)
        pltpu.make_async_remote_copy(
            src_ref=outbox.at[step],
            dst_ref=out_ref.at[source],
            send_sem=send_sem.at[step],
            recv_sem=recv_sem.at[source],
            device_id={"group": source},
            device_id_type=pl.DeviceIdType.MESH,
        ).wait()

    keep.wait()


def route(place, mixed, count, capacity):
    rows, feat = mixed.shape
    return pl.pallas_call(
        lambda *refs: route_kernel(count, *refs),
        name="route",
        out_shape=jax.ShapeDtypeStruct((count, capacity, feat), jnp.bfloat16),
        in_specs=[pl.BlockSpec(memory_space=pltpu.VMEM)] * 2,
        out_specs=pl.BlockSpec(memory_space=pl.ANY),
        scratch_shapes=[
            pltpu.VMEM((count, capacity, feat), jnp.bfloat16),
            pltpu.SemaphoreType.DMA((count,)),
            pltpu.SemaphoreType.DMA((count,)),
            pltpu.SemaphoreType.DMA,
        ],
        compiler_params=pltpu.CompilerParams(
            collective_id=0, has_side_effects=True, vmem_limit_bytes=32 * 2**20
        ),
        cost_estimate=pl.CostEstimate(
            flops=2 * count * capacity * rows * feat,
            transcendentals=0,
            bytes_accessed=4 * count * capacity * feat,
        ),
    )(place[None, :], mixed)


def shards(tokens, norm_gain, w_qkv, qk_gain, w_out, layer_scale, request, owner):
    rows, feat_local = tokens.shape
    tp_count = lax.axis_size("tp")
    group_count = lax.axis_size("group")
    local_width = w_qkv.shape[2]
    head_count = local_width // HD
    me_tp = lax.axis_index("tp")
    w_all = lax.all_gather(
        w_qkv.reshape(w_qkv.shape[0], 3 * local_width), "group", axis=0, tiled=True
    )
    whole = jnp.zeros((rows, feat_local * tp_count), jnp.bfloat16)
    gain_all = jnp.zeros((1, feat_local * tp_count), jnp.bfloat16)
    piece, gain = tokens, norm_gain.reshape(1, feat_local)
    for step in range(tp_count):
        at = ((me_tp + step) % tp_count) * feat_local
        whole = lax.dynamic_update_slice(whole, piece, (0, at))
        gain_all = lax.dynamic_update_slice(gain_all, gain, (0, at))
        if step < tp_count - 1:
            piece, gain = from_next(piece, "tp"), from_next(gain, "tp")
    whole, late_out = lax.optimization_barrier((whole, w_out))
    per = group_count // tp_count
    pairs = []
    for g in range(group_count):
        for b in range(tp_count):
            t, j = g // per, g % per
            to_g = b * per + j
            pairs.append((g * tp_count + b, to_g * tp_count + t))
    w_piece = lax.ppermute(late_out.T, ("group", "tp"), pairs)
    w_o = lax.all_gather(w_piece, "group", axis=0, tiled=True)
    w_o = w_o.reshape(tp_count, feat_local, local_width)
    xwide = whole.astype(jnp.float32)
    stat = jnp.mean(xwide * xwide, axis=-1, keepdims=True)
    normed = (xwide * lax.rsqrt(stat + 1e-06) * gain_all.astype(jnp.float32)).astype(jnp.bfloat16)
    qkv = jnp.dot(normed, w_all, preferred_element_type=jnp.float32)
    query = qkv[:, :local_width]
    key_rows = qkv[:, local_width : 2 * local_width]
    value = qkv[:, 2 * local_width :].astype(jnp.bfloat16)
    qsum, ksum = lax.psum(
        (jnp.sum(query * query, axis=-1), jnp.sum(key_rows * key_rows, axis=-1)), "tp"
    )
    total_width = local_width * tp_count
    qnorm = (query * lax.rsqrt(qsum / total_width + 1e-06)[:, None] * qk_gain[0]).astype(
        jnp.bfloat16
    )
    knorm = (key_rows * lax.rsqrt(ksum / total_width + 1e-06)[:, None] * qk_gain[1]).astype(
        jnp.bfloat16
    )
    parity = lax.axis_index("group") % 2
    seam = jnp.where(parity == 0, rows - SHARE, 0).astype(jnp.int32)
    key_window = lax.dynamic_slice_in_dim(knorm, seam, SHARE, 0)
    id_window = lax.dynamic_slice_in_dim(request, seam, SHARE, 0)
    paired_keys, paired_ids = swapped((key_window, id_window), "group", 0)
    value_window = lax.dynamic_slice_in_dim(value, seam, SHARE, 0)
    paired_values = swapped(value_window, "group", 0)
    attended = attend(qnorm, knorm, value, paired_keys, paired_values, request, paired_ids)

    branch = jnp.zeros((rows, feat_local), jnp.float32)
    for step in range(tp_count):
        onward = from_next(attended, "tp") if step < tp_count - 1 else None
        part = lax.dot_general(
            attended,
            lax.dynamic_index_in_dim(w_o, (me_tp + step) % tp_count, 0, keepdims=False),
            (((1,), (1,)), ((), ())),
            preferred_element_type=jnp.float32,
        )
        branch = branch + part.astype(jnp.bfloat16).astype(jnp.float32)
        attended = onward
    mixed = (tokens.astype(jnp.float32) + layer_scale * branch).astype(jnp.bfloat16)

    capacity = max(2, 2 * rows // group_count)
    target = owner[:, 0]
    onehot = target[:, None] == jnp.arange(group_count, dtype=jnp.int32)[None, :]
    order = jnp.arange(rows, dtype=jnp.int32)
    before = (order[:, None] > order[None, :]).astype(jnp.bfloat16)
    ranks = jnp.dot(before, onehot.astype(jnp.bfloat16), preferred_element_type=jnp.float32)
    slot = jnp.sum(jnp.where(onehot, ranks, 0.0), axis=-1).astype(jnp.int32)
    place = target * capacity + slot
    inbox = route(place, mixed, group_count, capacity)
    return inbox[None]


def solution(mesh):
    in_specs = (
        P("group", "tp"),
        P("tp"),
        P("group", None, "tp"),
        P(None, "tp"),
        P("tp", "group"),
        P("tp"),
        P("group"),
        P("group", None),
    )
    out_specs = P("group", None, None, "tp")
    return jax.shard_map(shards, mesh=mesh, in_specs=in_specs, out_specs=out_specs, check_vma=False)
```

```python
import functools
import math

import jax
import jax.numpy as jnp
from jax import lax
from jax.experimental import pallas as pl
from jax.experimental.pallas import tpu as pltpu
from jax.sharding import PartitionSpec as P

HD = 128
SHARE = 128


MESH = pl.DeviceIdType.MESH
BF16 = jnp.bfloat16
F32 = jnp.float32


def to_row(column):
    spread = jnp.broadcast_to(column, (column.shape[0], 128))
    return jnp.transpose(spread)[:8]


def to_column(row):
    spread = jnp.broadcast_to(row, (128, row.shape[1]))
    return jnp.transpose(spread)[:, :1]


def front_kernel(
    levels, tokens_ref, gain_ref, w_ref, qk_gain_ref, ids_ref, out_ref,
    w_send, w_got, w_all, n_send, n_all, ids_all, sum_mine, sum_got, qk_mine, qk_got,
    qk_wide, qn, kn, vb, probs,
    ws_sem, wr_sem, is_sem, ir_sem, ss_sem, sr_sem, ns_sem, nr_sem, nf_sem, nfr_sem,
    right_sem, left_sem, chain_sem, core_s_sem, core_r_sem, qs_sem, qr_sem,
):
    group, t = lax.axis_index("group"), lax.axis_index("tp")
    z, y, c = group // 4, lax.rem(group // 2, 2), lax.rem(group, 2)
    rows, feat = tokens_ref.shape
    slab = w_all.shape[1] // (2 * levels)
    depth = w_ref.shape[1]
    cols = w_all.shape[2]
    heads = cols // HD
    part = rows * 5 // 16
    edge_r, edge_l = z < levels - 1, z > 0

    def at(zz, yy, cc):
        return (zz * 2 + yy) * 2 + cc

    def remote(src, dst, send, recv, place, tt):
        return pltpu.make_async_remote_copy(
            src_ref=src, dst_ref=dst, send_sem=send, recv_sem=recv,
            device_id={"group": place, "tp": tt}, device_id_type=MESH,
        )

    barrier = pltpu.get_barrier_semaphore()

    def greet(place, tt):
        pl.semaphore_signal(
            barrier, inc=1, device_id={"group": place, "tp": tt}, device_id_type=MESH
        )

    for k in range(8):
        dt, dy, dc = k // 4, k // 2 % 2, k % 2
        if k:
            greet(at(z, lax.rem(y + dy, 2), lax.rem(c + dc, 2)), lax.rem(t + dt, 2))

    @pl.when(edge_r)
    def _():
        greet(group + 4, t)

    @pl.when(edge_l)
    def _():
        greet(group - 4, t)

    for yy in range(2):
        w_send[yy, :, :depth, :] = w_ref[:, :, yy * cols : (yy + 1) * cols]

    pl.semaphore_wait(barrier, 7 + edge_r.astype(jnp.int32) + edge_l.astype(jnp.int32))

    def pieces(yy):
        place = at(z, yy, y)
        return (
            remote(w_send.at[yy], w_got.at[c], ws_sem.at[yy], wr_sem.at[c], place, t),
            remote(ids_ref, ids_all.at[c], is_sem.at[yy], ir_sem.at[c], place, t),
        )

    def kept(yy):
        return (
            pltpu.make_async_copy(w_send.at[yy], w_got.at[c], wr_sem.at[c]),
            pltpu.make_async_copy(ids_ref, ids_all.at[c], ir_sem.at[c]),
        )

    def is_me(yy):
        return jnp.logical_and(y == yy, c == y)

    for yy in range(2):
        @pl.when(is_me(yy))
        def _():
            for copy in kept(yy):
                copy.start()

        @pl.when(jnp.logical_not(is_me(yy)))
        def _():
            for copy in pieces(yy):
                copy.start()

    wide = tokens_ref[...].astype(F32)
    mine = jnp.sum(wide * wide, axis=-1, keepdims=True)
    sum_mine[...] = to_row(mine)
    swap = remote(sum_mine, sum_got, ss_sem, sr_sem, group, lax.rem(t + 1, 2))
    swap.start()

    for cc in range(2):
        pltpu.make_async_copy(w_send.at[0], w_got.at[cc], wr_sem.at[cc]).wait()

    def rows_of(zz, cc):
        return pl.ds(pl.multiple_of((zz * 2 + cc) * slab, 16), slab)

    def piece(j, zz, cc):
        return w_all.at[j, rows_of(zz, cc), :]

    def go_right(j, zz):
        return remote(piece(j, zz, c), piece(j, zz, c), right_sem.at[j, zz], chain_sem.at[j, zz], group + 4, t)

    def go_left(j, zz):
        return remote(piece(j, zz, c), piece(j, zz, c), left_sem.at[j, zz], chain_sem.at[j, zz], group - 4, t)

    def go_core(j, zz):
        return remote(
            piece(j, zz, c), piece(j, zz, c), core_s_sem.at[j, zz], core_r_sem.at[j, zz],
            at(z, y, 1 - c), t,
        )

    def send_own(j):
        both = jnp.concatenate(
            [w_got[0, j].astype(F32)[:depth], w_got[1, j].astype(F32)[:depth]], axis=0
        )
        w_all[j, rows_of(z, c), :] = both.astype(BF16)

        @pl.when(edge_r)
        def _():
            go_right(j, z).start()

        @pl.when(edge_l)
        def _():
            go_left(j, z).start()

        go_core(j, z).start()

    def arrive(j, d):
        @pl.when(z - d >= 0)
        def _():
            go_right(j, z - d).wait_recv()

            @pl.when(edge_r)
            def _():
                go_right(j, z - d).start()

            go_core(j, z - d).start()

        @pl.when(z + d < levels)
        def _():
            go_left(j, z + d).wait_recv()

            @pl.when(edge_l)
            def _():
                go_left(j, z + d).start()

            go_core(j, z + d).start()

    send_own(0)
    send_own(1)

    swap.wait()
    whole = sum_mine[...] + sum_got[...]
    factor = to_column(lax.rsqrt(whole[:1] / (2 * feat) + 1e-06))
    n_send[...] = (tokens_ref[...].astype(F32) * factor * gain_ref[...].astype(F32)).astype(BF16)

    def n_rows(cc, start, size):
        return pl.ds(pl.multiple_of(cc * rows + start, 16), size)

    n_dst = n_all.at[t, n_rows(c, 0, rows), :]
    n_x = remote(n_send, n_dst, ns_sem.at[0], nr_sem.at[t, c], at(z, y, y), lax.rem(t + 1, 2))
    n_y = remote(n_send, n_dst, ns_sem.at[1], nr_sem.at[t, c], at(z, 1 - y, y), t)
    n_core = remote(n_send, n_dst, ns_sem.at[2], nr_sem.at[t, c], at(z, y, y), t)
    n_here = pltpu.make_async_copy(n_send, n_dst, nr_sem.at[t, c])
    n_x.start()
    n_y.start()

    @pl.when(c == y)
    def _():
        n_here.start()

    @pl.when(c != y)
    def _():
        n_core.start()

    def n_wait(tt, cc):
        pltpu.make_async_copy(n_send, n_all.at[tt, n_rows(cc, 0, rows), :], nr_sem.at[tt, cc]).wait()

    other_t = lax.rem(t + 1, 2)

    def forward_y(cc):
        ref = n_all.at[other_t, n_rows(cc, 0, part), :]
        return remote(ref, ref, nf_sem.at[cc], nfr_sem.at[0, cc], at(z, 1 - y, c), t)

    def forward_x(cc):
        ref = n_all.at[t, n_rows(cc, part, rows - part), :]
        return remote(ref, ref, nf_sem.at[cc], nfr_sem.at[1, cc], group, other_t)

    arrive(0, 1)
    arrive(1, 1)
    send_own(2)

    for cc in range(2):
        @pl.when(c == y)
        def _():
            n_wait(other_t, cc)
            forward_y(cc).start()

        @pl.when(c != y)
        def _():
            n_wait(t, cc)
            forward_x(cc).start()

    arrive(0, 2)
    arrive(1, 2)
    arrive(2, 1)
    for d in range(3, levels):
        arrive(0, d)
        arrive(1, d)
        arrive(2, d - 1)

    for cc in range(2):
        @pl.when(c == y)
        def _():
            n_wait(t, cc)

        @pl.when(c != y)
        def _():
            for way, (start, size) in enumerate(((0, part), (part, rows - part))):
                ref = n_all.at[other_t, n_rows(cc, start, size), :]
                pltpu.make_async_copy(ref, ref, nfr_sem.at[way, cc]).wait()

    def core_wait(j):
        for zz in range(levels):
            remote(
                piece(j, zz, 1 - c), piece(j, zz, 1 - c), core_s_sem.at[j, zz], core_r_sem.at[j, zz],
                at(z, y, 1 - c), t,
            ).wait_recv()

    def project(j, start, size):
        out = jnp.dot(n_all[0, pl.ds(start, size), :], w_all[j, :feat, :], preferred_element_type=F32)
        for tt in range(1, 2):
            out += jnp.dot(
                n_all[tt, pl.ds(start, size), :], w_all[j, tt * feat : (tt + 1) * feat, :],
                preferred_element_type=F32,
            )
        return out

    tall = 2 * rows
    step = tall // 4
    for j in range(2):
        core_wait(j)

        @pl.loop(0, 4)
        def _(i):
            start = pl.multiple_of(i * step, step)
            out = project(j, start, step)
            qk_wide[j, pl.ds(start, step), :] = out
            qk_mine[j, :, pl.ds(start, step)] = to_row(jnp.sum(out * out, axis=-1, keepdims=True))

    def stat_swap(k):
        return remote(
            qk_mine, qk_got.at[k - 1], qs_sem.at[k - 1], qr_sem.at[k - 1],
            at(z, lax.rem(y + k % 2, 2), c), lax.rem(t + k // 2, 2),
        )

    for k in range(1, 4):
        stat_swap(k).start()
    for k in range(1, 4):
        stat_swap(k).wait()
    stats = qk_mine[...] + qk_got[0] + qk_got[1] + qk_got[2]
    factors = lax.rsqrt(stats / (4 * cols) + 1e-06)
    for j, ref in ((0, qn), (1, kn)):
        column = to_column(factors[j, :1])
        near = qk_gain_ref[j : j + 1, :cols]
        far = qk_gain_ref[j : j + 1, cols:]
        gains = jnp.where(y == 0, near, far)
        ref[...] = (qk_wide[j] * column * gains).astype(BF16)

    for cc in range(2):
        pltpu.make_async_copy(ids_ref, ids_all.at[cc], ir_sem.at[cc]).wait()
    seam = rows + SHARE
    scale = 1.0 / math.sqrt(HD)
    ids = jnp.concatenate([ids_all[0, :1], ids_all[1, :1]], axis=1)
    for half in range(2):
        first = half * (rows - SHARE)
        same = to_column(ids[:, half * rows : (half + 1) * rows]) == ids[:, first : first + seam]

        @pl.loop(0, heads)
        def _(h):
            lanes = pl.ds(pl.multiple_of(h * HD, HD), HD)
            scores = lax.dot_general(
                qn[half * rows : (half + 1) * rows, lanes], kn[first : first + seam, lanes],
                (((1,), (1,)), ((), ())), preferred_element_type=F32,
            ) * scale
            scores = jnp.where(same, scores, -jnp.inf)
            expo = jnp.exp(scores - jnp.max(scores, axis=-1, keepdims=True))
            share = 1.0 / jnp.sum(expo, axis=-1, keepdims=True)
            probs[half, h] = (expo * share).astype(BF16)

    arrive(2, levels - 1)
    core_wait(2)

    @pl.loop(0, 4)
    def _(i):
        start = pl.multiple_of(i * step, step)
        vb[pl.ds(start, step), :] = project(2, start, step).astype(BF16)

    for half in range(2):
        first = half * (rows - SHARE)

        @pl.loop(0, heads)
        def _(h):
            lanes = pl.ds(pl.multiple_of(h * HD, HD), HD)
            out_ref[half * rows : (half + 1) * rows, lanes] = jnp.dot(
                probs[half, h], vb[first : first + seam, lanes], preferred_element_type=F32
            ).astype(BF16)

    for yy in range(2):
        @pl.when(jnp.logical_not(is_me(yy)))
        def _():
            for copy in pieces(yy):
                copy.wait_send()

    n_x.wait_send()
    n_y.wait_send()

    @pl.when(c != y)
    def _():
        n_core.wait_send()

    for cc in range(2):
        @pl.when(c == y)
        def _():
            forward_y(cc).wait_send()

        @pl.when(c != y)
        def _():
            forward_x(cc).wait_send()

    for j in range(3):
        for zz in range(levels):
            @pl.when(jnp.logical_and(zz <= z, edge_r))
            def _():
                go_right(j, zz).wait_send()

            @pl.when(jnp.logical_and(zz >= z, edge_l))
            def _():
                go_left(j, zz).wait_send()

            go_core(j, zz).wait_send()


def front(tokens, gain, w, qk_gain, ids, group_count):
    rows, feat = tokens.shape
    depth, width = w.shape[1], w.shape[2]
    levels, cols = group_count // 4, width // 2
    heads = cols // HD
    padded = -(-depth // 16) * 16
    seam = rows + SHARE
    dma = pltpu.SemaphoreType.DMA
    vmem = pl.BlockSpec(memory_space=pltpu.VMEM)
    return pl.pallas_call(
        functools.partial(front_kernel, levels),
        name="front",
        out_shape=jax.ShapeDtypeStruct((2 * rows, cols), BF16),
        in_specs=[vmem] * 5,
        out_specs=vmem,
        scratch_shapes=[
            pltpu.VMEM((2, 3, padded, cols), BF16),
            pltpu.VMEM((2, 3, padded, cols), BF16),
            pltpu.VMEM((3, 2 * feat, cols), BF16),
            pltpu.VMEM((rows, feat), BF16),
            pltpu.VMEM((2, 2 * rows, feat), BF16),
            pltpu.VMEM((2, 8, rows), F32),
            pltpu.VMEM((8, rows), F32),
            pltpu.VMEM((8, rows), F32),
            pltpu.VMEM((2, 8, 2 * rows), F32),
            pltpu.VMEM((3, 2, 8, 2 * rows), F32),
            pltpu.VMEM((2, 2 * rows, cols), F32),
            pltpu.VMEM((2 * rows, cols), BF16),
            pltpu.VMEM((2 * rows, cols), BF16),
            pltpu.VMEM((2 * rows, cols), BF16),
            pltpu.VMEM((2, heads, rows, seam), BF16),
            dma((2,)), dma((2,)), dma((2,)), dma((2,)), dma, dma,
            dma((3,)), dma((2, 2)), dma((2,)), dma((2, 2)),
            dma((3, levels)), dma((3, levels)), dma((3, levels)), dma((3, levels)), dma((3, levels)),
            dma((3,)), dma((3,)),
        ],
        compiler_params=pltpu.CompilerParams(
            collective_id=1, has_side_effects=True, vmem_limit_bytes=56 * 2**20
        ),
        cost_estimate=pl.CostEstimate(
            flops=12 * rows * feat * width, transcendentals=2 * heads * rows * seam,
            bytes_accessed=2 * 2**20,
        ),
    )(tokens, gain, w, qk_gain, ids)


def back_kernel(
    count, att_ref, w_ref, tokens_ref, scale_ref, place_ref, out_ref,
    att_all, select, mixed, outbox, as_sem, ar_sem, send_sem, recv_sem, keep_sem,
):
    group, t = lax.axis_index("group"), lax.axis_index("tp")
    z, y, c = group // 4, lax.rem(group // 2, 2), lax.rem(group, 2)
    rows, feat = tokens_ref.shape
    cols = att_ref.shape[1]
    capacity = out_ref.shape[1]

    def at(zz, yy, cc):
        return (zz * 2 + yy) * 2 + cc

    barrier = pltpu.get_barrier_semaphore()

    @pl.loop(1, count)
    def _(step):
        pl.semaphore_signal(
            barrier, inc=1, device_id={"group": lax.rem(group + step, count), "tp": t}, device_id_type=MESH
        )

    for k in range(4):
        pl.semaphore_signal(
            barrier, inc=1, device_id={"group": z * 4 + k, "tp": lax.rem(t + 1, 2)}, device_id_type=MESH
        )

    pl.semaphore_wait(barrier, count + 3)

    def to_peer(dt, cc):
        return pltpu.make_async_remote_copy(
            src_ref=att_ref.at[cc * rows : (cc + 1) * rows, :],
            dst_ref=att_all.at[t, :, pl.ds(pl.multiple_of(y * cols, 128), cols)],
            send_sem=as_sem.at[dt, cc], recv_sem=ar_sem.at[t, y],
            device_id={"group": at(z, c, cc), "tp": lax.rem(t + dt, 2)}, device_id_type=MESH,
        )

    def to_me(cc):
        return pltpu.make_async_copy(
            att_ref.at[cc * rows : (cc + 1) * rows, :],
            att_all.at[t, :, pl.ds(pl.multiple_of(y * cols, 128), cols)],
            ar_sem.at[t, y],
        )

    for dt in (1, 0):
        for cc in range(2):
            if dt:
                to_peer(dt, cc).start()
            else:
                mine = jnp.logical_and(y == c, c == cc)

                @pl.when(mine)
                def _():
                    to_me(cc).start()

                @pl.when(jnp.logical_not(mine))
                def _():
                    to_peer(dt, cc).start()

    slots = lax.broadcasted_iota(jnp.int32, (count * capacity, rows), 0)
    select[...] = (slots == place_ref[...]).astype(F32).astype(BF16)

    for tt in range(2):
        for yy in range(2):
            pltpu.make_async_copy(
                att_ref.at[:rows, :], att_all.at[tt, :, yy * cols : (yy + 1) * cols], ar_sem.at[tt, yy]
            ).wait()

    def sending(step):
        ahead = 1 + lax.rem(step - 1 + count // 2 - 1, count - 1)
        peer = lax.rem(group + ahead, count)
        return peer, pltpu.make_async_remote_copy(
            src_ref=outbox.at[peer], dst_ref=out_ref.at[group],
            send_sem=send_sem.at[step], recv_sem=recv_sem.at[group],
            device_id={"group": peer, "tp": t}, device_id_type=MESH,
        )

    first = 0
    while first < feat:
        size = min(640, feat - first)
        lanes = slice(first, first + size)
        total = jnp.zeros((rows, size), F32)
        for tt in range(2):
            term = lax.dot_general(
                att_all[tt], w_ref[tt, lanes, :], (((1,), (1,)), ((), ())), preferred_element_type=F32
            )
            total += term.astype(BF16).astype(F32)
        mixed[:, lanes] = (tokens_ref[:, lanes].astype(F32) + scale_ref[:, lanes] * total).astype(BF16)
        first += size

    def pick(owner):
        chosen = select[pl.ds(pl.multiple_of(owner * capacity, capacity), capacity), :]
        outbox[owner] = jnp.dot(chosen, mixed[...], preferred_element_type=F32).astype(BF16)

    @pl.loop(1, count)
    def _(step):
        peer, copy = sending(step)
        pick(peer)
        copy.start()

    pick(group)
    keep = pltpu.make_async_copy(outbox.at[group], out_ref.at[group], keep_sem)
    keep.start()

    @pl.loop(1, count)
    def _(step):
        _, copy = sending(step)
        copy.wait_send()
        source = lax.rem(group + step, count)
        pltpu.make_async_copy(outbox.at[source], out_ref.at[source], recv_sem.at[source]).wait()

    keep.wait()
    for dt in range(2):
        for cc in range(2):
            if dt:
                to_peer(dt, cc).wait_send()
            else:
                @pl.when(jnp.logical_not(jnp.logical_and(y == c, c == cc)))
                def _():
                    to_peer(dt, cc).wait_send()


def back(attended, w_o, tokens, layer_scale, place, count, capacity):
    rows, feat = tokens.shape
    cols = attended.shape[1]
    dma = pltpu.SemaphoreType.DMA
    vmem = pl.BlockSpec(memory_space=pltpu.VMEM)
    return pl.pallas_call(
        functools.partial(back_kernel, count),
        name="back",
        out_shape=jax.ShapeDtypeStruct((count, capacity, feat), BF16),
        in_specs=[vmem] * 5,
        out_specs=pl.BlockSpec(memory_space=pl.ANY),
        scratch_shapes=[
            pltpu.VMEM((2, rows, 2 * cols), BF16),
            pltpu.VMEM((count * capacity, rows), BF16),
            pltpu.VMEM((rows, feat), BF16),
            pltpu.VMEM((count, capacity, feat), BF16),
            dma((2, 2)), dma((2, 2)), dma((count,)), dma((count,)), dma,
        ],
        compiler_params=pltpu.CompilerParams(
            collective_id=2, has_side_effects=True, vmem_limit_bytes=48 * 2**20
        ),
        cost_estimate=pl.CostEstimate(
            flops=8 * rows * cols * feat + 2 * count * capacity * rows * feat, transcendentals=0,
            bytes_accessed=4 * count * capacity * feat,
        ),
    )(attended, w_o, tokens, layer_scale, place)


def swapped(value, axis, apart):
    mask = 2**apart
    pairs = [(source, source ^ mask) for source in range(lax.axis_size(axis))]
    return lax.ppermute(value, axis, pairs)


def from_next(value, axis):
    count = lax.axis_size(axis)
    return lax.ppermute(value, axis, [((i + 1) % count, i) for i in range(count)])


def attend_kernel(q_ref, k_ref, v_ref, kp_ref, vp_ref, row_ref, own_ref, pair_ref, out_ref):
    query = q_ref[...]
    over = (((1,), (1,)), ((), ()))
    scale = 1.0 / math.sqrt(HD)
    near = lax.dot_general(query, k_ref[...], over, preferred_element_type=jnp.float32) * scale
    far = lax.dot_general(query, kp_ref[...], over, preferred_element_type=jnp.float32) * scale
    near = jnp.where(row_ref[...] == own_ref[...], near, -jnp.inf)
    far = jnp.where(row_ref[...] == pair_ref[...], far, -jnp.inf)
    top = jnp.maximum(
        jnp.max(near, axis=-1, keepdims=True), jnp.max(far, axis=-1, keepdims=True)
    )
    near, far = jnp.exp(near - top), jnp.exp(far - top)
    share = 1.0 / (jnp.sum(near, axis=-1, keepdims=True) + jnp.sum(far, axis=-1, keepdims=True))
    near, far = (near * share).astype(jnp.bfloat16), (far * share).astype(jnp.bfloat16)
    total = jnp.dot(near, v_ref[...], preferred_element_type=jnp.float32)
    total += jnp.dot(far, vp_ref[...], preferred_element_type=jnp.float32)
    out_ref[...] = total.astype(jnp.bfloat16)


def attend(query, keys, values, paired_keys, paired_values, ids, paired_ids):
    rows, width = query.shape
    seam = paired_keys.shape[0]
    block = pl.BlockSpec((rows, HD), lambda h: (0, h))
    seam_block = pl.BlockSpec((seam, HD), lambda h: (0, h))
    fixed = lambda shape: pl.BlockSpec(shape, lambda h: (0, 0))
    return pl.pallas_call(
        attend_kernel,
        grid=(width // HD,),
        out_shape=jax.ShapeDtypeStruct((rows, width), jnp.bfloat16),
        in_specs=[
            block, block, block, seam_block, seam_block,
            fixed((rows, 1)), fixed((1, rows)), fixed((1, seam)),
        ],
        out_specs=block,
        compiler_params=pltpu.CompilerParams(vmem_limit_bytes=32 * 2**20),
        cost_estimate=pl.CostEstimate(
            flops=4 * rows * (rows + seam) * width,
            transcendentals=rows * (rows + seam) * width // HD,
            bytes_accessed=8 * rows * width,
        ),
    )(
        query, keys, values, paired_keys, paired_values,
        ids[:, None], ids[None, :], paired_ids[None, :],
    )


def route_kernel(count, place_ref, mixed_ref, out_ref, outbox, send_sem, recv_sem, keep_sem):
    me = lax.axis_index("group")
    capacity = outbox.shape[1]
    rows = mixed_ref.shape[0]
    barrier = pltpu.get_barrier_semaphore()

    @pl.loop(1, count)
    def _(step):
        pl.semaphore_signal(
            barrier, inc=1, device_id={"group": lax.rem(me + step, count)},
            device_id_type=pl.DeviceIdType.MESH,
        )

    pl.semaphore_wait(barrier, count - 1)

    def pick(owner):
        slots = lax.broadcasted_iota(jnp.int32, (capacity, rows), 0) + owner * capacity
        select = (slots == place_ref[...]).astype(jnp.float32).astype(jnp.bfloat16)
        return jnp.dot(select, mixed_ref[...], preferred_element_type=jnp.float32).astype(
            jnp.bfloat16
        )

    def sending(step):
        ahead = 1 + lax.rem(step - 1 + count // 2 - 1, count - 1)
        peer = lax.rem(me + ahead, count)
        return peer, pltpu.make_async_remote_copy(
            src_ref=outbox.at[step],
            dst_ref=out_ref.at[me],
            send_sem=send_sem.at[step],
            recv_sem=recv_sem.at[me],
            device_id={"group": peer},
            device_id_type=pl.DeviceIdType.MESH,
        )

    @pl.loop(1, count)
    def _(step):
        peer, copy = sending(step)
        outbox[step] = pick(peer)
        copy.start()

    outbox[0] = pick(me)
    keep = pltpu.make_async_copy(outbox.at[0], out_ref.at[me], keep_sem)
    keep.start()

    @pl.loop(1, count)
    def _(step):
        source = lax.rem(me + step, count)
        pltpu.make_async_remote_copy(
            src_ref=outbox.at[step],
            dst_ref=out_ref.at[source],
            send_sem=send_sem.at[step],
            recv_sem=recv_sem.at[source],
            device_id={"group": source},
            device_id_type=pl.DeviceIdType.MESH,
        ).wait()

    keep.wait()


def route(place, mixed, count, capacity):
    rows, feat = mixed.shape
    return pl.pallas_call(
        lambda *refs: route_kernel(count, *refs),
        name="route",
        out_shape=jax.ShapeDtypeStruct((count, capacity, feat), jnp.bfloat16),
        in_specs=[pl.BlockSpec(memory_space=pltpu.VMEM)] * 2,
        out_specs=pl.BlockSpec(memory_space=pl.ANY),
        scratch_shapes=[
            pltpu.VMEM((count, capacity, feat), jnp.bfloat16),
            pltpu.SemaphoreType.DMA((count,)),
            pltpu.SemaphoreType.DMA((count,)),
            pltpu.SemaphoreType.DMA,
        ],
        compiler_params=pltpu.CompilerParams(
            collective_id=0, has_side_effects=True, vmem_limit_bytes=32 * 2**20
        ),
        cost_estimate=pl.CostEstimate(
            flops=2 * count * capacity * rows * feat,
            transcendentals=0,
            bytes_accessed=4 * count * capacity * feat,
        ),
    )(place[None, :], mixed)


def spread_shards(tokens, norm_gain, w_qkv, qk_gain, w_out, layer_scale, request, owner):
    rows, feat_local = tokens.shape
    tp_count = lax.axis_size("tp")
    group_count = lax.axis_size("group")
    local_width = w_qkv.shape[2]
    head_count = local_width // HD
    me_tp = lax.axis_index("tp")
    w_all = lax.all_gather(
        w_qkv.reshape(w_qkv.shape[0], 3 * local_width), "group", axis=0, tiled=True
    )
    whole = jnp.zeros((rows, feat_local * tp_count), jnp.bfloat16)
    gain_all = jnp.zeros((1, feat_local * tp_count), jnp.bfloat16)
    piece, gain = tokens, norm_gain.reshape(1, feat_local)
    for step in range(tp_count):
        at = ((me_tp + step) % tp_count) * feat_local
        whole = lax.dynamic_update_slice(whole, piece, (0, at))
        gain_all = lax.dynamic_update_slice(gain_all, gain, (0, at))
        if step < tp_count - 1:
            piece, gain = from_next(piece, "tp"), from_next(gain, "tp")
    whole, late_out = lax.optimization_barrier((whole, w_out))
    per = group_count // tp_count
    pairs = []
    for g in range(group_count):
        for b in range(tp_count):
            t, j = g // per, g % per
            to_g = b * per + j
            pairs.append((g * tp_count + b, to_g * tp_count + t))
    w_piece = lax.ppermute(late_out.T, ("group", "tp"), pairs)
    w_o = lax.all_gather(w_piece, "group", axis=0, tiled=True)
    w_o = w_o.reshape(tp_count, feat_local, local_width)
    xwide = whole.astype(jnp.float32)
    stat = jnp.mean(xwide * xwide, axis=-1, keepdims=True)
    normed = (xwide * lax.rsqrt(stat + 1e-06) * gain_all.astype(jnp.float32)).astype(jnp.bfloat16)
    qkv = jnp.dot(normed, w_all, preferred_element_type=jnp.float32)
    query = qkv[:, :local_width]
    key_rows = qkv[:, local_width : 2 * local_width]
    value = qkv[:, 2 * local_width :].astype(jnp.bfloat16)
    qsum, ksum = lax.psum(
        (jnp.sum(query * query, axis=-1), jnp.sum(key_rows * key_rows, axis=-1)), "tp"
    )
    total_width = local_width * tp_count
    qnorm = (query * lax.rsqrt(qsum / total_width + 1e-06)[:, None] * qk_gain[0]).astype(
        jnp.bfloat16
    )
    knorm = (key_rows * lax.rsqrt(ksum / total_width + 1e-06)[:, None] * qk_gain[1]).astype(
        jnp.bfloat16
    )
    parity = lax.axis_index("group") % 2
    seam = jnp.where(parity == 0, rows - SHARE, 0).astype(jnp.int32)
    key_window = lax.dynamic_slice_in_dim(knorm, seam, SHARE, 0)
    id_window = lax.dynamic_slice_in_dim(request, seam, SHARE, 0)
    paired_keys, paired_ids = swapped((key_window, id_window), "group", 0)
    value_window = lax.dynamic_slice_in_dim(value, seam, SHARE, 0)
    paired_values = swapped(value_window, "group", 0)
    attended = attend(qnorm, knorm, value, paired_keys, paired_values, request, paired_ids)

    branch = jnp.zeros((rows, feat_local), jnp.float32)
    for step in range(tp_count):
        onward = from_next(attended, "tp") if step < tp_count - 1 else None
        part = lax.dot_general(
            attended,
            lax.dynamic_index_in_dim(w_o, (me_tp + step) % tp_count, 0, keepdims=False),
            (((1,), (1,)), ((), ())),
            preferred_element_type=jnp.float32,
        )
        branch = branch + part.astype(jnp.bfloat16).astype(jnp.float32)
        attended = onward
    mixed = (tokens.astype(jnp.float32) + layer_scale * branch).astype(jnp.bfloat16)

    capacity = max(2, 2 * rows // group_count)
    target = owner[:, 0]
    onehot = target[:, None] == jnp.arange(group_count, dtype=jnp.int32)[None, :]
    order = jnp.arange(rows, dtype=jnp.int32)
    before = (order[:, None] > order[None, :]).astype(jnp.bfloat16)
    ranks = jnp.dot(before, onehot.astype(jnp.bfloat16), preferred_element_type=jnp.float32)
    slot = jnp.sum(jnp.where(onehot, ranks, 0.0), axis=-1).astype(jnp.int32)
    place = target * capacity + slot
    inbox = route(place, mixed, group_count, capacity)
    return inbox[None]


def gathered_out(w_out, group_count, tp_count, feat_local):
    per = group_count // tp_count
    pairs = []
    for g in range(group_count):
        for b in range(tp_count):
            to_g = b * per + g % per
            pairs.append((g * tp_count + b, to_g * tp_count + g // per))
    w_piece = lax.ppermute(w_out.T, ("group", "tp"), pairs)
    w_o = lax.all_gather(w_piece, "group", axis=0, tiled=True)
    return w_o.reshape(tp_count, feat_local, w_out.shape[0])


def places(owner, rows, group_count, capacity):
    target = owner[:, 0]
    onehot = target[:, None] == jnp.arange(group_count, dtype=jnp.int32)[None, :]
    order = jnp.arange(rows, dtype=jnp.int32)
    before = (order[:, None] > order[None, :]).astype(jnp.bfloat16)
    ranks = jnp.dot(before, onehot.astype(jnp.bfloat16), preferred_element_type=jnp.float32)
    slot = jnp.sum(jnp.where(onehot, ranks, 0.0), axis=-1).astype(jnp.int32)
    return target * capacity + slot


def plane_shards(tokens, norm_gain, w_qkv, qk_gain, w_out, layer_scale, request, owner):
    rows, feat = tokens.shape
    count = lax.axis_size("group")
    capacity = max(2, 2 * rows // count)
    place = places(owner, rows, count, capacity)
    w_o = gathered_out(w_out, count, lax.axis_size("tp"), feat)
    ids = jnp.broadcast_to(request.astype(F32)[None, :], (8, rows))
    attended = front(tokens, norm_gain[None, :], w_qkv.transpose(1, 0, 2), qk_gain, ids, count)
    return back(attended, w_o, tokens, layer_scale[None, :], place[None, :], count, capacity)[None]


def shards(*arrays):
    w_qkv = arrays[2]
    count, tp = lax.axis_size("group"), lax.axis_size("tp")
    whole_tiles = 2 * w_qkv.shape[0] % 16 == 0 and w_qkv.shape[2] % (2 * HD) == 0
    if tp == 2 and count % 4 == 0 and count >= 12 and whole_tiles:
        return plane_shards(*arrays)
    return spread_shards(*arrays)


def solution(mesh):
    in_specs = (
        P("group", "tp"),
        P("tp"),
        P("group", None, "tp"),
        P(None, "tp"),
        P("tp", "group"),
        P("tp"),
        P("group"),
        P("group", None),
    )
    out_specs = P("group", None, None, "tp")
    return jax.shard_map(shards, mesh=mesh, in_specs=in_specs, out_specs=out_specs, check_vma=False)
```

```python
import functools
import math

import jax
import jax.numpy as jnp
from jax import lax
from jax.experimental import pallas as pl
from jax.experimental.pallas import tpu as pltpu
from jax.sharding import PartitionSpec as P

HD = 128
SHARE = 128


SPLIT = True
MESH = pl.DeviceIdType.MESH
BF16 = jnp.bfloat16
F32 = jnp.float32


def to_row(column):
    spread = jnp.broadcast_to(column, (column.shape[0], 128))
    return jnp.transpose(spread)[:8]


def to_column(row):
    spread = jnp.broadcast_to(row, (128, row.shape[1]))
    return jnp.transpose(spread)[:, :1]


def plane_kernel(
    levels, turned_ref, gain_ref, w_ref, qk_gain_ref, wo_ref, scale_ref, request_ref, owner_ref, out_ref,
    tokens_ref, ids_ref, w_send, w_got, w_all, n_send, n_all, ids_all, sum_mine, sum_got, qk_mine, qk_got,
    qk_wide, qn, kn, vb, probs, att, wo_send, wo_got, wo_line, wo_all, att_all, mixed, outbox,
    ws_sem, wr_sem, is_sem, ir_sem, ss_sem, sr_sem, ns_sem, nr_sem, nf_sem, nfr_sem,
    right_sem, left_sem, chain_sem, core_s_sem, core_r_sem, qs_sem, qr_sem,
    wos_sem, wor_sem, uright_sem, uleft_sem, uchain_sem, uhere_sem, ux_sem, uxr_sem, uy_sem, uyr_sem, uc_sem, ucr_sem,
    as_sem, ar_sem, send_sem, recv_sem, keep_sem,
):
    group, t = lax.axis_index("group"), lax.axis_index("tp")
    z, y, c = group // 4, lax.rem(group // 2, 2), lax.rem(group, 2)
    rows, feat = tokens_ref.shape
    count, capacity = out_ref.shape[:2]
    slab = w_all.shape[1] // (2 * levels)
    depth = w_ref.shape[1]
    cols = w_all.shape[2]
    heads = cols // HD
    sub = rows // 2
    part = sub // 4
    edge_r, edge_l = z < levels - 1, z > 0

    def at(zz, yy, cc):
        return (zz * 2 + yy) * 2 + cc

    def remote(src, dst, send, recv, place, tt):
        return pltpu.make_async_remote_copy(
            src_ref=src, dst_ref=dst, send_sem=send, recv_sem=recv,
            device_id={"group": place, "tp": tt}, device_id_type=MESH,
        )

    barrier = pltpu.get_barrier_semaphore()

    @pl.loop(1, count)
    def _(step):
        pl.semaphore_signal(
            barrier, inc=1, device_id={"group": lax.rem(group + step, count), "tp": t}, device_id_type=MESH
        )

    for k in range(4):
        pl.semaphore_signal(
            barrier, inc=1, device_id={"group": z * 4 + k, "tp": lax.rem(t + 1, 2)}, device_id_type=MESH
        )

    for yy in range(2):
        w_send[yy, :, :depth, :] = w_ref[:, :, yy * cols : (yy + 1) * cols]

    half_out = wo_ref.shape[1] // 2
    for cc in range(2):
        wo_send[cc, :depth, :] = wo_ref[:, cc * half_out : (cc + 1) * half_out]
    ids_ref[...] = jnp.broadcast_to(request_ref[...].astype(F32), (8, rows))
    pl.semaphore_wait(barrier, count + 3)

    def pieces(yy):
        place = at(z, yy, y)
        copies = [
            remote(w_send.at[yy, j], w_got.at[c, j], ws_sem.at[yy, j], wr_sem.at[c, j], place, t) for j in range(3)
        ]
        return copies + [remote(ids_ref, ids_all.at[c], is_sem.at[yy], ir_sem.at[c], place, t)]

    def kept(yy):
        copies = [pltpu.make_async_copy(w_send.at[yy, j], w_got.at[c, j], wr_sem.at[c, j]) for j in range(3)]
        return copies + [pltpu.make_async_copy(ids_ref, ids_all.at[c], ir_sem.at[c])]

    def is_me(yy):
        return jnp.logical_and(y == yy, c == y)

    for yy in range(2):
        @pl.when(is_me(yy))
        def _():
            for copy in kept(yy):
                copy.start()

        @pl.when(jnp.logical_not(is_me(yy)))
        def _():
            for copy in pieces(yy):
                copy.start()

    wo_swap = remote(wo_send.at[1 - c], wo_got, wos_sem, wor_sem, at(z, y, 1 - c), t)
    wo_swap.start()

    wide = turned_ref[...].astype(F32)
    sum_mine[...] = jnp.broadcast_to(jnp.sum(wide * wide, axis=0, keepdims=True), (8, rows))
    swap = remote(sum_mine, sum_got, ss_sem, sr_sem, group, lax.rem(t + 1, 2))
    swap.start()

    def rows_of(zz, cc):
        return pl.ds(pl.multiple_of((zz * 2 + cc) * slab, 16), slab)

    def piece(j, zz, cc):
        return w_all.at[j, rows_of(zz, cc), :]

    def go_right(j, zz):
        return remote(piece(j, zz, c), piece(j, zz, c), right_sem.at[j, zz], chain_sem.at[j, zz], group + 4, t)

    def go_left(j, zz):
        return remote(piece(j, zz, c), piece(j, zz, c), left_sem.at[j, zz], chain_sem.at[j, zz], group - 4, t)

    def go_core(j, zz):
        return remote(
            piece(j, zz, c), piece(j, zz, c), core_s_sem.at[j, zz], core_r_sem.at[j, zz],
            at(z, y, 1 - c), t,
        )

    def send_own(j):
        for cc in range(2):
            pltpu.make_async_copy(w_send.at[0, j], w_got.at[cc, j], wr_sem.at[cc, j]).wait()
        both = jnp.concatenate(
            [w_got[0, j].astype(F32)[:depth], w_got[1, j].astype(F32)[:depth]], axis=0
        )
        w_all[j, rows_of(z, c), :] = both.astype(BF16)

        @pl.when(edge_r)
        def _():
            go_right(j, z).start()

        @pl.when(edge_l)
        def _():
            go_left(j, z).start()

        go_core(j, z).start()

    def arrive(j, d):
        @pl.when(z - d >= 0)
        def _():
            go_right(j, z - d).wait_recv()

            @pl.when(edge_r)
            def _():
                go_right(j, z - d).start()

            go_core(j, z - d).start()

        @pl.when(z + d < levels)
        def _():
            go_left(j, z + d).wait_recv()

            @pl.when(edge_l)
            def _():
                go_left(j, z + d).start()

            go_core(j, z + d).start()

    send_own(0)
    send_own(1)

    tokens_ref[...] = jnp.transpose(turned_ref[...].astype(F32)).astype(BF16)
    swap.wait()
    whole = sum_mine[...] + sum_got[...]
    factor = to_column(lax.rsqrt(whole[:1] / (2 * feat) + 1e-06))

    def n_rows(cc, start, size):
        return pl.ds(pl.multiple_of(cc * rows + start, 16), size)

    def n_copies(s):
        src = n_send.at[s * sub : (s + 1) * sub, :]
        dst = n_all.at[t, n_rows(c, s * sub, sub), :]
        recv = nr_sem.at[t, c, s]
        return (
            remote(src, dst, ns_sem.at[0, s], recv, at(z, y, y), lax.rem(t + 1, 2)),
            remote(src, dst, ns_sem.at[1, s], recv, at(z, 1 - y, y), t),
            remote(src, dst, ns_sem.at[2, s], recv, at(z, y, y), t),
            pltpu.make_async_copy(src, dst, recv),
        )

    for s in range(2):
        span = slice(s * sub, (s + 1) * sub)
        n_send[span, :] = (
            tokens_ref[span, :].astype(F32) * factor[span] * gain_ref[...].astype(F32)
        ).astype(BF16)
        n_x, n_y, n_core, n_here = n_copies(s)
        n_x.start()
        n_y.start()

        @pl.when(c == y)
        def _():
            n_here.start()

        @pl.when(c != y)
        def _():
            n_core.start()

    def n_wait(tt, cc, s):
        ref = n_all.at[tt, n_rows(cc, s * sub, sub), :]
        pltpu.make_async_copy(ref, ref, nr_sem.at[tt, cc, s]).wait()

    other_t = lax.rem(t + 1, 2)

    def forward_y(cc, s):
        ref = n_all.at[other_t, n_rows(cc, s * sub, part), :]
        return remote(ref, ref, nf_sem.at[cc, s], nfr_sem.at[0, cc, s], at(z, 1 - y, c), t)

    def forward_x(cc, s):
        ref = n_all.at[t, n_rows(cc, s * sub + part, sub - part), :]
        return remote(ref, ref, nf_sem.at[cc, s], nfr_sem.at[1, cc, s], group, other_t)

    def n_forward(s):
        for cc in range(2):
            @pl.when(c == y)
            def _():
                n_wait(other_t, cc, s)
                forward_y(cc, s).start()

            @pl.when(c != y)
            def _():
                n_wait(t, cc, s)
                forward_x(cc, s).start()

    half_levels = levels // 2
    lanes_out = wo_all.shape[2] // 2

    def u_at(tt, i, yy, cc):
        return wo_all.at[
            tt, pl.ds(pl.multiple_of((i * 2 + yy) * slab, 16), slab),
            pl.ds(pl.multiple_of(cc * lanes_out, 128), lanes_out),
        ]

    def u_right(zz):
        return remote(wo_line.at[zz], wo_line.at[zz], uright_sem.at[zz], uchain_sem.at[zz], group + 4, t)

    def u_left(zz):
        return remote(wo_line.at[zz], wo_line.at[zz], uleft_sem.at[zz], uchain_sem.at[zz], group - 4, t)

    def u_here(i):
        return pltpu.make_async_copy(wo_line.at[t * half_levels + i], u_at(t, i, y, c), uhere_sem.at[i])

    def u_across(i):
        zz = other_t * half_levels + i
        return remote(wo_line.at[zz], u_at(t, i, y, c), ux_sem.at[i], uxr_sem.at[i], group, other_t)

    def u_over(tt, i, line):
        src = wo_line.at[t * half_levels + i] if line else u_at(tt, i, y, c)
        return remote(src, u_at(tt, i, y, c), uy_sem.at[tt, i], uyr_sem.at[tt, i], at(z, 1 - y, c), t)

    def u_core(tt, i, yy, line):
        src = wo_line.at[t * half_levels + i] if line else u_at(tt, i, yy, c)
        return remote(
            src, u_at(tt, i, yy, c), uc_sem.at[tt, i, yy], ucr_sem.at[tt, i, yy], at(z, y, 1 - c), t
        )

    def u_hops(zz):
        i = lax.rem(zz, half_levels)
        wanted = zz // half_levels == t

        @pl.when(wanted)
        def _():
            u_here(i).start()
            u_over(t, i, True).start()
            u_core(t, i, y, True).start()

        @pl.when(jnp.logical_not(wanted))
        def _():
            u_across(i).start()

    def u_own():
        wo_swap.wait()
        mine, theirs = wo_send[c].astype(F32)[:depth], wo_got[...].astype(F32)[:depth]
        low, high = jnp.where(c == 0, mine, theirs), jnp.where(c == 0, theirs, mine)
        wo_line[z] = jnp.concatenate([low, high], axis=0).astype(BF16)

        @pl.when(edge_r)
        def _():
            u_right(z).start()

        @pl.when(edge_l)
        def _():
            u_left(z).start()

    def u_arrive(d):
        @pl.when(z - d >= 0)
        def _():
            u_right(z - d).wait_recv()

            @pl.when(edge_r)
            def _():
                u_right(z - d).start()

            u_hops(z - d)

        @pl.when(z + d < levels)
        def _():
            u_left(z + d).wait_recv()

            @pl.when(edge_l)
            def _():
                u_left(z + d).start()

            u_hops(z + d)

    inner = jnp.logical_and(edge_l, edge_r)

    arrive(0, 1)
    arrive(1, 1)
    send_own(2)
    arrive(0, 2)
    arrive(1, 2)
    n_forward(0)
    arrive(2, 1)
    n_forward(1)
    u_own()
    arrive(2, 2)
    arrive(0, 3)
    arrive(1, 3)

    def n_rest(s):
        for cc in range(2):
            @pl.when(c == y)
            def _():
                n_wait(t, cc, s)

            @pl.when(c != y)
            def _():
                for way, (start, size) in enumerate(((0, part), (part, sub - part))):
                    ref = n_all.at[other_t, n_rows(cc, s * sub + start, size), :]
                    pltpu.make_async_copy(ref, ref, nfr_sem.at[way, cc, s]).wait()

    n_rest(0)
    n_rest(1)
    u_hops(z)

    @pl.when(inner)
    def _():
        u_arrive(1)

    def core_wait(j):
        for zz in range(levels):
            remote(
                piece(j, zz, 1 - c), piece(j, zz, 1 - c), core_s_sem.at[j, zz], core_r_sem.at[j, zz],
                at(z, y, 1 - c), t,
            ).wait_recv()

    def project(j, start, size):
        out = jnp.dot(n_all[0, pl.ds(start, size), :], w_all[j, :feat, :], preferred_element_type=F32)
        for tt in range(1, 2):
            out += jnp.dot(
                n_all[tt, pl.ds(start, size), :], w_all[j, tt * feat : (tt + 1) * feat, :],
                preferred_element_type=F32,
            )
        return out

    tall = 2 * rows
    step = tall // 4
    for j in range(2):
        core_wait(j)

        @pl.loop(0, 4)
        def _(i):
            start = pl.multiple_of(i * step, step)
            out = project(j, start, step)
            qk_wide[j, pl.ds(start, step), :] = out
            qk_mine[j, :, pl.ds(start, step)] = to_row(jnp.sum(out * out, axis=-1, keepdims=True))

    def stat_swap(k):
        return remote(
            qk_mine, qk_got.at[k - 1], qs_sem.at[k - 1], qr_sem.at[k - 1],
            at(z, lax.rem(y + k % 2, 2), c), lax.rem(t + k // 2, 2),
        )

    for k in range(1, 4):
        stat_swap(k).start()
    for k in range(1, 4):
        stat_swap(k).wait()
    stats = qk_mine[...] + qk_got[0] + qk_got[1] + qk_got[2]
    factors = lax.rsqrt(stats / (4 * cols) + 1e-06)
    for j, ref in ((0, qn), (1, kn)):
        column = to_column(factors[j, :1])
        near = qk_gain_ref[j : j + 1, :cols]
        far = qk_gain_ref[j : j + 1, cols:]
        gains = jnp.where(y == 0, near, far)
        ref[...] = (qk_wide[j] * column * gains).astype(BF16)

    for cc in range(2):
        pltpu.make_async_copy(ids_ref, ids_all.at[cc], ir_sem.at[cc]).wait()
    seam = rows + SHARE
    scale = 1.0 / math.sqrt(HD)
    ids = jnp.concatenate([ids_all[0, :1], ids_all[1, :1]], axis=1)
    for half in range(2):
        first = half * (rows - SHARE)
        same = to_column(ids[:, half * rows : (half + 1) * rows]) == ids[:, first : first + seam]

        @pl.loop(0, heads)
        def _(h):
            lanes = pl.ds(pl.multiple_of(h * HD, HD), HD)
            scores = lax.dot_general(
                qn[half * rows : (half + 1) * rows, lanes], kn[first : first + seam, lanes],
                (((1,), (1,)), ((), ())), preferred_element_type=F32,
            ) * scale
            scores = jnp.where(same, scores, -jnp.inf)
            expo = jnp.exp(scores - jnp.max(scores, axis=-1, keepdims=True))
            share = 1.0 / jnp.sum(expo, axis=-1, keepdims=True)
            probs[half, h] = (expo * share).astype(BF16)

    arrive(2, 3)
    core_wait(2)

    @pl.loop(0, 4)
    def _(i):
        start = pl.multiple_of(i * step, step)
        vb[pl.ds(start, step), :] = project(2, start, step).astype(BF16)

    def att_copy(dt, half):
        src = att.at[half * rows : (half + 1) * rows, :]
        dst = att_all.at[t, :, pl.ds(pl.multiple_of(y * cols, 128), cols)]
        mine = jnp.logical_and(y == c, c == half)
        away = remote(src, dst, as_sem.at[dt, half], ar_sem.at[t, y], at(z, c, half), lax.rem(t + dt, 2))
        return mine, away, pltpu.make_async_copy(src, dst, ar_sem.at[t, y])

    for half in range(2):
        first = half * (rows - SHARE)

        @pl.loop(0, heads)
        def _(h):
            lanes = pl.ds(pl.multiple_of(h * HD, HD), HD)
            att[half * rows : (half + 1) * rows, lanes] = jnp.dot(
                probs[half, h], vb[first : first + seam, lanes], preferred_element_type=F32
            ).astype(BF16)

        att_copy(1, half)[1].start()
        mine, away, here = att_copy(0, half)

        @pl.when(mine)
        def _():
            here.start()

        @pl.when(jnp.logical_not(mine))
        def _():
            away.start()

    target = owner_ref[...]
    named = lax.broadcasted_iota(jnp.int32, (count, rows), 0) == target
    earlier = lax.broadcasted_iota(jnp.int32, (rows, rows), 0) < lax.broadcasted_iota(jnp.int32, (rows, rows), 1)
    ranks = jnp.dot(
        named.astype(F32).astype(BF16), earlier.astype(F32).astype(BF16), preferred_element_type=F32
    )
    slot = jnp.sum(jnp.where(named, ranks, 0.0), axis=0, keepdims=True).astype(jnp.int32)
    place = target * capacity + slot

    @pl.when(jnp.logical_not(inner))
    def _():
        u_arrive(1)

    u_arrive(2)
    u_arrive(3)
    for i in range(half_levels):
        ref = u_at(other_t, i, y, c)
        pltpu.make_async_copy(ref, ref, uxr_sem.at[i]).wait()
        u_over(other_t, i, False).start()
        u_core(other_t, i, y, False).start()
    for i in range(half_levels):
        for tt in range(2):
            ref = u_at(tt, i, 1 - y, c)
            pltpu.make_async_copy(ref, ref, uyr_sem.at[tt, i]).wait()
            u_core(tt, i, 1 - y, False).start()
    for i in range(half_levels):
        u_here(i).wait()
        for tt in range(2):
            for yy in range(2):
                ref = u_at(tt, i, yy, 1 - c)
                pltpu.make_async_copy(ref, ref, ucr_sem.at[tt, i, yy]).wait()

    for tt in range(2):
        for yy in range(2):
            ref = att_all.at[tt, :, yy * cols : (yy + 1) * cols]
            pltpu.make_async_copy(ref, ref, ar_sem.at[tt, yy]).wait()

    def sending(f, lanes, owner_group):
        return pltpu.make_async_remote_copy(
            src_ref=outbox.at[owner_group, :, lanes], dst_ref=out_ref.at[group, :, lanes],
            send_sem=send_sem.at[f, owner_group], recv_sem=recv_sem.at[f, group],
            device_id={"group": owner_group, "tp": t}, device_id_type=MESH,
        )

    def keeping(f, lanes):
        return pltpu.make_async_copy(outbox.at[group, :, lanes], out_ref.at[group, :, lanes], keep_sem.at[f])

    cut = feat // 256 // 2 * 256 if SPLIT else 0
    spans = [slice(0, cut), slice(cut, feat)] if cut else [slice(0, feat)]
    planes = (3 - z, lax.rem(z + 2, 4), z + 1 - 2 * lax.rem(z, 2), z)
    for f, lanes in enumerate(spans):
        total = jnp.zeros((rows, lanes.stop - lanes.start), F32)
        for tt in range(2):
            term = lax.dot_general(
                att_all[tt], wo_all[tt, lanes, :], (((1,), (1,)), ((), ())), preferred_element_type=F32
            )
            total += term.astype(BF16).astype(F32)
        mixed[:, lanes] = (tokens_ref[:, lanes].astype(F32) + scale_ref[:, lanes] * total).astype(BF16)
        for plane in planes:
            slots = lax.broadcasted_iota(jnp.int32, (4 * capacity, rows), 0) + plane * 4 * capacity
            chosen = (slots == place).astype(F32).astype(BF16)
            picked = jnp.dot(chosen, mixed[:, lanes], preferred_element_type=F32).astype(BF16)
            outbox[pl.ds(plane * 4, 4), :, lanes] = picked.reshape(4, capacity, lanes.stop - lanes.start)
            for k in range(4):
                peer = plane * 4 + k

                @pl.when(peer == group)
                def _():
                    keeping(f, lanes).start()

                @pl.when(peer != group)
                def _():
                    sending(f, lanes, peer).start()

    for f, lanes in enumerate(spans):
        @pl.loop(1, count)
        def _(step):
            peer = lax.rem(group + step, count)
            sending(f, lanes, peer).wait_send()
            ref = out_ref.at[peer, :, lanes]
            pltpu.make_async_copy(ref, ref, recv_sem.at[f, peer]).wait()

        keeping(f, lanes).wait()

    for yy in range(2):
        @pl.when(jnp.logical_not(is_me(yy)))
        def _():
            for copy in pieces(yy):
                copy.wait_send()

    for s in range(2):
        n_x, n_y, n_core, n_here = n_copies(s)
        n_x.wait_send()
        n_y.wait_send()

        @pl.when(c != y)
        def _():
            n_core.wait_send()

        for cc in range(2):
            @pl.when(c == y)
            def _():
                forward_y(cc, s).wait_send()

            @pl.when(c != y)
            def _():
                forward_x(cc, s).wait_send()

    for half in range(2):
        att_copy(1, half)[1].wait_send()
        mine, away, here = att_copy(0, half)

        @pl.when(jnp.logical_not(mine))
        def _():
            away.wait_send()

    for zz in range(levels):
        @pl.when(jnp.logical_and(zz <= z, edge_r))
        def _():
            u_right(zz).wait_send()

        @pl.when(jnp.logical_and(zz >= z, edge_l))
        def _():
            u_left(zz).wait_send()

    for i in range(half_levels):
        u_across(i).wait_send()
        for tt in range(2):
            u_over(tt, i, False).wait_send()
            for yy in range(2):
                u_core(tt, i, yy, False).wait_send()

    for j in range(3):
        for zz in range(levels):
            @pl.when(jnp.logical_and(zz <= z, edge_r))
            def _():
                go_right(j, zz).wait_send()

            @pl.when(jnp.logical_and(zz >= z, edge_l))
            def _():
                go_left(j, zz).wait_send()

            go_core(j, zz).wait_send()


def plane_call(turned, gain, w, qk_gain, wo, scale, request, owner, count, capacity):
    feat, rows = turned.shape
    depth, width = w.shape[1], w.shape[2]
    levels, cols = count // 4, width // 2
    heads = cols // HD
    padded = -(-depth // 16) * 16
    seam = rows + SHARE
    dma = pltpu.SemaphoreType.DMA
    vmem = pl.BlockSpec(memory_space=pltpu.VMEM)
    return pl.pallas_call(
        functools.partial(plane_kernel, levels),
        name="plane",
        out_shape=jax.ShapeDtypeStruct((count, capacity, feat), BF16),
        in_specs=[vmem] * 8,
        out_specs=pl.BlockSpec(memory_space=pl.ANY),
        scratch_shapes=[
            pltpu.VMEM((rows, feat), BF16),
            pltpu.VMEM((8, rows), F32),
            pltpu.VMEM((2, 3, padded, cols), BF16),
            pltpu.VMEM((2, 3, padded, cols), BF16),
            pltpu.VMEM((3, 2 * feat, cols), BF16),
            pltpu.VMEM((rows, feat), BF16),
            pltpu.VMEM((2, 2 * rows, feat), BF16),
            pltpu.VMEM((2, 8, rows), F32),
            pltpu.VMEM((8, rows), F32),
            pltpu.VMEM((8, rows), F32),
            pltpu.VMEM((2, 8, 2 * rows), F32),
            pltpu.VMEM((3, 2, 8, 2 * rows), F32),
            pltpu.VMEM((2, 2 * rows, cols), F32),
            pltpu.VMEM((2 * rows, cols), BF16),
            pltpu.VMEM((2 * rows, cols), BF16),
            pltpu.VMEM((2 * rows, cols), BF16),
            pltpu.VMEM((2, heads, rows, seam), BF16),
            pltpu.VMEM((2 * rows, cols), BF16),
            pltpu.VMEM((2, padded, width // 2), BF16),
            pltpu.VMEM((padded, width // 2), BF16),
            pltpu.VMEM((levels, 2 * depth, width // 2), BF16),
            pltpu.VMEM((2, feat, width), BF16),
            pltpu.VMEM((2, rows, width), BF16),
            pltpu.VMEM((rows, feat), BF16),
            pltpu.VMEM((count, capacity, feat), BF16),
            dma((2, 3)), dma((2, 3)), dma((2,)), dma((2,)), dma, dma,
            dma((3, 2)), dma((2, 2, 2)), dma((2, 2)), dma((2, 2, 2)),
            dma((3, levels)), dma((3, levels)), dma((3, levels)), dma((3, levels)), dma((3, levels)),
            dma((3,)), dma((3,)),
            dma, dma, dma((levels,)), dma((levels,)), dma((levels,)), dma((2,)), dma((2,)), dma((2,)),
            dma((2, 2)), dma((2, 2)), dma((2, 2, 2)), dma((2, 2, 2)),
            dma((2, 2)), dma((2, 2)), dma((2, count)), dma((2, count)), dma((2,)),
        ],
        compiler_params=pltpu.CompilerParams(
            collective_id=1, has_side_effects=True, vmem_limit_bytes=60 * 2**20
        ),
        cost_estimate=pl.CostEstimate(
            flops=20 * rows * feat * width, transcendentals=2 * heads * rows * seam,
            bytes_accessed=8 * 2**20,
        ),
    )(turned, gain, w, qk_gain, wo, scale, request, owner)


def swapped(value, axis, apart):
    mask = 2**apart
    pairs = [(source, source ^ mask) for source in range(lax.axis_size(axis))]
    return lax.ppermute(value, axis, pairs)


def from_next(value, axis):
    count = lax.axis_size(axis)
    return lax.ppermute(value, axis, [((i + 1) % count, i) for i in range(count)])


def attend_kernel(q_ref, k_ref, v_ref, kp_ref, vp_ref, row_ref, own_ref, pair_ref, out_ref):
    query = q_ref[...]
    over = (((1,), (1,)), ((), ()))
    scale = 1.0 / math.sqrt(HD)
    near = lax.dot_general(query, k_ref[...], over, preferred_element_type=jnp.float32) * scale
    far = lax.dot_general(query, kp_ref[...], over, preferred_element_type=jnp.float32) * scale
    near = jnp.where(row_ref[...] == own_ref[...], near, -jnp.inf)
    far = jnp.where(row_ref[...] == pair_ref[...], far, -jnp.inf)
    top = jnp.maximum(
        jnp.max(near, axis=-1, keepdims=True), jnp.max(far, axis=-1, keepdims=True)
    )
    near, far = jnp.exp(near - top), jnp.exp(far - top)
    share = 1.0 / (jnp.sum(near, axis=-1, keepdims=True) + jnp.sum(far, axis=-1, keepdims=True))
    near, far = (near * share).astype(jnp.bfloat16), (far * share).astype(jnp.bfloat16)
    total = jnp.dot(near, v_ref[...], preferred_element_type=jnp.float32)
    total += jnp.dot(far, vp_ref[...], preferred_element_type=jnp.float32)
    out_ref[...] = total.astype(jnp.bfloat16)


def attend(query, keys, values, paired_keys, paired_values, ids, paired_ids):
    rows, width = query.shape
    seam = paired_keys.shape[0]
    block = pl.BlockSpec((rows, HD), lambda h: (0, h))
    seam_block = pl.BlockSpec((seam, HD), lambda h: (0, h))
    fixed = lambda shape: pl.BlockSpec(shape, lambda h: (0, 0))
    return pl.pallas_call(
        attend_kernel,
        grid=(width // HD,),
        out_shape=jax.ShapeDtypeStruct((rows, width), jnp.bfloat16),
        in_specs=[
            block, block, block, seam_block, seam_block,
            fixed((rows, 1)), fixed((1, rows)), fixed((1, seam)),
        ],
        out_specs=block,
        compiler_params=pltpu.CompilerParams(vmem_limit_bytes=32 * 2**20),
        cost_estimate=pl.CostEstimate(
            flops=4 * rows * (rows + seam) * width,
            transcendentals=rows * (rows + seam) * width // HD,
            bytes_accessed=8 * rows * width,
        ),
    )(
        query, keys, values, paired_keys, paired_values,
        ids[:, None], ids[None, :], paired_ids[None, :],
    )


def route_kernel(count, place_ref, mixed_ref, out_ref, outbox, send_sem, recv_sem, keep_sem):
    me = lax.axis_index("group")
    capacity = outbox.shape[1]
    rows = mixed_ref.shape[0]
    barrier = pltpu.get_barrier_semaphore()

    @pl.loop(1, count)
    def _(step):
        pl.semaphore_signal(
            barrier, inc=1, device_id={"group": lax.rem(me + step, count)},
            device_id_type=pl.DeviceIdType.MESH,
        )

    pl.semaphore_wait(barrier, count - 1)

    def pick(owner):
        slots = lax.broadcasted_iota(jnp.int32, (capacity, rows), 0) + owner * capacity
        select = (slots == place_ref[...]).astype(jnp.float32).astype(jnp.bfloat16)
        return jnp.dot(select, mixed_ref[...], preferred_element_type=jnp.float32).astype(
            jnp.bfloat16
        )

    def sending(step):
        ahead = 1 + lax.rem(step - 1 + count // 2 - 1, count - 1)
        peer = lax.rem(me + ahead, count)
        return peer, pltpu.make_async_remote_copy(
            src_ref=outbox.at[step],
            dst_ref=out_ref.at[me],
            send_sem=send_sem.at[step],
            recv_sem=recv_sem.at[me],
            device_id={"group": peer},
            device_id_type=pl.DeviceIdType.MESH,
        )

    @pl.loop(1, count)
    def _(step):
        peer, copy = sending(step)
        outbox[step] = pick(peer)
        copy.start()

    outbox[0] = pick(me)
    keep = pltpu.make_async_copy(outbox.at[0], out_ref.at[me], keep_sem)
    keep.start()

    @pl.loop(1, count)
    def _(step):
        source = lax.rem(me + step, count)
        pltpu.make_async_remote_copy(
            src_ref=outbox.at[step],
            dst_ref=out_ref.at[source],
            send_sem=send_sem.at[step],
            recv_sem=recv_sem.at[source],
            device_id={"group": source},
            device_id_type=pl.DeviceIdType.MESH,
        ).wait()

    keep.wait()


def route(place, mixed, count, capacity):
    rows, feat = mixed.shape
    return pl.pallas_call(
        lambda *refs: route_kernel(count, *refs),
        name="route",
        out_shape=jax.ShapeDtypeStruct((count, capacity, feat), jnp.bfloat16),
        in_specs=[pl.BlockSpec(memory_space=pltpu.VMEM)] * 2,
        out_specs=pl.BlockSpec(memory_space=pl.ANY),
        scratch_shapes=[
            pltpu.VMEM((count, capacity, feat), jnp.bfloat16),
            pltpu.SemaphoreType.DMA((count,)),
            pltpu.SemaphoreType.DMA((count,)),
            pltpu.SemaphoreType.DMA,
        ],
        compiler_params=pltpu.CompilerParams(
            collective_id=0, has_side_effects=True, vmem_limit_bytes=32 * 2**20
        ),
        cost_estimate=pl.CostEstimate(
            flops=2 * count * capacity * rows * feat,
            transcendentals=0,
            bytes_accessed=4 * count * capacity * feat,
        ),
    )(place[None, :], mixed)


def spread_shards(tokens, norm_gain, w_qkv, qk_gain, w_out, layer_scale, request, owner):
    rows, feat_local = tokens.shape
    tp_count = lax.axis_size("tp")
    group_count = lax.axis_size("group")
    local_width = w_qkv.shape[2]
    head_count = local_width // HD
    me_tp = lax.axis_index("tp")
    w_all = lax.all_gather(
        w_qkv.reshape(w_qkv.shape[0], 3 * local_width), "group", axis=0, tiled=True
    )
    whole = jnp.zeros((rows, feat_local * tp_count), jnp.bfloat16)
    gain_all = jnp.zeros((1, feat_local * tp_count), jnp.bfloat16)
    piece, gain = tokens, norm_gain.reshape(1, feat_local)
    for step in range(tp_count):
        at = ((me_tp + step) % tp_count) * feat_local
        whole = lax.dynamic_update_slice(whole, piece, (0, at))
        gain_all = lax.dynamic_update_slice(gain_all, gain, (0, at))
        if step < tp_count - 1:
            piece, gain = from_next(piece, "tp"), from_next(gain, "tp")
    whole, late_out = lax.optimization_barrier((whole, w_out))
    per = group_count // tp_count
    pairs = []
    for g in range(group_count):
        for b in range(tp_count):
            t, j = g // per, g % per
            to_g = b * per + j
            pairs.append((g * tp_count + b, to_g * tp_count + t))
    w_piece = lax.ppermute(late_out.T, ("group", "tp"), pairs)
    w_o = lax.all_gather(w_piece, "group", axis=0, tiled=True)
    w_o = w_o.reshape(tp_count, feat_local, local_width)
    xwide = whole.astype(jnp.float32)
    stat = jnp.mean(xwide * xwide, axis=-1, keepdims=True)
    normed = (xwide * lax.rsqrt(stat + 1e-06) * gain_all.astype(jnp.float32)).astype(jnp.bfloat16)
    qkv = jnp.dot(normed, w_all, preferred_element_type=jnp.float32)
    query = qkv[:, :local_width]
    key_rows = qkv[:, local_width : 2 * local_width]
    value = qkv[:, 2 * local_width :].astype(jnp.bfloat16)
    qsum, ksum = lax.psum(
        (jnp.sum(query * query, axis=-1), jnp.sum(key_rows * key_rows, axis=-1)), "tp"
    )
    total_width = local_width * tp_count
    qnorm = (query * lax.rsqrt(qsum / total_width + 1e-06)[:, None] * qk_gain[0]).astype(
        jnp.bfloat16
    )
    knorm = (key_rows * lax.rsqrt(ksum / total_width + 1e-06)[:, None] * qk_gain[1]).astype(
        jnp.bfloat16
    )
    parity = lax.axis_index("group") % 2
    seam = jnp.where(parity == 0, rows - SHARE, 0).astype(jnp.int32)
    key_window = lax.dynamic_slice_in_dim(knorm, seam, SHARE, 0)
    id_window = lax.dynamic_slice_in_dim(request, seam, SHARE, 0)
    paired_keys, paired_ids = swapped((key_window, id_window), "group", 0)
    value_window = lax.dynamic_slice_in_dim(value, seam, SHARE, 0)
    paired_values = swapped(value_window, "group", 0)
    attended = attend(qnorm, knorm, value, paired_keys, paired_values, request, paired_ids)

    branch = jnp.zeros((rows, feat_local), jnp.float32)
    for step in range(tp_count):
        onward = from_next(attended, "tp") if step < tp_count - 1 else None
        part = lax.dot_general(
            attended,
            lax.dynamic_index_in_dim(w_o, (me_tp + step) % tp_count, 0, keepdims=False),
            (((1,), (1,)), ((), ())),
            preferred_element_type=jnp.float32,
        )
        branch = branch + part.astype(jnp.bfloat16).astype(jnp.float32)
        attended = onward
    mixed = (tokens.astype(jnp.float32) + layer_scale * branch).astype(jnp.bfloat16)

    capacity = max(2, 2 * rows // group_count)
    target = owner[:, 0]
    onehot = target[:, None] == jnp.arange(group_count, dtype=jnp.int32)[None, :]
    order = jnp.arange(rows, dtype=jnp.int32)
    before = (order[:, None] > order[None, :]).astype(jnp.bfloat16)
    ranks = jnp.dot(before, onehot.astype(jnp.bfloat16), preferred_element_type=jnp.float32)
    slot = jnp.sum(jnp.where(onehot, ranks, 0.0), axis=-1).astype(jnp.int32)
    place = target * capacity + slot
    inbox = route(place, mixed, group_count, capacity)
    return inbox[None]


def plane_shards(tokens, norm_gain, w_qkv, qk_gain, w_out, layer_scale, request, owner):
    count = lax.axis_size("group")
    capacity = max(2, 2 * tokens.shape[0] // count)
    return plane_call(
        tokens.T, norm_gain[None, :], w_qkv.transpose(1, 0, 2), qk_gain, w_out.T, layer_scale[None, :],
        request[None, :], owner.T, count, capacity,
    )[None]


def shards(*arrays):
    w_qkv = arrays[2]
    count, tp = lax.axis_size("group"), lax.axis_size("tp")
    whole_tiles = 2 * w_qkv.shape[0] % 16 == 0 and w_qkv.shape[2] % (2 * HD) == 0
    if tp == 2 and count == 16 and whole_tiles:
        return plane_shards(*arrays)
    return spread_shards(*arrays)


def solution(mesh):
    in_specs = (
        P("group", "tp"),
        P("tp"),
        P("group", None, "tp"),
        P(None, "tp"),
        P("tp", "group"),
        P("tp"),
        P("group"),
        P("group", None),
    )
    out_specs = P("group", None, None, "tp")
    return jax.shard_map(shards, mesh=mesh, in_specs=in_specs, out_specs=out_specs, check_vma=False)
```

```python
import functools
import math

import jax
import jax.numpy as jnp
from jax import lax
from jax.experimental import pallas as pl
from jax.experimental.pallas import tpu as pltpu
from jax.sharding import PartitionSpec as P

HD = 128
SHARE = 128


SPLIT = True
MESH = pl.DeviceIdType.MESH
BF16 = jnp.bfloat16
F32 = jnp.float32


def to_row(column):
    spread = jnp.broadcast_to(column, (column.shape[0], 128))
    return jnp.transpose(spread)[:8]


def to_column(row):
    spread = jnp.broadcast_to(row, (128, row.shape[1]))
    return jnp.transpose(spread)[:, :1]


def plane_kernel(
    levels, turned_ref, vectors_ref, w_ref, qk_gain_ref, wo_ref, request_ref, owner_ref, out_ref,
    tokens_ref, ids_ref, w_send, w_got, w_all, n_send, n_all, ids_all, sum_mine, sum_got, qk_mine, qk_got,
    qk_wide, qn, kn, vb, probs, att, wo_send, wo_got, wo_line, wo_all, att_all,
    ws_sem, wr_sem, is_sem, ir_sem, ss_sem, sr_sem, ns_sem, nr_sem, nf_sem, nfr_sem,
    right_sem, left_sem, chain_sem, core_s_sem, core_r_sem, qs_sem, qr_sem,
    wos_sem, wor_sem, uright_sem, uleft_sem, uchain_sem, uhere_sem, ux_sem, uxr_sem, uy_sem, uyr_sem, uc_sem, ucr_sem,
    as_sem, ar_sem, send_sem, recv_sem, keep_sem,
):
    group, t = lax.axis_index("group"), lax.axis_index("tp")
    z, y, c = group // 4, lax.rem(group // 2, 2), lax.rem(group, 2)
    rows, feat = tokens_ref.shape
    count, capacity = out_ref.shape[:2]
    slab = w_all.shape[1] // (2 * levels)
    depth = w_ref.shape[1]
    cols = w_all.shape[2]
    heads = cols // HD
    sub = rows // 2
    part = sub // 8
    half_cols = cols // 2
    edge_r, edge_l = z < levels - 1, z > 0

    def at(zz, yy, cc):
        return (zz * 2 + yy) * 2 + cc

    def remote(src, dst, send, recv, place, tt):
        return pltpu.make_async_remote_copy(
            src_ref=src, dst_ref=dst, send_sem=send, recv_sem=recv,
            device_id={"group": place, "tp": tt}, device_id_type=MESH,
        )

    barrier = pltpu.get_barrier_semaphore()

    @pl.loop(1, count)
    def _(step):
        pl.semaphore_signal(
            barrier, inc=1, device_id={"group": lax.rem(group + step, count), "tp": t}, device_id_type=MESH
        )

    for k in range(4):
        pl.semaphore_signal(
            barrier, inc=1, device_id={"group": z * 4 + k, "tp": lax.rem(t + 1, 2)}, device_id_type=MESH
        )

    for yy in range(2):
        w_send[yy, :, :depth, :] = w_ref[:, :, yy * cols : (yy + 1) * cols]

    half_out = wo_ref.shape[1] // 2
    for cc in range(2):
        wo_send[cc, :depth, :] = wo_ref[:, cc * half_out : (cc + 1) * half_out]
    ids_ref[...] = jnp.broadcast_to(request_ref[...].astype(F32), (8, rows))
    pl.semaphore_wait(barrier, count + 3)

    def pieces(yy):
        place = at(z, yy, y)
        copies = [
            remote(w_send.at[yy, j], w_got.at[c, j], ws_sem.at[yy, j], wr_sem.at[c, j], place, t) for j in range(3)
        ]
        return copies + [remote(ids_ref, ids_all.at[c], is_sem.at[yy], ir_sem.at[c], place, t)]

    def kept(yy):
        copies = [pltpu.make_async_copy(w_send.at[yy, j], w_got.at[c, j], wr_sem.at[c, j]) for j in range(3)]
        return copies + [pltpu.make_async_copy(ids_ref, ids_all.at[c], ir_sem.at[c])]

    def is_me(yy):
        return jnp.logical_and(y == yy, c == y)

    for yy in range(2):
        @pl.when(is_me(yy))
        def _():
            for copy in kept(yy):
                copy.start()

        @pl.when(jnp.logical_not(is_me(yy)))
        def _():
            for copy in pieces(yy):
                copy.start()

    wo_swap = remote(wo_send.at[1 - c], wo_got, wos_sem, wor_sem, at(z, y, 1 - c), t)
    wo_swap.start()

    wide = turned_ref[...].astype(F32)
    sum_mine[...] = jnp.broadcast_to(jnp.sum(wide * wide, axis=0, keepdims=True), (8, rows))
    swap = remote(sum_mine, sum_got, ss_sem, sr_sem, group, lax.rem(t + 1, 2))
    swap.start()

    def rows_of(zz, cc):
        return pl.ds(pl.multiple_of((zz * 2 + cc) * slab, 16), slab)

    def piece(j, zz, cc):
        if j < 2:
            return w_all.at[j, rows_of(zz, cc), :]
        return w_all.at[2, rows_of(zz, cc), (j - 2) * half_cols : (j - 1) * half_cols]

    def go_right(j, zz):
        return remote(piece(j, zz, c), piece(j, zz, c), right_sem.at[j, zz], chain_sem.at[j, zz], group + 4, t)

    def go_left(j, zz):
        return remote(piece(j, zz, c), piece(j, zz, c), left_sem.at[j, zz], chain_sem.at[j, zz], group - 4, t)

    def go_core(j, zz):
        return remote(
            piece(j, zz, c), piece(j, zz, c), core_s_sem.at[j, zz], core_r_sem.at[j, zz],
            at(z, y, 1 - c), t,
        )

    def build(j):
        for cc in range(2):
            pltpu.make_async_copy(w_send.at[0, j], w_got.at[cc, j], wr_sem.at[cc, j]).wait()
        both = jnp.concatenate(
            [w_got[0, j].astype(F32)[:depth], w_got[1, j].astype(F32)[:depth]], axis=0
        )
        w_all[j, rows_of(z, c), :] = both.astype(BF16)

    def send_own(j):
        @pl.when(edge_r)
        def _():
            go_right(j, z).start()

        @pl.when(edge_l)
        def _():
            go_left(j, z).start()

        go_core(j, z).start()

    def arrive(j, d):
        @pl.when(z - d >= 0)
        def _():
            go_right(j, z - d).wait_recv()

            @pl.when(edge_r)
            def _():
                go_right(j, z - d).start()

            go_core(j, z - d).start()

        @pl.when(z + d < levels)
        def _():
            go_left(j, z + d).wait_recv()

            @pl.when(edge_l)
            def _():
                go_left(j, z + d).start()

            go_core(j, z + d).start()

    other_t = lax.rem(t + 1, 2)
    half_levels = levels // 2
    lanes_out = wo_all.shape[2] // 2

    def u_at(tt, i, yy, cc):
        return wo_all.at[
            tt, pl.ds(pl.multiple_of((i * 2 + yy) * slab, 16), slab),
            pl.ds(pl.multiple_of(cc * lanes_out, 128), lanes_out),
        ]

    def u_right(zz):
        return remote(wo_line.at[zz], wo_line.at[zz], uright_sem.at[zz], uchain_sem.at[zz], group + 4, t)

    def u_left(zz):
        return remote(wo_line.at[zz], wo_line.at[zz], uleft_sem.at[zz], uchain_sem.at[zz], group - 4, t)

    def u_here(i):
        return pltpu.make_async_copy(wo_line.at[t * half_levels + i], u_at(t, i, y, c), uhere_sem.at[i])

    def u_across(i):
        zz = other_t * half_levels + i
        return remote(wo_line.at[zz], u_at(t, i, y, c), ux_sem.at[i], uxr_sem.at[i], group, other_t)

    def u_over(tt, i, line):
        src = wo_line.at[t * half_levels + i] if line else u_at(tt, i, y, c)
        return remote(src, u_at(tt, i, y, c), uy_sem.at[tt, i], uyr_sem.at[tt, i], at(z, 1 - y, c), t)

    def u_core(tt, i, yy, line):
        src = wo_line.at[t * half_levels + i] if line else u_at(tt, i, yy, c)
        return remote(
            src, u_at(tt, i, yy, c), uc_sem.at[tt, i, yy], ucr_sem.at[tt, i, yy], at(z, y, 1 - c), t
        )

    def u_hops(zz):
        i = lax.rem(zz, half_levels)
        wanted = zz // half_levels == t

        @pl.when(wanted)
        def _():
            u_here(i).start()
            u_over(t, i, True).start()
            u_core(t, i, y, True).start()

        @pl.when(jnp.logical_not(wanted))
        def _():
            u_across(i).start()

    def u_own():
        wo_swap.wait()
        mine, theirs = wo_send[c].astype(F32)[:depth], wo_got[...].astype(F32)[:depth]
        low, high = jnp.where(c == 0, mine, theirs), jnp.where(c == 0, theirs, mine)
        wo_line[z] = jnp.concatenate([low, high], axis=0).astype(BF16)

        @pl.when(edge_r)
        def _():
            u_right(z).start()

        @pl.when(edge_l)
        def _():
            u_left(z).start()

    def u_arrive(d):
        @pl.when(z - d >= 0)
        def _():
            u_right(z - d).wait_recv()

            @pl.when(edge_r)
            def _():
                u_right(z - d).start()

            u_hops(z - d)

        @pl.when(z + d < levels)
        def _():
            u_left(z + d).wait_recv()

            @pl.when(edge_l)
            def _():
                u_left(z + d).start()

            u_hops(z + d)

    def ux_take(d):
        for zz in ((z - d, z + d) if d else (z,)):
            here = jnp.logical_and(jnp.logical_and(zz >= 0, zz < levels), (zz + levels) // half_levels == t + 2)

            @pl.when(here)
            def _():
                i = lax.rem(zz, half_levels)
                ref = u_at(other_t, i, y, c)
                pltpu.make_async_copy(ref, ref, uxr_sem.at[i]).wait()
                u_over(other_t, i, False).start()
                u_core(other_t, i, y, False).start()

    inner = jnp.logical_and(edge_l, edge_r)
    outer = jnp.logical_not(inner)
    build(0)
    send_own(0)
    build(1)
    send_own(1)
    u_own()
    u_hops(z)
    build(2)

    @pl.when(outer)
    def _():
        send_own(2)
        send_own(3)

    tokens_ref[...] = jnp.transpose(turned_ref[...].astype(F32)).astype(BF16)
    swap.wait()
    whole = sum_mine[...] + sum_got[...]
    factor = to_column(lax.rsqrt(whole[:1] / (2 * feat) + 1e-06))

    def n_rows(cc, start, size):
        return pl.ds(pl.multiple_of(cc * rows + start, 16), size)

    def n_copies(s):
        src = n_send.at[s * sub : (s + 1) * sub, :]
        dst = n_all.at[t, n_rows(c, s * sub, sub), :]
        recv = nr_sem.at[t, c, s]
        return (
            remote(src, dst, ns_sem.at[0, s], recv, at(z, y, y), lax.rem(t + 1, 2)),
            remote(src, dst, ns_sem.at[1, s], recv, at(z, 1 - y, y), t),
            remote(src, dst, ns_sem.at[2, s], recv, at(z, y, y), t),
            pltpu.make_async_copy(src, dst, recv),
        )

    for s in range(2):
        span = slice(s * sub, (s + 1) * sub)
        n_send[span, :] = (
            tokens_ref[span, :].astype(F32) * factor[span] * vectors_ref[:1, :]
        ).astype(BF16)
        n_x, n_y, n_core, n_here = n_copies(s)
        n_x.start()
        n_y.start()

        @pl.when(c == y)
        def _():
            n_here.start()

        @pl.when(c != y)
        def _():
            n_core.start()

    def n_wait(tt, cc, s):
        ref = n_all.at[tt, n_rows(cc, s * sub, sub), :]
        pltpu.make_async_copy(ref, ref, nr_sem.at[tt, cc, s]).wait()


    def forward_y(cc, s):
        ref = n_all.at[other_t, n_rows(cc, s * sub, part), :]
        return remote(ref, ref, nf_sem.at[cc, s], nfr_sem.at[0, cc, s], at(z, 1 - y, c), t)

    def forward_x(cc, s):
        ref = n_all.at[t, n_rows(cc, s * sub + part, sub - part), :]
        return remote(ref, ref, nf_sem.at[cc, s], nfr_sem.at[1, cc, s], group, other_t)

    def n_forward(s):
        for cc in range(2):
            @pl.when(c == y)
            def _():
                n_wait(other_t, cc, s)
                forward_y(cc, s).start()

            @pl.when(c != y)
            def _():
                n_wait(t, cc, s)
                forward_x(cc, s).start()

    arrive(0, 1)
    arrive(1, 1)
    u_arrive(1)
    ux_take(0)
    n_forward(0)
    arrive(0, 2)
    arrive(1, 2)
    u_arrive(2)
    n_forward(1)
    ux_take(1)

    @pl.when(inner)
    def _():
        for j in (2, 3):
            send_own(j)
            arrive(j, 1)
            arrive(j, 2)

    arrive(0, 3)
    arrive(1, 3)

    def n_rest(s):
        for cc in range(2):
            @pl.when(c == y)
            def _():
                n_wait(t, cc, s)

            @pl.when(c != y)
            def _():
                for way, (start, size) in enumerate(((0, part), (part, sub - part))):
                    ref = n_all.at[other_t, n_rows(cc, s * sub + start, size), :]
                    pltpu.make_async_copy(ref, ref, nfr_sem.at[way, cc, s]).wait()

    n_rest(0)
    n_rest(1)
    def core_wait(j):
        for zz in range(levels):
            remote(
                piece(j, zz, 1 - c), piece(j, zz, 1 - c), core_s_sem.at[j, zz], core_r_sem.at[j, zz],
                at(z, y, 1 - c), t,
            ).wait_recv()

    def project(j, start, size, lanes):
        return jnp.dot(
            n_all[0, pl.ds(start, size), :], w_all[j, :feat, lanes], preferred_element_type=F32
        ) + jnp.dot(n_all[1, pl.ds(start, size), :], w_all[j, feat:, lanes], preferred_element_type=F32)

    tall = 2 * rows
    step = tall // 4
    for j in range(2):
        core_wait(j)

        @pl.loop(0, 4)
        def _(i):
            start = pl.multiple_of(i * step, step)
            out = project(j, start, step, slice(None))
            qk_wide[j, pl.ds(start, step), :] = out
            qk_mine[j, :, pl.ds(start, step)] = to_row(jnp.sum(out * out, axis=-1, keepdims=True))

    def stat_swap(k):
        return remote(
            qk_mine, qk_got.at[k - 1], qs_sem.at[k - 1], qr_sem.at[k - 1],
            at(z, lax.rem(y + k % 2, 2), c), lax.rem(t + k // 2, 2),
        )

    for k in range(1, 4):
        stat_swap(k).start()
    ux_take(2)
    for k in range(1, 4):
        stat_swap(k).wait()
    stats = qk_mine[...] + qk_got[0] + qk_got[1] + qk_got[2]
    factors = lax.rsqrt(stats / (4 * cols) + 1e-06)
    for j, ref in ((0, qn), (1, kn)):
        column = to_column(factors[j, :1])
        near = qk_gain_ref[j : j + 1, :cols]
        far = qk_gain_ref[j : j + 1, cols:]
        gains = jnp.where(y == 0, near, far)
        ref[...] = (qk_wide[j] * column * gains).astype(BF16)

    u_arrive(3)

    for cc in range(2):
        pltpu.make_async_copy(ids_ref, ids_all.at[cc], ir_sem.at[cc]).wait()
    seam = rows + SHARE
    scale = 1.0 / math.sqrt(HD)
    ids = jnp.concatenate([ids_all[0, :1], ids_all[1, :1]], axis=1)
    for half in range(2):
        first = half * (rows - SHARE)
        same = to_column(ids[:, half * rows : (half + 1) * rows]) == ids[:, first : first + seam]

        @pl.loop(0, heads)
        def _(h):
            lanes = pl.ds(pl.multiple_of(h * HD, HD), HD)
            scores = lax.dot_general(
                qn[half * rows : (half + 1) * rows, lanes], kn[first : first + seam, lanes],
                (((1,), (1,)), ((), ())), preferred_element_type=F32,
            ) * scale
            scores = jnp.where(same, scores, -jnp.inf)
            expo = jnp.exp(scores - jnp.max(scores, axis=-1, keepdims=True))
            share = 1.0 / jnp.sum(expo, axis=-1, keepdims=True)
            probs[half, h] = (expo * share).astype(BF16)

    def att_copy(dt, half, j):
        src = att.at[half * rows : (half + 1) * rows, j * half_cols : (j + 1) * half_cols]
        dst = att_all.at[t, :, pl.ds(pl.multiple_of(y * cols + j * half_cols, 128), half_cols)]
        mine = jnp.logical_and(y == c, c == half)
        recv = ar_sem.at[t, y, j]
        away = remote(src, dst, as_sem.at[dt, half, j], recv, at(z, c, half), lax.rem(t + dt, 2))
        return mine, away, pltpu.make_async_copy(src, dst, recv)

    for j in range(2):
        @pl.when(outer)
        def _():
            for d in range(1, levels):
                arrive(2 + j, d)

        core_wait(2 + j)
        span = slice(j * half_cols, (j + 1) * half_cols)

        @pl.loop(0, 2)
        def _(i):
            start = pl.multiple_of(i * rows, rows)
            vb[pl.ds(start, rows), span] = project(2, start, rows, span).astype(BF16)

        for half in range(2):
            first = half * (rows - SHARE)
            for h in range(j * heads // 2, (j + 1) * heads // 2):
                lanes = slice(h * HD, (h + 1) * HD)
                att[half * rows : (half + 1) * rows, lanes] = jnp.dot(
                    probs[half, h], vb[first : first + seam, lanes], preferred_element_type=F32
                ).astype(BF16)

            att_copy(1, half, j)[1].start()
            mine, away, here = att_copy(0, half, j)

            @pl.when(mine)
            def _():
                here.start()

            @pl.when(jnp.logical_not(mine))
            def _():
                away.start()

    target = owner_ref[...]
    named = lax.broadcasted_iota(jnp.int32, (count, rows), 0) == target
    earlier = lax.broadcasted_iota(jnp.int32, (rows, rows), 0) < lax.broadcasted_iota(jnp.int32, (rows, rows), 1)
    ranks = jnp.dot(
        named.astype(F32).astype(BF16), earlier.astype(F32).astype(BF16), preferred_element_type=F32
    )
    slot = jnp.sum(jnp.where(named, ranks, 0.0), axis=0, keepdims=True).astype(jnp.int32)
    place = target * capacity + slot

    ux_take(3)
    for i in range(half_levels):
        for tt in range(2):
            ref = u_at(tt, i, 1 - y, c)
            pltpu.make_async_copy(ref, ref, uyr_sem.at[tt, i]).wait()
            u_core(tt, i, 1 - y, False).start()
    for i in range(half_levels):
        u_here(i).wait()
        for tt in range(2):
            for yy in range(2):
                ref = u_at(tt, i, yy, 1 - c)
                pltpu.make_async_copy(ref, ref, ucr_sem.at[tt, i, yy]).wait()

    for tt in range(2):
        for yy in range(2):
            for j in range(2):
                ref = att_all.at[tt, :, yy * cols + j * half_cols : yy * cols + (j + 1) * half_cols]
                pltpu.make_async_copy(ref, ref, ar_sem.at[tt, yy, j]).wait()

    for s in range(2):
        n_x, n_y, n_core, n_here = n_copies(s)
        n_x.wait_send()
        n_y.wait_send()

        @pl.when(c != y)
        def _():
            n_core.wait_send()

        for cc in range(2):
            @pl.when(c == y)
            def _():
                forward_y(cc, s).wait_send()

            @pl.when(c != y)
            def _():
                forward_x(cc, s).wait_send()

    mixed = n_send

    def slots_of(owner_group, lanes):
        return n_all.at[0, pl.ds(pl.multiple_of(owner_group * capacity, 16), capacity), lanes]

    def sending(f, lanes, owner_group):
        return pltpu.make_async_remote_copy(
            src_ref=slots_of(owner_group, lanes), dst_ref=out_ref.at[group, :, lanes],
            send_sem=send_sem.at[f, owner_group], recv_sem=recv_sem.at[f, group],
            device_id={"group": owner_group, "tp": t}, device_id_type=MESH,
        )

    def keeping(f, lanes):
        return pltpu.make_async_copy(slots_of(group, lanes), out_ref.at[group, :, lanes], keep_sem.at[f])

    cut = feat // 256 // 2 * 256 if SPLIT else 0
    spans = [slice(0, cut), slice(cut, feat)] if cut else [slice(0, feat)]
    planes = (3 - z, lax.rem(z + 2, 4), z + 1 - 2 * lax.rem(z, 2), z)
    for f, lanes in enumerate(spans):
        total = jnp.zeros((rows, lanes.stop - lanes.start), F32)
        for tt in range(2):
            term = lax.dot_general(
                att_all[tt], wo_all[tt, lanes, :], (((1,), (1,)), ((), ())), preferred_element_type=F32
            )
            total += term.astype(BF16).astype(F32)
        mixed[:, lanes] = (tokens_ref[:, lanes].astype(F32) + vectors_ref[1:, lanes] * total).astype(BF16)
        for plane in planes:
            slots = lax.broadcasted_iota(jnp.int32, (4 * capacity, rows), 0) + plane * 4 * capacity
            chosen = (slots == place).astype(F32).astype(BF16)
            picked = jnp.dot(chosen, mixed[:, lanes], preferred_element_type=F32).astype(BF16)
            n_all[0, pl.ds(pl.multiple_of(plane * 4 * capacity, 16), 4 * capacity), lanes] = picked
            for k in range(4):
                peer = plane * 4 + k

                @pl.when(peer == group)
                def _():
                    keeping(f, lanes).start()

                @pl.when(peer != group)
                def _():
                    sending(f, lanes, peer).start()

    for f, lanes in enumerate(spans):
        @pl.loop(1, count)
        def _(step):
            peer = lax.rem(group + step, count)
            sending(f, lanes, peer).wait_send()
            ref = out_ref.at[peer, :, lanes]
            pltpu.make_async_copy(ref, ref, recv_sem.at[f, peer]).wait()

        keeping(f, lanes).wait()

    for yy in range(2):
        @pl.when(jnp.logical_not(is_me(yy)))
        def _():
            for copy in pieces(yy):
                copy.wait_send()

    for half in range(2):
        for j in range(2):
            att_copy(1, half, j)[1].wait_send()
            mine, away, here = att_copy(0, half, j)

            @pl.when(jnp.logical_not(mine))
            def _():
                away.wait_send()

    for zz in range(levels):
        @pl.when(jnp.logical_and(zz <= z, edge_r))
        def _():
            u_right(zz).wait_send()

        @pl.when(jnp.logical_and(zz >= z, edge_l))
        def _():
            u_left(zz).wait_send()

    for i in range(half_levels):
        u_across(i).wait_send()
        for tt in range(2):
            u_over(tt, i, False).wait_send()
            for yy in range(2):
                u_core(tt, i, yy, False).wait_send()

    for j in range(4):
        for zz in range(levels):
            @pl.when(jnp.logical_and(zz <= z, edge_r))
            def _():
                go_right(j, zz).wait_send()

            @pl.when(jnp.logical_and(zz >= z, edge_l))
            def _():
                go_left(j, zz).wait_send()

            go_core(j, zz).wait_send()


def plane_call(turned, vectors, w, qk_gain, wo, request, owner, count, capacity):
    feat, rows = turned.shape
    depth, width = w.shape[1], w.shape[2]
    levels, cols = count // 4, width // 2
    heads = cols // HD
    padded = -(-depth // 16) * 16
    seam = rows + SHARE
    dma = pltpu.SemaphoreType.DMA
    vmem = pl.BlockSpec(memory_space=pltpu.VMEM)
    return pl.pallas_call(
        functools.partial(plane_kernel, levels),
        name="plane",
        out_shape=jax.ShapeDtypeStruct((count, capacity, feat), BF16),
        in_specs=[vmem] * 7,
        out_specs=pl.BlockSpec(memory_space=pl.ANY),
        scratch_shapes=[
            pltpu.VMEM((rows, feat), BF16),
            pltpu.VMEM((8, rows), F32),
            pltpu.VMEM((2, 3, padded, cols), BF16),
            pltpu.VMEM((2, 3, padded, cols), BF16),
            pltpu.VMEM((3, 2 * feat, cols), BF16),
            pltpu.VMEM((rows, feat), BF16),
            pltpu.VMEM((2, 2 * rows, feat), BF16),
            pltpu.VMEM((2, 8, rows), F32),
            pltpu.VMEM((8, rows), F32),
            pltpu.VMEM((8, rows), F32),
            pltpu.VMEM((2, 8, 2 * rows), F32),
            pltpu.VMEM((3, 2, 8, 2 * rows), F32),
            pltpu.VMEM((2, 2 * rows, cols), F32),
            pltpu.VMEM((2 * rows, cols), BF16),
            pltpu.VMEM((2 * rows, cols), BF16),
            pltpu.VMEM((2 * rows, cols), BF16),
            pltpu.VMEM((2, heads, rows, seam), BF16),
            pltpu.VMEM((2 * rows, cols), BF16),
            pltpu.VMEM((2, padded, width // 2), BF16),
            pltpu.VMEM((padded, width // 2), BF16),
            pltpu.VMEM((levels, 2 * depth, width // 2), BF16),
            pltpu.VMEM((2, feat, width), BF16),
            pltpu.VMEM((2, rows, width), BF16),
            dma((2, 3)), dma((2, 3)), dma((2,)), dma((2,)), dma, dma,
            dma((3, 2)), dma((2, 2, 2)), dma((2, 2)), dma((2, 2, 2)),
            dma((4, levels)), dma((4, levels)), dma((4, levels)), dma((4, levels)), dma((4, levels)),
            dma((3,)), dma((3,)),
            dma, dma, dma((levels,)), dma((levels,)), dma((levels,)), dma((2,)), dma((2,)), dma((2,)),
            dma((2, 2)), dma((2, 2)), dma((2, 2, 2)), dma((2, 2, 2)),
            dma((2, 2, 2)), dma((2, 2, 2)), dma((2, count)), dma((2, count)), dma((2,)),
        ],
        compiler_params=pltpu.CompilerParams(
            collective_id=1, has_side_effects=True, vmem_limit_bytes=53 * 2**20
        ),
        cost_estimate=pl.CostEstimate(
            flops=20 * rows * feat * width, transcendentals=2 * heads * rows * seam,
            bytes_accessed=8 * 2**20,
        ),
    )(turned, vectors, w, qk_gain, wo, request, owner)


def swapped(value, axis, apart):
    mask = 2**apart
    pairs = [(source, source ^ mask) for source in range(lax.axis_size(axis))]
    return lax.ppermute(value, axis, pairs)


def from_next(value, axis):
    count = lax.axis_size(axis)
    return lax.ppermute(value, axis, [((i + 1) % count, i) for i in range(count)])


def attend_kernel(q_ref, k_ref, v_ref, kp_ref, vp_ref, row_ref, own_ref, pair_ref, out_ref):
    query = q_ref[...]
    over = (((1,), (1,)), ((), ()))
    scale = 1.0 / math.sqrt(HD)
    near = lax.dot_general(query, k_ref[...], over, preferred_element_type=jnp.float32) * scale
    far = lax.dot_general(query, kp_ref[...], over, preferred_element_type=jnp.float32) * scale
    near = jnp.where(row_ref[...] == own_ref[...], near, -jnp.inf)
    far = jnp.where(row_ref[...] == pair_ref[...], far, -jnp.inf)
    top = jnp.maximum(
        jnp.max(near, axis=-1, keepdims=True), jnp.max(far, axis=-1, keepdims=True)
    )
    near, far = jnp.exp(near - top), jnp.exp(far - top)
    share = 1.0 / (jnp.sum(near, axis=-1, keepdims=True) + jnp.sum(far, axis=-1, keepdims=True))
    near, far = (near * share).astype(jnp.bfloat16), (far * share).astype(jnp.bfloat16)
    total = jnp.dot(near, v_ref[...], preferred_element_type=jnp.float32)
    total += jnp.dot(far, vp_ref[...], preferred_element_type=jnp.float32)
    out_ref[...] = total.astype(jnp.bfloat16)


def attend(query, keys, values, paired_keys, paired_values, ids, paired_ids):
    rows, width = query.shape
    seam = paired_keys.shape[0]
    block = pl.BlockSpec((rows, HD), lambda h: (0, h))
    seam_block = pl.BlockSpec((seam, HD), lambda h: (0, h))
    fixed = lambda shape: pl.BlockSpec(shape, lambda h: (0, 0))
    return pl.pallas_call(
        attend_kernel,
        grid=(width // HD,),
        out_shape=jax.ShapeDtypeStruct((rows, width), jnp.bfloat16),
        in_specs=[
            block, block, block, seam_block, seam_block,
            fixed((rows, 1)), fixed((1, rows)), fixed((1, seam)),
        ],
        out_specs=block,
        compiler_params=pltpu.CompilerParams(vmem_limit_bytes=32 * 2**20),
        cost_estimate=pl.CostEstimate(
            flops=4 * rows * (rows + seam) * width,
            transcendentals=rows * (rows + seam) * width // HD,
            bytes_accessed=8 * rows * width,
        ),
    )(
        query, keys, values, paired_keys, paired_values,
        ids[:, None], ids[None, :], paired_ids[None, :],
    )


def route_kernel(count, place_ref, mixed_ref, out_ref, outbox, send_sem, recv_sem, keep_sem):
    me = lax.axis_index("group")
    capacity = outbox.shape[1]
    rows = mixed_ref.shape[0]
    barrier = pltpu.get_barrier_semaphore()

    @pl.loop(1, count)
    def _(step):
        pl.semaphore_signal(
            barrier, inc=1, device_id={"group": lax.rem(me + step, count)},
            device_id_type=pl.DeviceIdType.MESH,
        )

    pl.semaphore_wait(barrier, count - 1)

    def pick(owner):
        slots = lax.broadcasted_iota(jnp.int32, (capacity, rows), 0) + owner * capacity
        select = (slots == place_ref[...]).astype(jnp.float32).astype(jnp.bfloat16)
        return jnp.dot(select, mixed_ref[...], preferred_element_type=jnp.float32).astype(
            jnp.bfloat16
        )

    def sending(step):
        ahead = 1 + lax.rem(step - 1 + count // 2 - 1, count - 1)
        peer = lax.rem(me + ahead, count)
        return peer, pltpu.make_async_remote_copy(
            src_ref=outbox.at[step],
            dst_ref=out_ref.at[me],
            send_sem=send_sem.at[step],
            recv_sem=recv_sem.at[me],
            device_id={"group": peer},
            device_id_type=pl.DeviceIdType.MESH,
        )

    @pl.loop(1, count)
    def _(step):
        peer, copy = sending(step)
        outbox[step] = pick(peer)
        copy.start()

    outbox[0] = pick(me)
    keep = pltpu.make_async_copy(outbox.at[0], out_ref.at[me], keep_sem)
    keep.start()

    @pl.loop(1, count)
    def _(step):
        source = lax.rem(me + step, count)
        pltpu.make_async_remote_copy(
            src_ref=outbox.at[step],
            dst_ref=out_ref.at[source],
            send_sem=send_sem.at[step],
            recv_sem=recv_sem.at[source],
            device_id={"group": source},
            device_id_type=pl.DeviceIdType.MESH,
        ).wait()

    keep.wait()


def route(place, mixed, count, capacity):
    rows, feat = mixed.shape
    return pl.pallas_call(
        lambda *refs: route_kernel(count, *refs),
        name="route",
        out_shape=jax.ShapeDtypeStruct((count, capacity, feat), jnp.bfloat16),
        in_specs=[pl.BlockSpec(memory_space=pltpu.VMEM)] * 2,
        out_specs=pl.BlockSpec(memory_space=pl.ANY),
        scratch_shapes=[
            pltpu.VMEM((count, capacity, feat), jnp.bfloat16),
            pltpu.SemaphoreType.DMA((count,)),
            pltpu.SemaphoreType.DMA((count,)),
            pltpu.SemaphoreType.DMA,
        ],
        compiler_params=pltpu.CompilerParams(
            collective_id=0, has_side_effects=True, vmem_limit_bytes=32 * 2**20
        ),
        cost_estimate=pl.CostEstimate(
            flops=2 * count * capacity * rows * feat,
            transcendentals=0,
            bytes_accessed=4 * count * capacity * feat,
        ),
    )(place[None, :], mixed)


def spread_shards(tokens, norm_gain, w_qkv, qk_gain, w_out, layer_scale, request, owner):
    rows, feat_local = tokens.shape
    tp_count = lax.axis_size("tp")
    group_count = lax.axis_size("group")
    local_width = w_qkv.shape[2]
    head_count = local_width // HD
    me_tp = lax.axis_index("tp")
    w_all = lax.all_gather(
        w_qkv.reshape(w_qkv.shape[0], 3 * local_width), "group", axis=0, tiled=True
    )
    whole = jnp.zeros((rows, feat_local * tp_count), jnp.bfloat16)
    gain_all = jnp.zeros((1, feat_local * tp_count), jnp.bfloat16)
    piece, gain = tokens, norm_gain.reshape(1, feat_local)
    for step in range(tp_count):
        at = ((me_tp + step) % tp_count) * feat_local
        whole = lax.dynamic_update_slice(whole, piece, (0, at))
        gain_all = lax.dynamic_update_slice(gain_all, gain, (0, at))
        if step < tp_count - 1:
            piece, gain = from_next(piece, "tp"), from_next(gain, "tp")
    whole, late_out = lax.optimization_barrier((whole, w_out))
    per = group_count // tp_count
    pairs = []
    for g in range(group_count):
        for b in range(tp_count):
            t, j = g // per, g % per
            to_g = b * per + j
            pairs.append((g * tp_count + b, to_g * tp_count + t))
    w_piece = lax.ppermute(late_out.T, ("group", "tp"), pairs)
    w_o = lax.all_gather(w_piece, "group", axis=0, tiled=True)
    w_o = w_o.reshape(tp_count, feat_local, local_width)
    xwide = whole.astype(jnp.float32)
    stat = jnp.mean(xwide * xwide, axis=-1, keepdims=True)
    normed = (xwide * lax.rsqrt(stat + 1e-06) * gain_all.astype(jnp.float32)).astype(jnp.bfloat16)
    qkv = jnp.dot(normed, w_all, preferred_element_type=jnp.float32)
    query = qkv[:, :local_width]
    key_rows = qkv[:, local_width : 2 * local_width]
    value = qkv[:, 2 * local_width :].astype(jnp.bfloat16)
    qsum, ksum = lax.psum(
        (jnp.sum(query * query, axis=-1), jnp.sum(key_rows * key_rows, axis=-1)), "tp"
    )
    total_width = local_width * tp_count
    qnorm = (query * lax.rsqrt(qsum / total_width + 1e-06)[:, None] * qk_gain[0]).astype(
        jnp.bfloat16
    )
    knorm = (key_rows * lax.rsqrt(ksum / total_width + 1e-06)[:, None] * qk_gain[1]).astype(
        jnp.bfloat16
    )
    parity = lax.axis_index("group") % 2
    seam = jnp.where(parity == 0, rows - SHARE, 0).astype(jnp.int32)
    key_window = lax.dynamic_slice_in_dim(knorm, seam, SHARE, 0)
    id_window = lax.dynamic_slice_in_dim(request, seam, SHARE, 0)
    paired_keys, paired_ids = swapped((key_window, id_window), "group", 0)
    value_window = lax.dynamic_slice_in_dim(value, seam, SHARE, 0)
    paired_values = swapped(value_window, "group", 0)
    attended = attend(qnorm, knorm, value, paired_keys, paired_values, request, paired_ids)

    branch = jnp.zeros((rows, feat_local), jnp.float32)
    for step in range(tp_count):
        onward = from_next(attended, "tp") if step < tp_count - 1 else None
        part = lax.dot_general(
            attended,
            lax.dynamic_index_in_dim(w_o, (me_tp + step) % tp_count, 0, keepdims=False),
            (((1,), (1,)), ((), ())),
            preferred_element_type=jnp.float32,
        )
        branch = branch + part.astype(jnp.bfloat16).astype(jnp.float32)
        attended = onward
    mixed = (tokens.astype(jnp.float32) + layer_scale * branch).astype(jnp.bfloat16)

    capacity = max(2, 2 * rows // group_count)
    target = owner[:, 0]
    onehot = target[:, None] == jnp.arange(group_count, dtype=jnp.int32)[None, :]
    order = jnp.arange(rows, dtype=jnp.int32)
    before = (order[:, None] > order[None, :]).astype(jnp.bfloat16)
    ranks = jnp.dot(before, onehot.astype(jnp.bfloat16), preferred_element_type=jnp.float32)
    slot = jnp.sum(jnp.where(onehot, ranks, 0.0), axis=-1).astype(jnp.int32)
    place = target * capacity + slot
    inbox = route(place, mixed, group_count, capacity)
    return inbox[None]


def plane_shards(tokens, norm_gain, w_qkv, qk_gain, w_out, layer_scale, request, owner):
    count = lax.axis_size("group")
    capacity = max(2, 2 * tokens.shape[0] // count)
    return plane_call(
        tokens.T, jnp.stack([norm_gain.astype(F32), layer_scale]), w_qkv.transpose(1, 0, 2), qk_gain, w_out.T,
        request[None, :], owner.T, count, capacity,
    )[None]


def shards(*arrays):
    w_qkv = arrays[2]
    count, tp = lax.axis_size("group"), lax.axis_size("tp")
    whole_tiles = 2 * w_qkv.shape[0] % 16 == 0 and w_qkv.shape[2] % (2 * HD) == 0
    if tp == 2 and count == 16 and whole_tiles:
        return plane_shards(*arrays)
    return spread_shards(*arrays)


def solution(mesh):
    in_specs = (
        P("group", "tp"),
        P("tp"),
        P("group", None, "tp"),
        P(None, "tp"),
        P("tp", "group"),
        P("tp"),
        P("group"),
        P("group", None),
    )
    out_specs = P("group", None, None, "tp")
    return jax.shard_map(shards, mesh=mesh, in_specs=in_specs, out_specs=out_specs, check_vma=False)
```

```python
import functools
import math

import jax
import jax.numpy as jnp
from jax import lax
from jax.experimental import pallas as pl
from jax.experimental.pallas import tpu as pltpu
from jax.sharding import PartitionSpec as P

HD = 128
SHARE = 128


MESH = pl.DeviceIdType.MESH
BF16 = jnp.bfloat16
F32 = jnp.float32


def to_row(column):
    spread = jnp.broadcast_to(column, (column.shape[0], 128))
    return jnp.transpose(spread)[:8]


def to_column(row):
    spread = jnp.broadcast_to(row, (128, row.shape[1]))
    return jnp.transpose(spread)[:, :1]


def plane_kernel(
    levels, turned_ref, vectors_ref, w_ref, qk_gain_ref, wo_ref, request_ref, owner_ref, out_ref,
    tokens_ref, ids_ref, w_send, w_got, w_all, n_send, n_all, ids_all, sum_mine, sum_got, qk_mine, qk_got,
    qk_wide, qn, kn, vb, probs, att, wo_send, wo_got, wo_line, wo_all, att_all,
    ws_sem, wr_sem, is_sem, ir_sem, ss_sem, sr_sem, ns_sem, nr_sem, nf_sem, nfr_sem,
    right_sem, left_sem, chain_sem, core_s_sem, core_r_sem, qs_sem, qr_sem,
    wos_sem, wor_sem, uright_sem, uleft_sem, uchain_sem, uhere_sem, ux_sem, uxr_sem, uy_sem, uyr_sem, uc_sem, ucr_sem,
    as_sem, ar_sem, send_sem, recv_sem, keep_sem,
):
    group, t = lax.axis_index("group"), lax.axis_index("tp")
    z, y, c = group // 4, lax.rem(group // 2, 2), lax.rem(group, 2)
    rows, feat = tokens_ref.shape
    count, capacity = out_ref.shape[:2]
    slab = w_all.shape[1] // (2 * levels)
    depth = w_ref.shape[1]
    cols = w_all.shape[2]
    heads = cols // HD
    sub = rows // 2
    part = sub * 5 // 16
    half_cols = cols // 2
    edge_r, edge_l = z < levels - 1, z > 0

    def at(zz, yy, cc):
        return (zz * 2 + yy) * 2 + cc

    def remote(src, dst, send, recv, place, tt):
        return pltpu.make_async_remote_copy(
            src_ref=src, dst_ref=dst, send_sem=send, recv_sem=recv,
            device_id={"group": place, "tp": tt}, device_id_type=MESH,
        )

    barrier = pltpu.get_barrier_semaphore()

    @pl.loop(1, count)
    def _(step):
        pl.semaphore_signal(
            barrier, inc=1, device_id={"group": lax.rem(group + step, count), "tp": t}, device_id_type=MESH
        )

    for k in range(4):
        pl.semaphore_signal(
            barrier, inc=1, device_id={"group": z * 4 + k, "tp": lax.rem(t + 1, 2)}, device_id_type=MESH
        )

    for yy in range(2):
        w_send[yy, :, :depth, :] = w_ref[:, :, yy * cols : (yy + 1) * cols]

    half_out = wo_ref.shape[1] // 2
    for cc in range(2):
        wo_send[cc, :depth, :] = wo_ref[:, cc * half_out : (cc + 1) * half_out]
    ids_ref[...] = jnp.broadcast_to(request_ref[...].astype(F32), (8, rows))
    pl.semaphore_wait(barrier, count + 3)

    def pieces(yy):
        place = at(z, yy, y)
        copies = [
            remote(w_send.at[yy, j], w_got.at[c, j], ws_sem.at[yy, j], wr_sem.at[c, j], place, t) for j in range(3)
        ]
        return copies[:2] + [remote(ids_ref, ids_all.at[c], is_sem.at[yy], ir_sem.at[c], place, t)] + copies[2:]

    def kept(yy):
        copies = [pltpu.make_async_copy(w_send.at[yy, j], w_got.at[c, j], wr_sem.at[c, j]) for j in range(3)]
        return copies[:2] + [pltpu.make_async_copy(ids_ref, ids_all.at[c], ir_sem.at[c])] + copies[2:]

    def is_me(yy):
        return jnp.logical_and(y == yy, c == y)

    def start_pieces(which):
        for yy in range(2):
            @pl.when(is_me(yy))
            def _():
                for copy in kept(yy)[which]:
                    copy.start()

            @pl.when(jnp.logical_not(is_me(yy)))
            def _():
                for copy in pieces(yy)[which]:
                    copy.start()

    start_pieces(slice(0, 3))
    wo_swap = remote(wo_send.at[1 - c], wo_got, wos_sem, wor_sem, at(z, y, 1 - c), t)
    wo_swap.start()

    wide = turned_ref[...].astype(F32)
    sum_mine[...] = jnp.broadcast_to(jnp.sum(wide * wide, axis=0, keepdims=True), (8, rows))
    swap = remote(sum_mine, sum_got, ss_sem, sr_sem, group, lax.rem(t + 1, 2))
    swap.start()

    def rows_of(zz, cc):
        return pl.ds(pl.multiple_of((zz * 2 + cc) * slab, 16), slab)

    def piece(j, zz, cc):
        if j < 2:
            return w_all.at[j, rows_of(zz, cc), :]
        return w_all.at[2, rows_of(zz, cc), (j - 2) * half_cols : (j - 1) * half_cols]

    def go_right(j, zz):
        return remote(piece(j, zz, c), piece(j, zz, c), right_sem.at[j, zz], chain_sem.at[j, zz], group + 4, t)

    def go_left(j, zz):
        return remote(piece(j, zz, c), piece(j, zz, c), left_sem.at[j, zz], chain_sem.at[j, zz], group - 4, t)

    def go_core(j, zz):
        return remote(
            piece(j, zz, c), piece(j, zz, c), core_s_sem.at[j, zz], core_r_sem.at[j, zz],
            at(z, y, 1 - c), t,
        )

    def build(j):
        for cc in range(2):
            pltpu.make_async_copy(w_send.at[0, j], w_got.at[cc, j], wr_sem.at[cc, j]).wait()
        both = jnp.concatenate(
            [w_got[0, j].astype(F32)[:depth], w_got[1, j].astype(F32)[:depth]], axis=0
        )
        w_all[j, rows_of(z, c), :] = both.astype(BF16)

    def send_own(j):
        @pl.when(edge_r)
        def _():
            go_right(j, z).start()

        @pl.when(edge_l)
        def _():
            go_left(j, z).start()

        go_core(j, z).start()

    def arrive(j, d):
        @pl.when(z - d >= 0)
        def _():
            go_right(j, z - d).wait_recv()

            @pl.when(edge_r)
            def _():
                go_right(j, z - d).start()

            go_core(j, z - d).start()

        @pl.when(z + d < levels)
        def _():
            go_left(j, z + d).wait_recv()

            @pl.when(edge_l)
            def _():
                go_left(j, z + d).start()

            go_core(j, z + d).start()

    other_t = lax.rem(t + 1, 2)
    half_levels = levels // 2
    lanes_out = wo_all.shape[2] // 2

    def u_at(tt, i, yy, cc):
        return wo_all.at[
            tt, pl.ds(pl.multiple_of((i * 2 + yy) * slab, 16), slab),
            pl.ds(pl.multiple_of(cc * lanes_out, 128), lanes_out),
        ]

    def u_right(zz):
        return remote(wo_line.at[zz], wo_line.at[zz], uright_sem.at[zz], uchain_sem.at[zz], group + 4, t)

    def u_left(zz):
        return remote(wo_line.at[zz], wo_line.at[zz], uleft_sem.at[zz], uchain_sem.at[zz], group - 4, t)

    def u_here(i):
        return pltpu.make_async_copy(wo_line.at[t * half_levels + i], u_at(t, i, y, c), uhere_sem.at[i])

    def u_across(i):
        zz = other_t * half_levels + i
        return remote(wo_line.at[zz], u_at(t, i, y, c), ux_sem.at[i], uxr_sem.at[i], group, other_t)

    def u_over(tt, i, line):
        src = wo_line.at[t * half_levels + i] if line else u_at(tt, i, y, c)
        return remote(src, u_at(tt, i, y, c), uy_sem.at[tt, i], uyr_sem.at[tt, i], at(z, 1 - y, c), t)

    def u_core(tt, i, yy, line):
        src = wo_line.at[t * half_levels + i] if line else u_at(tt, i, yy, c)
        return remote(
            src, u_at(tt, i, yy, c), uc_sem.at[tt, i, yy], ucr_sem.at[tt, i, yy], at(z, y, 1 - c), t
        )

    def u_hops(zz):
        i = lax.rem(zz, half_levels)
        wanted = zz // half_levels == t

        @pl.when(wanted)
        def _():
            u_here(i).start()
            u_over(t, i, True).start()
            u_core(t, i, y, True).start()

        @pl.when(jnp.logical_not(wanted))
        def _():
            u_across(i).start()

    def u_own():
        wo_swap.wait()
        mine, theirs = wo_send[c].astype(F32)[:depth], wo_got[...].astype(F32)[:depth]
        low, high = jnp.where(c == 0, mine, theirs), jnp.where(c == 0, theirs, mine)
        wo_line[z] = jnp.concatenate([low, high], axis=0).astype(BF16)

        @pl.when(edge_r)
        def _():
            u_right(z).start()

        @pl.when(edge_l)
        def _():
            u_left(z).start()

    def u_arrive(d):
        @pl.when(z - d >= 0)
        def _():
            u_right(z - d).wait_recv()

            @pl.when(edge_r)
            def _():
                u_right(z - d).start()

        @pl.when(z + d < levels)
        def _():
            u_left(z + d).wait_recv()

            @pl.when(edge_l)
            def _():
                u_left(z + d).start()

    def u_hops_of(d):
        @pl.when(z - d >= 0)
        def _():
            u_hops(z - d)

        @pl.when(z + d < levels)
        def _():
            u_hops(z + d)

    def ux_take(d):
        for zz in ((z - d, z + d) if d else (z,)):
            here = jnp.logical_and(jnp.logical_and(zz >= 0, zz < levels), (zz + levels) // half_levels == t + 2)

            @pl.when(here)
            def _():
                i = lax.rem(zz, half_levels)
                ref = u_at(other_t, i, y, c)
                pltpu.make_async_copy(ref, ref, uxr_sem.at[i]).wait()
                u_over(other_t, i, False).start()
                u_core(other_t, i, y, False).start()

    inner = jnp.logical_and(edge_l, edge_r)
    outer = jnp.logical_not(inner)
    def own_first():
        for j in range(2):
            build(j)
            send_own(j)

    pl.when(c == y)(own_first)

    tokens_ref[...] = jnp.transpose(turned_ref[...].astype(F32)).astype(BF16)
    swap.wait()
    whole = sum_mine[...] + sum_got[...]
    factor = to_column(lax.rsqrt(whole[:1] / (2 * feat) + 1e-06))

    def n_rows(cc, start, size):
        return pl.ds(pl.multiple_of(cc * rows + start, 16), size)

    def n_copies(s):
        src = n_send.at[s * sub : (s + 1) * sub, :]
        dst = n_all.at[t, n_rows(c, s * sub, sub), :]
        recv = nr_sem.at[t, c, s]
        return (
            remote(src, dst, ns_sem.at[0, s], recv, at(z, y, y), lax.rem(t + 1, 2)),
            remote(src, dst, ns_sem.at[1, s], recv, at(z, 1 - y, y), t),
            remote(src, dst, ns_sem.at[2, s], recv, at(z, y, y), t),
            pltpu.make_async_copy(src, dst, recv),
        )

    for s in range(2):
        span = slice(s * sub, (s + 1) * sub)
        n_send[span, :] = (
            tokens_ref[span, :].astype(F32) * factor[span] * vectors_ref[:1, :]
        ).astype(BF16)
        n_x, n_y, n_core, n_here = n_copies(s)
        n_x.start()
        n_y.start()

        @pl.when(c == y)
        def _():
            n_here.start()

        @pl.when(c != y)
        def _():
            n_core.start()

    def n_wait(tt, cc, s):
        ref = n_all.at[tt, n_rows(cc, s * sub, sub), :]
        pltpu.make_async_copy(ref, ref, nr_sem.at[tt, cc, s]).wait()


    def forward_y(cc, s):
        ref = n_all.at[other_t, n_rows(cc, s * sub, part), :]
        return remote(ref, ref, nf_sem.at[cc, s], nfr_sem.at[0, cc, s], at(z, 1 - y, c), t)

    def forward_x(cc, s):
        ref = n_all.at[t, n_rows(cc, s * sub + part, sub - part), :]
        return remote(ref, ref, nf_sem.at[cc, s], nfr_sem.at[1, cc, s], group, other_t)

    def n_forward(s):
        for cc in range(2):
            @pl.when(c == y)
            def _():
                n_wait(other_t, cc, s)
                forward_y(cc, s).start()

            @pl.when(c != y)
            def _():
                n_wait(t, cc, s)
                forward_x(cc, s).start()

    pl.when(c != y)(own_first)
    start_pieces(slice(3, 4))
    arrive(0, 1)
    arrive(1, 1)
    u_own()
    build(2)

    @pl.when(outer)
    def _():
        send_own(2)
        send_own(3)

    n_forward(0)
    arrive(0, 2)
    arrive(1, 2)

    @pl.when(inner)
    def _():
        u_arrive(1)

    n_forward(1)

    @pl.when(inner)
    def _():
        send_own(2)
        send_own(3)

    def n_rest(s):
        for cc in range(2):
            @pl.when(c == y)
            def _():
                n_wait(t, cc, s)

            @pl.when(c != y)
            def _():
                for way, (start, size) in enumerate(((0, part), (part, sub - part))):
                    ref = n_all.at[other_t, n_rows(cc, s * sub + start, size), :]
                    pltpu.make_async_copy(ref, ref, nfr_sem.at[way, cc, s]).wait()

    def core_wait(j):
        for zz in range(levels):
            remote(
                piece(j, zz, 1 - c), piece(j, zz, 1 - c), core_s_sem.at[j, zz], core_r_sem.at[j, zz],
                at(z, y, 1 - c), t,
            ).wait_recv()

    def project(j, start, size, lanes):
        return jnp.dot(
            n_all[0, pl.ds(start, size), :], w_all[j, :feat, lanes], preferred_element_type=F32
        ) + jnp.dot(n_all[1, pl.ds(start, size), :], w_all[j, feat:, lanes], preferred_element_type=F32)

    arrive(0, 3)
    arrive(1, 3)
    core_wait(0)
    core_wait(1)
    for s in range(2):
        n_rest(s)
        if s:
            u_hops(z)

            @pl.when(inner)
            def _():
                u_hops_of(1)
                arrive(2, 1)
                arrive(3, 1)

        @pl.loop(0, 2)
        def _(cc):
            start = pl.multiple_of(cc * rows + s * sub, sub)
            for j in range(2):
                out = project(j, start, sub, slice(None))
                qk_wide[j, pl.ds(start, sub), :] = out
                qk_mine[j, :, pl.ds(start, sub)] = to_row(jnp.sum(out * out, axis=-1, keepdims=True))

    def stat_swap(k):
        return remote(
            qk_mine, qk_got.at[k - 1], qs_sem.at[k - 1], qr_sem.at[k - 1],
            at(z, lax.rem(y + k % 2, 2), c), lax.rem(t + k // 2, 2),
        )

    for k in range(1, 4):
        stat_swap(k).start()
    ux_take(0)

    @pl.when(inner)
    def _():
        arrive(2, 2)

    @pl.when(outer)
    def _():
        u_arrive(1)
        u_hops_of(1)

    for k in range(1, 4):
        stat_swap(k).wait()
    stats = qk_mine[...] + qk_got[0] + qk_got[1] + qk_got[2]
    factors = lax.rsqrt(stats / (4 * cols) + 1e-06)
    for j, ref in ((0, qn), (1, kn)):
        column = to_column(factors[j, :1])
        near = qk_gain_ref[j : j + 1, :cols]
        far = qk_gain_ref[j : j + 1, cols:]
        gains = jnp.where(y == 0, near, far)
        ref[...] = (qk_wide[j] * column * gains).astype(BF16)

    for cc in range(2):
        pltpu.make_async_copy(ids_ref, ids_all.at[cc], ir_sem.at[cc]).wait()
    seam = rows + SHARE
    scale = 1.0 / math.sqrt(HD)
    ids = jnp.concatenate([ids_all[0, :1], ids_all[1, :1]], axis=1)
    for half in range(2):
        first = half * (rows - SHARE)
        same = to_column(ids[:, half * rows : (half + 1) * rows]) == ids[:, first : first + seam]

        @pl.loop(0, heads)
        def _(h):
            lanes = pl.ds(pl.multiple_of(h * HD, HD), HD)
            scores = lax.dot_general(
                qn[half * rows : (half + 1) * rows, lanes], kn[first : first + seam, lanes],
                (((1,), (1,)), ((), ())), preferred_element_type=F32,
            ) * scale
            scores = jnp.where(same, scores, -jnp.inf)
            expo = jnp.exp(scores - jnp.max(scores, axis=-1, keepdims=True))
            share = 1.0 / jnp.sum(expo, axis=-1, keepdims=True)
            probs[half, h] = (expo * share).astype(BF16)

        if half == 0:
            @pl.when(inner)
            def _():
                arrive(3, 2)
                u_arrive(2)

            @pl.when(outer)
            def _():
                u_arrive(2)
                u_hops_of(2)

            ux_take(1)
        else:
            @pl.when(outer)
            def _():
                ux_take(2)

    def att_copy(dt, half, j):
        src = att.at[half * rows : (half + 1) * rows, j * half_cols : (j + 1) * half_cols]
        dst = att_all.at[t, :, pl.ds(pl.multiple_of(y * cols + j * half_cols, 128), half_cols)]
        mine = jnp.logical_and(y == c, c == half)
        recv = ar_sem.at[t, y, j]
        away = remote(src, dst, as_sem.at[dt, half, j], recv, at(z, c, half), lax.rem(t + dt, 2))
        return mine, away, pltpu.make_async_copy(src, dst, recv)

    def uy_take(i):
        for tt in range(2):
            ref = u_at(tt, i, 1 - y, c)
            pltpu.make_async_copy(ref, ref, uyr_sem.at[tt, i]).wait()
            u_core(tt, i, 1 - y, False).start()

    def u_ready(i):
        u_here(i).wait()
        for tt in range(2):
            for yy in range(2):
                ref = u_at(tt, i, yy, 1 - c)
                pltpu.make_async_copy(ref, ref, ucr_sem.at[tt, i, yy]).wait()

    upper = z // half_levels
    for j in range(2):
        @pl.when(outer)
        def _():
            for d in range(1, levels):
                arrive(2 + j, d)

        core_wait(2 + j)
        span = slice(j * half_cols, (j + 1) * half_cols)

        @pl.loop(0, 2)
        def _(i):
            start = pl.multiple_of(i * rows, rows)
            vb[pl.ds(start, rows), span] = project(2, start, rows, span).astype(BF16)

        for half in range(2):
            first = half * (rows - SHARE)
            for h in range(j * heads // 2, (j + 1) * heads // 2):
                lanes = slice(h * HD, (h + 1) * HD)
                att[half * rows : (half + 1) * rows, lanes] = jnp.dot(
                    probs[half, h], vb[first : first + seam, lanes], preferred_element_type=F32
                ).astype(BF16)

            att_copy(1, half, j)[1].start()
            mine, away, here = att_copy(0, half, j)

            @pl.when(mine)
            def _():
                here.start()

            @pl.when(jnp.logical_not(mine))
            def _():
                away.start()

        if j == 0:
            uy_take(upper)
        else:
            @pl.when(inner)
            def _():
                u_hops_of(2)

            @pl.when(outer)
            def _():
                u_arrive(3)
                u_hops_of(3)

    target = owner_ref[...]
    named = lax.broadcasted_iota(jnp.int32, (count, rows), 0) == target
    earlier = lax.broadcasted_iota(jnp.int32, (rows, rows), 0) < lax.broadcasted_iota(jnp.int32, (rows, rows), 1)
    ranks = jnp.dot(
        named.astype(F32).astype(BF16), earlier.astype(F32).astype(BF16), preferred_element_type=F32
    )
    slot = jnp.sum(jnp.where(named, ranks, 0.0), axis=0, keepdims=True).astype(jnp.int32)
    place = target * capacity + slot

    for tt in range(2):
        for yy in range(2):
            for j in range(2):
                ref = att_all.at[tt, :, yy * cols + j * half_cols : yy * cols + (j + 1) * half_cols]
                pltpu.make_async_copy(ref, ref, ar_sem.at[tt, yy, j]).wait()

    u_ready(upper)

    for s in range(2):
        n_x, n_y, n_core, n_here = n_copies(s)
        n_x.wait_send()
        n_y.wait_send()

        @pl.when(c != y)
        def _():
            n_core.wait_send()

        for cc in range(2):
            @pl.when(c == y)
            def _():
                forward_y(cc, s).wait_send()

            @pl.when(c != y)
            def _():
                forward_x(cc, s).wait_send()

    mixed = n_send

    def slots_of(owner_group, lanes):
        return n_all.at[0, pl.ds(pl.multiple_of(owner_group * capacity, 16), capacity), lanes]

    def sending(f, lanes, owner_group):
        return pltpu.make_async_remote_copy(
            src_ref=slots_of(owner_group, lanes), dst_ref=out_ref.at[group, :, lanes],
            send_sem=send_sem.at[f, owner_group], recv_sem=recv_sem.at[group],
            device_id={"group": owner_group, "tp": t}, device_id_type=MESH,
        )

    def keeping(f, lanes):
        return pltpu.make_async_copy(slots_of(group, lanes), out_ref.at[group, :, lanes], keep_sem.at[f])

    middle = feat // 2
    below, above = middle // 128 * 128, -(-middle // 128) * 128
    spans = (
        (slice(0, below), slice(below, feat)),
        (slice(above, feat), slice(0, above)),
    )
    planes = (3 - z, lax.rem(z + 2, 4), z + 1 - 2 * lax.rem(z, 2), z)

    def finish(f, lanes):
        total = jnp.zeros((rows, lanes.stop - lanes.start), F32)
        for tt in range(2):
            term = lax.dot_general(
                att_all[tt], wo_all[tt, lanes, :], (((1,), (1,)), ((), ())), preferred_element_type=F32
            )
            total += term.astype(BF16).astype(F32)
        mixed[:, lanes] = (tokens_ref[:, lanes].astype(F32) + vectors_ref[1:, lanes] * total).astype(BF16)
        for plane in planes:
            slots = lax.broadcasted_iota(jnp.int32, (4 * capacity, rows), 0) + plane * 4 * capacity
            chosen = (slots == place).astype(F32).astype(BF16)
            picked = jnp.dot(chosen, mixed[:, lanes], preferred_element_type=F32).astype(BF16)
            n_all[0, pl.ds(pl.multiple_of(plane * 4 * capacity, 16), 4 * capacity), lanes] = picked
            for k in range(4):
                peer = plane * 4 + k

                @pl.when(peer == group)
                def _():
                    keeping(f, lanes).start()

                @pl.when(peer != group)
                def _():
                    sending(f, lanes, peer).start()

    def left(f, lanes):
        @pl.loop(1, count)
        def _(step):
            sending(f, lanes, lax.rem(group + step, count)).wait_send()

        keeping(f, lanes).wait()

    for f in range(2):
        if f:
            @pl.when(inner)
            def _():
                ux_take(2)

            ux_take(3)
            uy_take(1 - upper)
            u_ready(1 - upper)

        for which in range(2):
            @pl.when(upper == which)
            def _():
                finish(f, spans[which][f])

    for f in range(2):
        for which in range(2):
            @pl.when(upper == which)
            def _():
                left(f, spans[which][f])

    @pl.loop(1, count)
    def _(step):
        ref = out_ref.at[lax.rem(group + step, count)]
        pltpu.make_async_copy(ref, ref, recv_sem.at[lax.rem(group + step, count)]).wait()

    for yy in range(2):
        @pl.when(jnp.logical_not(is_me(yy)))
        def _():
            for copy in pieces(yy):
                copy.wait_send()

    for half in range(2):
        for j in range(2):
            att_copy(1, half, j)[1].wait_send()
            mine, away, here = att_copy(0, half, j)

            @pl.when(jnp.logical_not(mine))
            def _():
                away.wait_send()

    for zz in range(levels):
        @pl.when(jnp.logical_and(zz <= z, edge_r))
        def _():
            u_right(zz).wait_send()

        @pl.when(jnp.logical_and(zz >= z, edge_l))
        def _():
            u_left(zz).wait_send()

    for i in range(half_levels):
        u_across(i).wait_send()
        for tt in range(2):
            u_over(tt, i, False).wait_send()
            for yy in range(2):
                u_core(tt, i, yy, False).wait_send()

    for j in range(4):
        for zz in range(levels):
            @pl.when(jnp.logical_and(zz <= z, edge_r))
            def _():
                go_right(j, zz).wait_send()

            @pl.when(jnp.logical_and(zz >= z, edge_l))
            def _():
                go_left(j, zz).wait_send()

            go_core(j, zz).wait_send()


def plane_call(turned, vectors, w, qk_gain, wo, request, owner, count, capacity):
    feat, rows = turned.shape
    depth, width = w.shape[1], w.shape[2]
    levels, cols = count // 4, width // 2
    heads = cols // HD
    padded = -(-depth // 16) * 16
    seam = rows + SHARE
    dma = pltpu.SemaphoreType.DMA
    vmem = pl.BlockSpec(memory_space=pltpu.VMEM)
    return pl.pallas_call(
        functools.partial(plane_kernel, levels),
        name="plane",
        out_shape=jax.ShapeDtypeStruct((count, capacity, feat), BF16),
        in_specs=[vmem] * 7,
        out_specs=pl.BlockSpec(memory_space=pl.ANY),
        scratch_shapes=[
            pltpu.VMEM((rows, feat), BF16),
            pltpu.VMEM((8, rows), F32),
            pltpu.VMEM((2, 3, padded, cols), BF16),
            pltpu.VMEM((2, 3, padded, cols), BF16),
            pltpu.VMEM((3, 2 * feat, cols), BF16),
            pltpu.VMEM((rows, feat), BF16),
            pltpu.VMEM((2, 2 * rows, feat), BF16),
            pltpu.VMEM((2, 8, rows), F32),
            pltpu.VMEM((8, rows), F32),
            pltpu.VMEM((8, rows), F32),
            pltpu.VMEM((2, 8, 2 * rows), F32),
            pltpu.VMEM((3, 2, 8, 2 * rows), F32),
            pltpu.VMEM((2, 2 * rows, cols), F32),
            pltpu.VMEM((2 * rows, cols), BF16),
            pltpu.VMEM((2 * rows, cols), BF16),
            pltpu.VMEM((2 * rows, cols), BF16),
            pltpu.VMEM((2, heads, rows, seam), BF16),
            pltpu.VMEM((2 * rows, cols), BF16),
            pltpu.VMEM((2, padded, width // 2), BF16),
            pltpu.VMEM((padded, width // 2), BF16),
            pltpu.VMEM((levels, 2 * depth, width // 2), BF16),
            pltpu.VMEM((2, feat, width), BF16),
            pltpu.VMEM((2, rows, width), BF16),
            dma((2, 3)), dma((2, 3)), dma((2,)), dma((2,)), dma, dma,
            dma((3, 2)), dma((2, 2, 2)), dma((2, 2)), dma((2, 2, 2)),
            dma((4, levels)), dma((4, levels)), dma((4, levels)), dma((4, levels)), dma((4, levels)),
            dma((3,)), dma((3,)),
            dma, dma, dma((levels,)), dma((levels,)), dma((levels,)), dma((2,)), dma((2,)), dma((2,)),
            dma((2, 2)), dma((2, 2)), dma((2, 2, 2)), dma((2, 2, 2)),
            dma((2, 2, 2)), dma((2, 2, 2)), dma((2, count)), dma((count,)), dma((2,)),
        ],
        compiler_params=pltpu.CompilerParams(
            collective_id=1, has_side_effects=True, vmem_limit_bytes=60 * 2**20
        ),
        cost_estimate=pl.CostEstimate(
            flops=20 * rows * feat * width, transcendentals=2 * heads * rows * seam,
            bytes_accessed=8 * 2**20,
        ),
    )(turned, vectors, w, qk_gain, wo, request, owner)


def swapped(value, axis, apart):
    mask = 2**apart
    pairs = [(source, source ^ mask) for source in range(lax.axis_size(axis))]
    return lax.ppermute(value, axis, pairs)


def from_next(value, axis):
    count = lax.axis_size(axis)
    return lax.ppermute(value, axis, [((i + 1) % count, i) for i in range(count)])


def attend_kernel(q_ref, k_ref, v_ref, kp_ref, vp_ref, row_ref, own_ref, pair_ref, out_ref):
    query = q_ref[...]
    over = (((1,), (1,)), ((), ()))
    scale = 1.0 / math.sqrt(HD)
    near = lax.dot_general(query, k_ref[...], over, preferred_element_type=jnp.float32) * scale
    far = lax.dot_general(query, kp_ref[...], over, preferred_element_type=jnp.float32) * scale
    near = jnp.where(row_ref[...] == own_ref[...], near, -jnp.inf)
    far = jnp.where(row_ref[...] == pair_ref[...], far, -jnp.inf)
    top = jnp.maximum(
        jnp.max(near, axis=-1, keepdims=True), jnp.max(far, axis=-1, keepdims=True)
    )
    near, far = jnp.exp(near - top), jnp.exp(far - top)
    share = 1.0 / (jnp.sum(near, axis=-1, keepdims=True) + jnp.sum(far, axis=-1, keepdims=True))
    near, far = (near * share).astype(jnp.bfloat16), (far * share).astype(jnp.bfloat16)
    total = jnp.dot(near, v_ref[...], preferred_element_type=jnp.float32)
    total += jnp.dot(far, vp_ref[...], preferred_element_type=jnp.float32)
    out_ref[...] = total.astype(jnp.bfloat16)


def attend(query, keys, values, paired_keys, paired_values, ids, paired_ids):
    rows, width = query.shape
    seam = paired_keys.shape[0]
    block = pl.BlockSpec((rows, HD), lambda h: (0, h))
    seam_block = pl.BlockSpec((seam, HD), lambda h: (0, h))
    fixed = lambda shape: pl.BlockSpec(shape, lambda h: (0, 0))
    return pl.pallas_call(
        attend_kernel,
        grid=(width // HD,),
        out_shape=jax.ShapeDtypeStruct((rows, width), jnp.bfloat16),
        in_specs=[
            block, block, block, seam_block, seam_block,
            fixed((rows, 1)), fixed((1, rows)), fixed((1, seam)),
        ],
        out_specs=block,
        compiler_params=pltpu.CompilerParams(vmem_limit_bytes=32 * 2**20),
        cost_estimate=pl.CostEstimate(
            flops=4 * rows * (rows + seam) * width,
            transcendentals=rows * (rows + seam) * width // HD,
            bytes_accessed=8 * rows * width,
        ),
    )(
        query, keys, values, paired_keys, paired_values,
        ids[:, None], ids[None, :], paired_ids[None, :],
    )


def route_kernel(count, place_ref, mixed_ref, out_ref, outbox, send_sem, recv_sem, keep_sem):
    me = lax.axis_index("group")
    capacity = outbox.shape[1]
    rows = mixed_ref.shape[0]
    barrier = pltpu.get_barrier_semaphore()

    @pl.loop(1, count)
    def _(step):
        pl.semaphore_signal(
            barrier, inc=1, device_id={"group": lax.rem(me + step, count)},
            device_id_type=pl.DeviceIdType.MESH,
        )

    pl.semaphore_wait(barrier, count - 1)

    def pick(owner):
        slots = lax.broadcasted_iota(jnp.int32, (capacity, rows), 0) + owner * capacity
        select = (slots == place_ref[...]).astype(jnp.float32).astype(jnp.bfloat16)
        return jnp.dot(select, mixed_ref[...], preferred_element_type=jnp.float32).astype(
            jnp.bfloat16
        )

    def sending(step):
        ahead = 1 + lax.rem(step - 1 + count // 2 - 1, count - 1)
        peer = lax.rem(me + ahead, count)
        return peer, pltpu.make_async_remote_copy(
            src_ref=outbox.at[step],
            dst_ref=out_ref.at[me],
            send_sem=send_sem.at[step],
            recv_sem=recv_sem.at[me],
            device_id={"group": peer},
            device_id_type=pl.DeviceIdType.MESH,
        )

    @pl.loop(1, count)
    def _(step):
        peer, copy = sending(step)
        outbox[step] = pick(peer)
        copy.start()

    outbox[0] = pick(me)
    keep = pltpu.make_async_copy(outbox.at[0], out_ref.at[me], keep_sem)
    keep.start()

    @pl.loop(1, count)
    def _(step):
        source = lax.rem(me + step, count)
        pltpu.make_async_remote_copy(
            src_ref=outbox.at[step],
            dst_ref=out_ref.at[source],
            send_sem=send_sem.at[step],
            recv_sem=recv_sem.at[source],
            device_id={"group": source},
            device_id_type=pl.DeviceIdType.MESH,
        ).wait()

    keep.wait()


def route(place, mixed, count, capacity):
    rows, feat = mixed.shape
    return pl.pallas_call(
        lambda *refs: route_kernel(count, *refs),
        name="route",
        out_shape=jax.ShapeDtypeStruct((count, capacity, feat), jnp.bfloat16),
        in_specs=[pl.BlockSpec(memory_space=pltpu.VMEM)] * 2,
        out_specs=pl.BlockSpec(memory_space=pl.ANY),
        scratch_shapes=[
            pltpu.VMEM((count, capacity, feat), jnp.bfloat16),
            pltpu.SemaphoreType.DMA((count,)),
            pltpu.SemaphoreType.DMA((count,)),
            pltpu.SemaphoreType.DMA,
        ],
        compiler_params=pltpu.CompilerParams(
            collective_id=0, has_side_effects=True, vmem_limit_bytes=32 * 2**20
        ),
        cost_estimate=pl.CostEstimate(
            flops=2 * count * capacity * rows * feat,
            transcendentals=0,
            bytes_accessed=4 * count * capacity * feat,
        ),
    )(place[None, :], mixed)


def spread_shards(tokens, norm_gain, w_qkv, qk_gain, w_out, layer_scale, request, owner):
    rows, feat_local = tokens.shape
    tp_count = lax.axis_size("tp")
    group_count = lax.axis_size("group")
    local_width = w_qkv.shape[2]
    head_count = local_width // HD
    me_tp = lax.axis_index("tp")
    w_all = lax.all_gather(
        w_qkv.reshape(w_qkv.shape[0], 3 * local_width), "group", axis=0, tiled=True
    )
    whole = jnp.zeros((rows, feat_local * tp_count), jnp.bfloat16)
    gain_all = jnp.zeros((1, feat_local * tp_count), jnp.bfloat16)
    piece, gain = tokens, norm_gain.reshape(1, feat_local)
    for step in range(tp_count):
        at = ((me_tp + step) % tp_count) * feat_local
        whole = lax.dynamic_update_slice(whole, piece, (0, at))
        gain_all = lax.dynamic_update_slice(gain_all, gain, (0, at))
        if step < tp_count - 1:
            piece, gain = from_next(piece, "tp"), from_next(gain, "tp")
    whole, late_out = lax.optimization_barrier((whole, w_out))
    per = group_count // tp_count
    pairs = []
    for g in range(group_count):
        for b in range(tp_count):
            t, j = g // per, g % per
            to_g = b * per + j
            pairs.append((g * tp_count + b, to_g * tp_count + t))
    w_piece = lax.ppermute(late_out.T, ("group", "tp"), pairs)
    w_o = lax.all_gather(w_piece, "group", axis=0, tiled=True)
    w_o = w_o.reshape(tp_count, feat_local, local_width)
    xwide = whole.astype(jnp.float32)
    stat = jnp.mean(xwide * xwide, axis=-1, keepdims=True)
    normed = (xwide * lax.rsqrt(stat + 1e-06) * gain_all.astype(jnp.float32)).astype(jnp.bfloat16)
    qkv = jnp.dot(normed, w_all, preferred_element_type=jnp.float32)
    query = qkv[:, :local_width]
    key_rows = qkv[:, local_width : 2 * local_width]
    value = qkv[:, 2 * local_width :].astype(jnp.bfloat16)
    qsum, ksum = lax.psum(
        (jnp.sum(query * query, axis=-1), jnp.sum(key_rows * key_rows, axis=-1)), "tp"
    )
    total_width = local_width * tp_count
    qnorm = (query * lax.rsqrt(qsum / total_width + 1e-06)[:, None] * qk_gain[0]).astype(
        jnp.bfloat16
    )
    knorm = (key_rows * lax.rsqrt(ksum / total_width + 1e-06)[:, None] * qk_gain[1]).astype(
        jnp.bfloat16
    )
    parity = lax.axis_index("group") % 2
    seam = jnp.where(parity == 0, rows - SHARE, 0).astype(jnp.int32)
    key_window = lax.dynamic_slice_in_dim(knorm, seam, SHARE, 0)
    id_window = lax.dynamic_slice_in_dim(request, seam, SHARE, 0)
    paired_keys, paired_ids = swapped((key_window, id_window), "group", 0)
    value_window = lax.dynamic_slice_in_dim(value, seam, SHARE, 0)
    paired_values = swapped(value_window, "group", 0)
    attended = attend(qnorm, knorm, value, paired_keys, paired_values, request, paired_ids)

    branch = jnp.zeros((rows, feat_local), jnp.float32)
    for step in range(tp_count):
        onward = from_next(attended, "tp") if step < tp_count - 1 else None
        part = lax.dot_general(
            attended,
            lax.dynamic_index_in_dim(w_o, (me_tp + step) % tp_count, 0, keepdims=False),
            (((1,), (1,)), ((), ())),
            preferred_element_type=jnp.float32,
        )
        branch = branch + part.astype(jnp.bfloat16).astype(jnp.float32)
        attended = onward
    mixed = (tokens.astype(jnp.float32) + layer_scale * branch).astype(jnp.bfloat16)

    capacity = max(2, 2 * rows // group_count)
    target = owner[:, 0]
    onehot = target[:, None] == jnp.arange(group_count, dtype=jnp.int32)[None, :]
    order = jnp.arange(rows, dtype=jnp.int32)
    before = (order[:, None] > order[None, :]).astype(jnp.bfloat16)
    ranks = jnp.dot(before, onehot.astype(jnp.bfloat16), preferred_element_type=jnp.float32)
    slot = jnp.sum(jnp.where(onehot, ranks, 0.0), axis=-1).astype(jnp.int32)
    place = target * capacity + slot
    inbox = route(place, mixed, group_count, capacity)
    return inbox[None]


def plane_shards(tokens, norm_gain, w_qkv, qk_gain, w_out, layer_scale, request, owner):
    count = lax.axis_size("group")
    capacity = max(2, 2 * tokens.shape[0] // count)
    return plane_call(
        tokens.T, jnp.stack([norm_gain.astype(F32), layer_scale]), w_qkv.transpose(1, 0, 2), qk_gain, w_out.T,
        request[None, :], owner.T, count, capacity,
    )[None]


def shards(*arrays):
    w_qkv = arrays[2]
    count, tp = lax.axis_size("group"), lax.axis_size("tp")
    whole_tiles = 2 * w_qkv.shape[0] % 16 == 0 and w_qkv.shape[2] % (2 * HD) == 0
    if tp == 2 and count == 16 and whole_tiles:
        return plane_shards(*arrays)
    return spread_shards(*arrays)


def solution(mesh):
    in_specs = (
        P("group", "tp"),
        P("tp"),
        P("group", None, "tp"),
        P(None, "tp"),
        P("tp", "group"),
        P("tp"),
        P("group"),
        P("group", None),
    )
    out_specs = P("group", None, None, "tp")
    return jax.shard_map(shards, mesh=mesh, in_specs=in_specs, out_specs=out_specs, check_vma=False)
```

```python
import functools
import math

import jax
import jax.numpy as jnp
from jax import lax
from jax.experimental import pallas as pl
from jax.experimental.pallas import tpu as pltpu
from jax.sharding import PartitionSpec as P

HD = 128
SHARE = 128


MESH = pl.DeviceIdType.MESH
BF16 = jnp.bfloat16
F32 = jnp.float32


def to_row(column):
    spread = jnp.broadcast_to(column, (column.shape[0], 128))
    return jnp.transpose(spread)[:8]


def to_column(row):
    spread = jnp.broadcast_to(row, (128, row.shape[1]))
    return jnp.transpose(spread)[:, :1]


def plane_kernel(
    levels, turned_ref, vectors_ref, w_ref, qk_gain_ref, wo_ref, request_ref, owner_ref, out_ref,
    tokens_ref, ids_ref, w_send, w_got, w_all, n_send, n_all, ids_all, sum_mine, sum_got, qk_mine, qk_got,
    qk_wide, qn, kn, vb, probs, att, wo_send, wo_got, wo_line, wo_all, att_all,
    ws_sem, wr_sem, is_sem, ir_sem, ss_sem, sr_sem, ns_sem, nr_sem, nf_sem, nfr_sem,
    right_sem, left_sem, chain_sem, core_s_sem, core_r_sem, qs_sem, qr_sem,
    wos_sem, wor_sem, uright_sem, uleft_sem, uchain_sem, uhere_sem, ux_sem, uxr_sem, uy_sem, uyr_sem, uc_sem, ucr_sem,
    as_sem, ar_sem, send_sem, recv_sem, keep_sem,
):
    group, t = lax.axis_index("group"), lax.axis_index("tp")
    z, y, c = group // 4, lax.rem(group // 2, 2), lax.rem(group, 2)
    rows, feat = tokens_ref.shape
    count, capacity = out_ref.shape[:2]
    slab = w_all.shape[1] // (2 * levels)
    depth = w_ref.shape[1]
    cols = w_all.shape[2]
    heads = cols // HD
    sub = rows // 2
    part = sub * 5 // 16
    half_cols = cols // 2
    edge_r, edge_l = z < levels - 1, z > 0

    def at(zz, yy, cc):
        return (zz * 2 + yy) * 2 + cc

    def remote(src, dst, send, recv, place, tt):
        return pltpu.make_async_remote_copy(
            src_ref=src, dst_ref=dst, send_sem=send, recv_sem=recv,
            device_id={"group": place, "tp": tt}, device_id_type=MESH,
        )

    barrier = pltpu.get_barrier_semaphore()

    @pl.loop(1, count)
    def _(step):
        pl.semaphore_signal(
            barrier, inc=1, device_id={"group": lax.rem(group + step, count), "tp": t}, device_id_type=MESH
        )

    for k in range(4):
        pl.semaphore_signal(
            barrier, inc=1, device_id={"group": z * 4 + k, "tp": lax.rem(t + 1, 2)}, device_id_type=MESH
        )

    for yy in range(2):
        w_send[yy, :, :depth, :] = w_ref[:, :, yy * cols : (yy + 1) * cols]

    half_out = wo_ref.shape[1] // 2
    for cc in range(2):
        wo_send[cc, :depth, :] = wo_ref[:, cc * half_out : (cc + 1) * half_out]
    ids_ref[...] = jnp.broadcast_to(request_ref[...].astype(F32), (8, rows))
    pl.semaphore_wait(barrier, count + 3)

    def pieces(yy):
        place = at(z, yy, y)
        copies = [
            remote(w_send.at[yy, j], w_got.at[c, j], ws_sem.at[yy, j], wr_sem.at[c, j], place, t) for j in range(3)
        ]
        return copies[:2] + [remote(ids_ref, ids_all.at[c], is_sem.at[yy], ir_sem.at[c], place, t)] + copies[2:]

    def kept(yy):
        copies = [pltpu.make_async_copy(w_send.at[yy, j], w_got.at[c, j], wr_sem.at[c, j]) for j in range(3)]
        return copies[:2] + [pltpu.make_async_copy(ids_ref, ids_all.at[c], ir_sem.at[c])] + copies[2:]

    def is_me(yy):
        return jnp.logical_and(y == yy, c == y)

    def start_pieces(which):
        for yy in range(2):
            @pl.when(is_me(yy))
            def _():
                for copy in kept(yy)[which]:
                    copy.start()

            @pl.when(jnp.logical_not(is_me(yy)))
            def _():
                for copy in pieces(yy)[which]:
                    copy.start()

    start_pieces(slice(0, 3))
    wo_swap = remote(wo_send.at[1 - c], wo_got, wos_sem, wor_sem, at(z, y, 1 - c), t)
    wo_swap.start()

    wide = turned_ref[...].astype(F32)
    sum_mine[...] = jnp.broadcast_to(jnp.sum(wide * wide, axis=0, keepdims=True), (8, rows))
    swap = remote(sum_mine, sum_got, ss_sem, sr_sem, group, lax.rem(t + 1, 2))
    swap.start()

    def rows_of(zz, cc):
        return pl.ds(pl.multiple_of((zz * 2 + cc) * slab, 16), slab)

    def piece(j, zz, cc):
        if j < 2:
            return w_all.at[j, rows_of(zz, cc), :]
        return w_all.at[2, rows_of(zz, cc), (j - 2) * half_cols : (j - 1) * half_cols]

    def go_right(j, zz):
        return remote(piece(j, zz, c), piece(j, zz, c), right_sem.at[j, zz], chain_sem.at[j, zz], group + 4, t)

    def go_left(j, zz):
        return remote(piece(j, zz, c), piece(j, zz, c), left_sem.at[j, zz], chain_sem.at[j, zz], group - 4, t)

    def go_core(j, zz):
        return remote(
            piece(j, zz, c), piece(j, zz, c), core_s_sem.at[j, zz], core_r_sem.at[j, zz],
            at(z, y, 1 - c), t,
        )

    def build(j):
        for cc in range(2):
            pltpu.make_async_copy(w_send.at[0, j], w_got.at[cc, j], wr_sem.at[cc, j]).wait()
        both = jnp.concatenate(
            [w_got[0, j].astype(F32)[:depth], w_got[1, j].astype(F32)[:depth]], axis=0
        )
        w_all[j, rows_of(z, c), :] = both.astype(BF16)

    def send_own(j):
        @pl.when(edge_r)
        def _():
            go_right(j, z).start()

        @pl.when(edge_l)
        def _():
            go_left(j, z).start()

        go_core(j, z).start()

    def arrive(j, d):
        @pl.when(z - d >= 0)
        def _():
            go_right(j, z - d).wait_recv()

            @pl.when(edge_r)
            def _():
                go_right(j, z - d).start()

            go_core(j, z - d).start()

        @pl.when(z + d < levels)
        def _():
            go_left(j, z + d).wait_recv()

            @pl.when(edge_l)
            def _():
                go_left(j, z + d).start()

            go_core(j, z + d).start()

    other_t = lax.rem(t + 1, 2)
    half_levels = levels // 2
    lanes_out = wo_all.shape[2] // 2

    def u_at(tt, i, yy, cc):
        return wo_all.at[
            tt, pl.ds(pl.multiple_of((i * 2 + yy) * slab, 16), slab),
            pl.ds(pl.multiple_of(cc * lanes_out, 128), lanes_out),
        ]

    def u_right(zz):
        return remote(wo_line.at[zz], wo_line.at[zz], uright_sem.at[zz], uchain_sem.at[zz], group + 4, t)

    def u_left(zz):
        return remote(wo_line.at[zz], wo_line.at[zz], uleft_sem.at[zz], uchain_sem.at[zz], group - 4, t)

    def u_here(i):
        return pltpu.make_async_copy(wo_line.at[t * half_levels + i], u_at(t, i, y, c), uhere_sem.at[i])

    def u_across(i):
        zz = other_t * half_levels + i
        return remote(wo_line.at[zz], u_at(t, i, y, c), ux_sem.at[i], uxr_sem.at[i], group, other_t)

    def u_over(tt, i, line):
        src = wo_line.at[t * half_levels + i] if line else u_at(tt, i, y, c)
        return remote(src, u_at(tt, i, y, c), uy_sem.at[tt, i], uyr_sem.at[tt, i], at(z, 1 - y, c), t)

    def u_core(tt, i, yy, line):
        src = wo_line.at[t * half_levels + i] if line else u_at(tt, i, yy, c)
        return remote(
            src, u_at(tt, i, yy, c), uc_sem.at[tt, i, yy], ucr_sem.at[tt, i, yy], at(z, y, 1 - c), t
        )

    def u_hops(zz):
        i = lax.rem(zz, half_levels)
        wanted = zz // half_levels == t

        @pl.when(wanted)
        def _():
            u_here(i).start()
            u_over(t, i, True).start()
            u_core(t, i, y, True).start()

        @pl.when(jnp.logical_not(wanted))
        def _():
            u_across(i).start()

    def u_own():
        wo_swap.wait()
        mine, theirs = wo_send[c].astype(F32)[:depth], wo_got[...].astype(F32)[:depth]
        low, high = jnp.where(c == 0, mine, theirs), jnp.where(c == 0, theirs, mine)
        wo_line[z] = jnp.concatenate([low, high], axis=0).astype(BF16)

        @pl.when(edge_r)
        def _():
            u_right(z).start()

        @pl.when(edge_l)
        def _():
            u_left(z).start()

    def u_arrive(d):
        @pl.when(z - d >= 0)
        def _():
            u_right(z - d).wait_recv()

            @pl.when(edge_r)
            def _():
                u_right(z - d).start()

        @pl.when(z + d < levels)
        def _():
            u_left(z + d).wait_recv()

            @pl.when(edge_l)
            def _():
                u_left(z + d).start()

    def u_hops_of(d):
        @pl.when(z - d >= 0)
        def _():
            u_hops(z - d)

        @pl.when(z + d < levels)
        def _():
            u_hops(z + d)

    def ux_take(d):
        for zz in ((z - d, z + d) if d else (z,)):
            here = jnp.logical_and(jnp.logical_and(zz >= 0, zz < levels), (zz + levels) // half_levels == t + 2)

            @pl.when(here)
            def _():
                i = lax.rem(zz, half_levels)
                ref = u_at(other_t, i, y, c)
                pltpu.make_async_copy(ref, ref, uxr_sem.at[i]).wait()
                u_over(other_t, i, False).start()
                u_core(other_t, i, y, False).start()

    inner = jnp.logical_and(edge_l, edge_r)
    outer = jnp.logical_not(inner)
    def own_first():
        for j in range(2):
            build(j)
            send_own(j)

    pl.when(c == y)(own_first)

    swap.wait()
    whole = sum_mine[...] + sum_got[...]
    factor = to_column(lax.rsqrt(whole[:1] / (2 * feat) + 1e-06))

    def n_rows(cc, start, size):
        return pl.ds(pl.multiple_of(cc * rows + start, 16), size)

    def n_copies(s):
        src = n_send.at[s * sub : (s + 1) * sub, :]
        dst = n_all.at[t, n_rows(c, s * sub, sub), :]
        recv = nr_sem.at[t, c, s]
        return (
            remote(src, dst, ns_sem.at[0, s], recv, at(z, y, y), lax.rem(t + 1, 2)),
            remote(src, dst, ns_sem.at[1, s], recv, at(z, 1 - y, y), t),
            remote(src, dst, ns_sem.at[2, s], recv, at(z, y, y), t),
            pltpu.make_async_copy(src, dst, recv),
        )

    start_pieces(slice(3, 4))
    for s in range(2):
        span = slice(s * sub, (s + 1) * sub)
        tokens_ref[span, :] = jnp.transpose(turned_ref[:, span].astype(F32)).astype(BF16)
        n_send[span, :] = (
            tokens_ref[span, :].astype(F32) * factor[span] * vectors_ref[:1, :]
        ).astype(BF16)
        n_x, n_y, n_core, n_here = n_copies(s)
        n_x.start()
        n_y.start()

        @pl.when(c == y)
        def _():
            n_here.start()

        @pl.when(c != y)
        def _():
            n_core.start()

    def n_wait(tt, cc, s):
        ref = n_all.at[tt, n_rows(cc, s * sub, sub), :]
        pltpu.make_async_copy(ref, ref, nr_sem.at[tt, cc, s]).wait()


    def forward_y(cc, s):
        ref = n_all.at[other_t, n_rows(cc, s * sub, part), :]
        return remote(ref, ref, nf_sem.at[cc, s], nfr_sem.at[0, cc, s], at(z, 1 - y, c), t)

    def forward_x(cc, s):
        ref = n_all.at[t, n_rows(cc, s * sub + part, sub - part), :]
        return remote(ref, ref, nf_sem.at[cc, s], nfr_sem.at[1, cc, s], group, other_t)

    def n_forward(s):
        for cc in range(2):
            @pl.when(c == y)
            def _():
                n_wait(other_t, cc, s)
                forward_y(cc, s).start()

            @pl.when(c != y)
            def _():
                n_wait(t, cc, s)
                forward_x(cc, s).start()

    pl.when(c != y)(own_first)
    arrive(0, 1)
    arrive(1, 1)
    u_own()
    build(2)

    @pl.when(outer)
    def _():
        send_own(2)
        send_own(3)

    n_forward(0)
    arrive(0, 2)
    arrive(1, 2)

    @pl.when(inner)
    def _():
        u_arrive(1)

    n_forward(1)

    @pl.when(inner)
    def _():
        send_own(2)
        send_own(3)

    def n_rest(s):
        for cc in range(2):
            @pl.when(c == y)
            def _():
                n_wait(t, cc, s)

            @pl.when(c != y)
            def _():
                for way, (start, size) in enumerate(((0, part), (part, sub - part))):
                    ref = n_all.at[other_t, n_rows(cc, s * sub + start, size), :]
                    pltpu.make_async_copy(ref, ref, nfr_sem.at[way, cc, s]).wait()

    def core_wait(j):
        for zz in range(levels):
            remote(
                piece(j, zz, 1 - c), piece(j, zz, 1 - c), core_s_sem.at[j, zz], core_r_sem.at[j, zz],
                at(z, y, 1 - c), t,
            ).wait_recv()

    def project(j, start, size, lanes):
        return jnp.dot(
            n_all[0, pl.ds(start, size), :], w_all[j, :feat, lanes], preferred_element_type=F32
        ) + jnp.dot(n_all[1, pl.ds(start, size), :], w_all[j, feat:, lanes], preferred_element_type=F32)

    arrive(0, 3)
    arrive(1, 3)
    core_wait(0)
    core_wait(1)
    for s in range(2):
        n_rest(s)
        if s:
            u_hops(z)

            @pl.when(inner)
            def _():
                u_hops_of(1)
                arrive(2, 1)
                arrive(3, 1)

        @pl.loop(0, 2)
        def _(cc):
            start = pl.multiple_of(cc * rows + s * sub, sub)
            for j in range(2):
                out = project(j, start, sub, slice(None))
                qk_wide[j, pl.ds(start, sub), :] = out
                qk_mine[j, :, pl.ds(start, sub)] = to_row(jnp.sum(out * out, axis=-1, keepdims=True))

    def stat_swap(k):
        return remote(
            qk_mine, qk_got.at[k - 1], qs_sem.at[k - 1], qr_sem.at[k - 1],
            at(z, lax.rem(y + k % 2, 2), c), lax.rem(t + k // 2, 2),
        )

    for k in range(1, 4):
        stat_swap(k).start()
    ux_take(0)

    @pl.when(inner)
    def _():
        arrive(2, 2)

    @pl.when(outer)
    def _():
        u_arrive(1)
        u_hops_of(1)

    for k in range(1, 4):
        stat_swap(k).wait()
    stats = qk_mine[...] + qk_got[0] + qk_got[1] + qk_got[2]
    factors = lax.rsqrt(stats / (4 * cols) + 1e-06)
    for j, ref in ((0, qn), (1, kn)):
        column = to_column(factors[j, :1])
        near = qk_gain_ref[j : j + 1, :cols]
        far = qk_gain_ref[j : j + 1, cols:]
        gains = jnp.where(y == 0, near, far)
        ref[...] = (qk_wide[j] * column * gains).astype(BF16)

    for cc in range(2):
        pltpu.make_async_copy(ids_ref, ids_all.at[cc], ir_sem.at[cc]).wait()
    seam = rows + SHARE
    scale = 1.0 / math.sqrt(HD)
    ids = jnp.concatenate([ids_all[0, :1], ids_all[1, :1]], axis=1)
    for half in range(2):
        first = half * (rows - SHARE)
        same = to_column(ids[:, half * rows : (half + 1) * rows]) == ids[:, first : first + seam]

        @pl.loop(0, heads)
        def _(h):
            lanes = pl.ds(pl.multiple_of(h * HD, HD), HD)
            scores = lax.dot_general(
                qn[half * rows : (half + 1) * rows, lanes], kn[first : first + seam, lanes],
                (((1,), (1,)), ((), ())), preferred_element_type=F32,
            ) * scale
            scores = jnp.where(same, scores, -jnp.inf)
            expo = jnp.exp(scores - jnp.max(scores, axis=-1, keepdims=True))
            share = 1.0 / jnp.sum(expo, axis=-1, keepdims=True)
            probs[half, h] = (expo * share).astype(BF16)

        if half == 0:
            @pl.when(inner)
            def _():
                arrive(3, 2)
                u_arrive(2)

            @pl.when(outer)
            def _():
                u_arrive(2)
                u_hops_of(2)

            ux_take(1)
        else:
            @pl.when(outer)
            def _():
                ux_take(2)

    def att_copy(dt, half, j):
        src = att.at[half * rows : (half + 1) * rows, j * half_cols : (j + 1) * half_cols]
        dst = att_all.at[t, :, pl.ds(pl.multiple_of(y * cols + j * half_cols, 128), half_cols)]
        mine = jnp.logical_and(y == c, c == half)
        recv = ar_sem.at[t, y, j]
        away = remote(src, dst, as_sem.at[dt, half, j], recv, at(z, c, half), lax.rem(t + dt, 2))
        return mine, away, pltpu.make_async_copy(src, dst, recv)

    def uy_take(i):
        for tt in range(2):
            ref = u_at(tt, i, 1 - y, c)
            pltpu.make_async_copy(ref, ref, uyr_sem.at[tt, i]).wait()
            u_core(tt, i, 1 - y, False).start()

    def u_ready(i):
        u_here(i).wait()
        for tt in range(2):
            for yy in range(2):
                ref = u_at(tt, i, yy, 1 - c)
                pltpu.make_async_copy(ref, ref, ucr_sem.at[tt, i, yy]).wait()

    upper = z // half_levels
    for j in range(2):
        @pl.when(outer)
        def _():
            for d in range(1, levels):
                arrive(2 + j, d)

        core_wait(2 + j)
        span = slice(j * half_cols, (j + 1) * half_cols)

        @pl.loop(0, 2)
        def _(i):
            start = pl.multiple_of(i * rows, rows)
            vb[pl.ds(start, rows), span] = project(2, start, rows, span).astype(BF16)

        for half in range(2):
            first = half * (rows - SHARE)
            for h in range(j * heads // 2, (j + 1) * heads // 2):
                lanes = slice(h * HD, (h + 1) * HD)
                att[half * rows : (half + 1) * rows, lanes] = jnp.dot(
                    probs[half, h], vb[first : first + seam, lanes], preferred_element_type=F32
                ).astype(BF16)

            att_copy(1, half, j)[1].start()
            mine, away, here = att_copy(0, half, j)

            @pl.when(mine)
            def _():
                here.start()

            @pl.when(jnp.logical_not(mine))
            def _():
                away.start()

        if j == 0:
            uy_take(upper)
        else:
            @pl.when(inner)
            def _():
                u_hops_of(2)

            @pl.when(outer)
            def _():
                u_arrive(3)
                u_hops_of(3)

    target = owner_ref[...]
    named = lax.broadcasted_iota(jnp.int32, (count, rows), 0) == target
    earlier = lax.broadcasted_iota(jnp.int32, (rows, rows), 0) < lax.broadcasted_iota(jnp.int32, (rows, rows), 1)
    ranks = jnp.dot(
        named.astype(F32).astype(BF16), earlier.astype(F32).astype(BF16), preferred_element_type=F32
    )
    slot = jnp.sum(jnp.where(named, ranks, 0.0), axis=0, keepdims=True).astype(jnp.int32)
    place = target * capacity + slot

    for tt in range(2):
        for yy in range(2):
            for j in range(2):
                ref = att_all.at[tt, :, yy * cols + j * half_cols : yy * cols + (j + 1) * half_cols]
                pltpu.make_async_copy(ref, ref, ar_sem.at[tt, yy, j]).wait()

    u_ready(upper)

    for s in range(2):
        n_x, n_y, n_core, n_here = n_copies(s)
        n_x.wait_send()
        n_y.wait_send()

        @pl.when(c != y)
        def _():
            n_core.wait_send()

        for cc in range(2):
            @pl.when(c == y)
            def _():
                forward_y(cc, s).wait_send()

            @pl.when(c != y)
            def _():
                forward_x(cc, s).wait_send()

    mixed = n_send

    def slots_of(owner_group, lanes):
        return n_all.at[0, pl.ds(pl.multiple_of(owner_group * capacity, 16), capacity), lanes]

    def sending(f, lanes, owner_group):
        return pltpu.make_async_remote_copy(
            src_ref=slots_of(owner_group, lanes), dst_ref=out_ref.at[group, :, lanes],
            send_sem=send_sem.at[f, owner_group], recv_sem=recv_sem.at[group],
            device_id={"group": owner_group, "tp": t}, device_id_type=MESH,
        )

    def keeping(f, lanes):
        return pltpu.make_async_copy(slots_of(group, lanes), out_ref.at[group, :, lanes], keep_sem.at[f])

    middle = feat // 2
    below, above = middle // 128 * 128, -(-middle // 128) * 128
    spans = (
        (slice(0, below), slice(below, feat)),
        (slice(above, feat), slice(0, above)),
    )
    planes = (3 - z, lax.rem(z + 2, 4), z + 1 - 2 * lax.rem(z, 2), z)

    def finish(f, lanes):
        total = jnp.zeros((rows, lanes.stop - lanes.start), F32)
        for tt in range(2):
            term = lax.dot_general(
                att_all[tt], wo_all[tt, lanes, :], (((1,), (1,)), ((), ())), preferred_element_type=F32
            )
            total += term.astype(BF16).astype(F32)
        mixed[:, lanes] = (tokens_ref[:, lanes].astype(F32) + vectors_ref[1:, lanes] * total).astype(BF16)
        for plane in planes:
            slots = lax.broadcasted_iota(jnp.int32, (4 * capacity, rows), 0) + plane * 4 * capacity
            chosen = (slots == place).astype(F32).astype(BF16)
            picked = jnp.dot(chosen, mixed[:, lanes], preferred_element_type=F32).astype(BF16)
            n_all[0, pl.ds(pl.multiple_of(plane * 4 * capacity, 16), 4 * capacity), lanes] = picked
            for k in range(4):
                peer = plane * 4 + lax.rem(k + group, 4)

                @pl.when(peer == group)
                def _():
                    keeping(f, lanes).start()

                @pl.when(peer != group)
                def _():
                    sending(f, lanes, peer).start()

    def left(f, lanes):
        @pl.loop(1, count)
        def _(step):
            sending(f, lanes, lax.rem(group + step, count)).wait_send()

        keeping(f, lanes).wait()

    for f in range(2):
        if f:
            @pl.when(inner)
            def _():
                ux_take(2)

            ux_take(3)
            uy_take(1 - upper)
            u_ready(1 - upper)

        for which in range(2):
            @pl.when(upper == which)
            def _():
                finish(f, spans[which][f])

    for f in range(2):
        for which in range(2):
            @pl.when(upper == which)
            def _():
                left(f, spans[which][f])

    @pl.loop(1, count)
    def _(step):
        ref = out_ref.at[lax.rem(group + step, count)]
        pltpu.make_async_copy(ref, ref, recv_sem.at[lax.rem(group + step, count)]).wait()

    for yy in range(2):
        @pl.when(jnp.logical_not(is_me(yy)))
        def _():
            for copy in pieces(yy):
                copy.wait_send()

    for half in range(2):
        for j in range(2):
            att_copy(1, half, j)[1].wait_send()
            mine, away, here = att_copy(0, half, j)

            @pl.when(jnp.logical_not(mine))
            def _():
                away.wait_send()

    for zz in range(levels):
        @pl.when(jnp.logical_and(zz <= z, edge_r))
        def _():
            u_right(zz).wait_send()

        @pl.when(jnp.logical_and(zz >= z, edge_l))
        def _():
            u_left(zz).wait_send()

    for i in range(half_levels):
        u_across(i).wait_send()
        for tt in range(2):
            u_over(tt, i, False).wait_send()
            for yy in range(2):
                u_core(tt, i, yy, False).wait_send()

    for j in range(4):
        for zz in range(levels):
            @pl.when(jnp.logical_and(zz <= z, edge_r))
            def _():
                go_right(j, zz).wait_send()

            @pl.when(jnp.logical_and(zz >= z, edge_l))
            def _():
                go_left(j, zz).wait_send()

            go_core(j, zz).wait_send()


def plane_call(turned, vectors, w, qk_gain, wo, request, owner, count, capacity):
    feat, rows = turned.shape
    depth, width = w.shape[1], w.shape[2]
    levels, cols = count // 4, width // 2
    heads = cols // HD
    padded = -(-depth // 16) * 16
    seam = rows + SHARE
    dma = pltpu.SemaphoreType.DMA
    vmem = pl.BlockSpec(memory_space=pltpu.VMEM)
    return pl.pallas_call(
        functools.partial(plane_kernel, levels),
        name="plane",
        out_shape=jax.ShapeDtypeStruct((count, capacity, feat), BF16),
        in_specs=[vmem] * 7,
        out_specs=pl.BlockSpec(memory_space=pl.ANY),
        scratch_shapes=[
            pltpu.VMEM((rows, feat), BF16),
            pltpu.VMEM((8, rows), F32),
            pltpu.VMEM((2, 3, padded, cols), BF16),
            pltpu.VMEM((2, 3, padded, cols), BF16),
            pltpu.VMEM((3, 2 * feat, cols), BF16),
            pltpu.VMEM((rows, feat), BF16),
            pltpu.VMEM((2, 2 * rows, feat), BF16),
            pltpu.VMEM((2, 8, rows), F32),
            pltpu.VMEM((8, rows), F32),
            pltpu.VMEM((8, rows), F32),
            pltpu.VMEM((2, 8, 2 * rows), F32),
            pltpu.VMEM((3, 2, 8, 2 * rows), F32),
            pltpu.VMEM((2, 2 * rows, cols), F32),
            pltpu.VMEM((2 * rows, cols), BF16),
            pltpu.VMEM((2 * rows, cols), BF16),
            pltpu.VMEM((2 * rows, cols), BF16),
            pltpu.VMEM((2, heads, rows, seam), BF16),
            pltpu.VMEM((2 * rows, cols), BF16),
            pltpu.VMEM((2, padded, width // 2), BF16),
            pltpu.VMEM((padded, width // 2), BF16),
            pltpu.VMEM((levels, 2 * depth, width // 2), BF16),
            pltpu.VMEM((2, feat, width), BF16),
            pltpu.VMEM((2, rows, width), BF16),
            dma((2, 3)), dma((2, 3)), dma((2,)), dma((2,)), dma, dma,
            dma((3, 2)), dma((2, 2, 2)), dma((2, 2)), dma((2, 2, 2)),
            dma((4, levels)), dma((4, levels)), dma((4, levels)), dma((4, levels)), dma((4, levels)),
            dma((3,)), dma((3,)),
            dma, dma, dma((levels,)), dma((levels,)), dma((levels,)), dma((2,)), dma((2,)), dma((2,)),
            dma((2, 2)), dma((2, 2)), dma((2, 2, 2)), dma((2, 2, 2)),
            dma((2, 2, 2)), dma((2, 2, 2)), dma((2, count)), dma((count,)), dma((2,)),
        ],
        compiler_params=pltpu.CompilerParams(
            collective_id=1, has_side_effects=True, vmem_limit_bytes=60 * 2**20
        ),
        cost_estimate=pl.CostEstimate(
            flops=20 * rows * feat * width, transcendentals=2 * heads * rows * seam,
            bytes_accessed=8 * 2**20,
        ),
    )(turned, vectors, w, qk_gain, wo, request, owner)


def swapped(value, axis, apart):
    mask = 2**apart
    pairs = [(source, source ^ mask) for source in range(lax.axis_size(axis))]
    return lax.ppermute(value, axis, pairs)


def from_next(value, axis):
    count = lax.axis_size(axis)
    return lax.ppermute(value, axis, [((i + 1) % count, i) for i in range(count)])


def attend_kernel(q_ref, k_ref, v_ref, kp_ref, vp_ref, row_ref, own_ref, pair_ref, out_ref):
    query = q_ref[...]
    over = (((1,), (1,)), ((), ()))
    scale = 1.0 / math.sqrt(HD)
    near = lax.dot_general(query, k_ref[...], over, preferred_element_type=jnp.float32) * scale
    far = lax.dot_general(query, kp_ref[...], over, preferred_element_type=jnp.float32) * scale
    near = jnp.where(row_ref[...] == own_ref[...], near, -jnp.inf)
    far = jnp.where(row_ref[...] == pair_ref[...], far, -jnp.inf)
    top = jnp.maximum(
        jnp.max(near, axis=-1, keepdims=True), jnp.max(far, axis=-1, keepdims=True)
    )
    near, far = jnp.exp(near - top), jnp.exp(far - top)
    share = 1.0 / (jnp.sum(near, axis=-1, keepdims=True) + jnp.sum(far, axis=-1, keepdims=True))
    near, far = (near * share).astype(jnp.bfloat16), (far * share).astype(jnp.bfloat16)
    total = jnp.dot(near, v_ref[...], preferred_element_type=jnp.float32)
    total += jnp.dot(far, vp_ref[...], preferred_element_type=jnp.float32)
    out_ref[...] = total.astype(jnp.bfloat16)


def attend(query, keys, values, paired_keys, paired_values, ids, paired_ids):
    rows, width = query.shape
    seam = paired_keys.shape[0]
    block = pl.BlockSpec((rows, HD), lambda h: (0, h))
    seam_block = pl.BlockSpec((seam, HD), lambda h: (0, h))
    fixed = lambda shape: pl.BlockSpec(shape, lambda h: (0, 0))
    return pl.pallas_call(
        attend_kernel,
        grid=(width // HD,),
        out_shape=jax.ShapeDtypeStruct((rows, width), jnp.bfloat16),
        in_specs=[
            block, block, block, seam_block, seam_block,
            fixed((rows, 1)), fixed((1, rows)), fixed((1, seam)),
        ],
        out_specs=block,
        compiler_params=pltpu.CompilerParams(vmem_limit_bytes=32 * 2**20),
        cost_estimate=pl.CostEstimate(
            flops=4 * rows * (rows + seam) * width,
            transcendentals=rows * (rows + seam) * width // HD,
            bytes_accessed=8 * rows * width,
        ),
    )(
        query, keys, values, paired_keys, paired_values,
        ids[:, None], ids[None, :], paired_ids[None, :],
    )


def route_kernel(count, place_ref, mixed_ref, out_ref, outbox, send_sem, recv_sem, keep_sem):
    me = lax.axis_index("group")
    capacity = outbox.shape[1]
    rows = mixed_ref.shape[0]
    barrier = pltpu.get_barrier_semaphore()

    @pl.loop(1, count)
    def _(step):
        pl.semaphore_signal(
            barrier, inc=1, device_id={"group": lax.rem(me + step, count)},
            device_id_type=pl.DeviceIdType.MESH,
        )

    pl.semaphore_wait(barrier, count - 1)

    def pick(owner):
        slots = lax.broadcasted_iota(jnp.int32, (capacity, rows), 0) + owner * capacity
        select = (slots == place_ref[...]).astype(jnp.float32).astype(jnp.bfloat16)
        return jnp.dot(select, mixed_ref[...], preferred_element_type=jnp.float32).astype(
            jnp.bfloat16
        )

    def sending(step):
        ahead = 1 + lax.rem(step - 1 + count // 2 - 1, count - 1)
        peer = lax.rem(me + ahead, count)
        return peer, pltpu.make_async_remote_copy(
            src_ref=outbox.at[step],
            dst_ref=out_ref.at[me],
            send_sem=send_sem.at[step],
            recv_sem=recv_sem.at[me],
            device_id={"group": peer},
            device_id_type=pl.DeviceIdType.MESH,
        )

    @pl.loop(1, count)
    def _(step):
        peer, copy = sending(step)
        outbox[step] = pick(peer)
        copy.start()

    outbox[0] = pick(me)
    keep = pltpu.make_async_copy(outbox.at[0], out_ref.at[me], keep_sem)
    keep.start()

    @pl.loop(1, count)
    def _(step):
        source = lax.rem(me + step, count)
        pltpu.make_async_remote_copy(
            src_ref=outbox.at[step],
            dst_ref=out_ref.at[source],
            send_sem=send_sem.at[step],
            recv_sem=recv_sem.at[source],
            device_id={"group": source},
            device_id_type=pl.DeviceIdType.MESH,
        ).wait()

    keep.wait()


def route(place, mixed, count, capacity):
    rows, feat = mixed.shape
    return pl.pallas_call(
        lambda *refs: route_kernel(count, *refs),
        name="route",
        out_shape=jax.ShapeDtypeStruct((count, capacity, feat), jnp.bfloat16),
        in_specs=[pl.BlockSpec(memory_space=pltpu.VMEM)] * 2,
        out_specs=pl.BlockSpec(memory_space=pl.ANY),
        scratch_shapes=[
            pltpu.VMEM((count, capacity, feat), jnp.bfloat16),
            pltpu.SemaphoreType.DMA((count,)),
            pltpu.SemaphoreType.DMA((count,)),
            pltpu.SemaphoreType.DMA,
        ],
        compiler_params=pltpu.CompilerParams(
            collective_id=0, has_side_effects=True, vmem_limit_bytes=32 * 2**20
        ),
        cost_estimate=pl.CostEstimate(
            flops=2 * count * capacity * rows * feat,
            transcendentals=0,
            bytes_accessed=4 * count * capacity * feat,
        ),
    )(place[None, :], mixed)


def spread_shards(tokens, norm_gain, w_qkv, qk_gain, w_out, layer_scale, request, owner):
    rows, feat_local = tokens.shape
    tp_count = lax.axis_size("tp")
    group_count = lax.axis_size("group")
    local_width = w_qkv.shape[2]
    head_count = local_width // HD
    me_tp = lax.axis_index("tp")
    w_all = lax.all_gather(
        w_qkv.reshape(w_qkv.shape[0], 3 * local_width), "group", axis=0, tiled=True
    )
    whole = jnp.zeros((rows, feat_local * tp_count), jnp.bfloat16)
    gain_all = jnp.zeros((1, feat_local * tp_count), jnp.bfloat16)
    piece, gain = tokens, norm_gain.reshape(1, feat_local)
    for step in range(tp_count):
        at = ((me_tp + step) % tp_count) * feat_local
        whole = lax.dynamic_update_slice(whole, piece, (0, at))
        gain_all = lax.dynamic_update_slice(gain_all, gain, (0, at))
        if step < tp_count - 1:
            piece, gain = from_next(piece, "tp"), from_next(gain, "tp")
    whole, late_out = lax.optimization_barrier((whole, w_out))
    per = group_count // tp_count
    pairs = []
    for g in range(group_count):
        for b in range(tp_count):
            t, j = g // per, g % per
            to_g = b * per + j
            pairs.append((g * tp_count + b, to_g * tp_count + t))
    w_piece = lax.ppermute(late_out.T, ("group", "tp"), pairs)
    w_o = lax.all_gather(w_piece, "group", axis=0, tiled=True)
    w_o = w_o.reshape(tp_count, feat_local, local_width)
    xwide = whole.astype(jnp.float32)
    stat = jnp.mean(xwide * xwide, axis=-1, keepdims=True)
    normed = (xwide * lax.rsqrt(stat + 1e-06) * gain_all.astype(jnp.float32)).astype(jnp.bfloat16)
    qkv = jnp.dot(normed, w_all, preferred_element_type=jnp.float32)
    query = qkv[:, :local_width]
    key_rows = qkv[:, local_width : 2 * local_width]
    value = qkv[:, 2 * local_width :].astype(jnp.bfloat16)
    qsum, ksum = lax.psum(
        (jnp.sum(query * query, axis=-1), jnp.sum(key_rows * key_rows, axis=-1)), "tp"
    )
    total_width = local_width * tp_count
    qnorm = (query * lax.rsqrt(qsum / total_width + 1e-06)[:, None] * qk_gain[0]).astype(
        jnp.bfloat16
    )
    knorm = (key_rows * lax.rsqrt(ksum / total_width + 1e-06)[:, None] * qk_gain[1]).astype(
        jnp.bfloat16
    )
    parity = lax.axis_index("group") % 2
    seam = jnp.where(parity == 0, rows - SHARE, 0).astype(jnp.int32)
    key_window = lax.dynamic_slice_in_dim(knorm, seam, SHARE, 0)
    id_window = lax.dynamic_slice_in_dim(request, seam, SHARE, 0)
    paired_keys, paired_ids = swapped((key_window, id_window), "group", 0)
    value_window = lax.dynamic_slice_in_dim(value, seam, SHARE, 0)
    paired_values = swapped(value_window, "group", 0)
    attended = attend(qnorm, knorm, value, paired_keys, paired_values, request, paired_ids)

    branch = jnp.zeros((rows, feat_local), jnp.float32)
    for step in range(tp_count):
        onward = from_next(attended, "tp") if step < tp_count - 1 else None
        part = lax.dot_general(
            attended,
            lax.dynamic_index_in_dim(w_o, (me_tp + step) % tp_count, 0, keepdims=False),
            (((1,), (1,)), ((), ())),
            preferred_element_type=jnp.float32,
        )
        branch = branch + part.astype(jnp.bfloat16).astype(jnp.float32)
        attended = onward
    mixed = (tokens.astype(jnp.float32) + layer_scale * branch).astype(jnp.bfloat16)

    capacity = max(2, 2 * rows // group_count)
    target = owner[:, 0]
    onehot = target[:, None] == jnp.arange(group_count, dtype=jnp.int32)[None, :]
    order = jnp.arange(rows, dtype=jnp.int32)
    before = (order[:, None] > order[None, :]).astype(jnp.bfloat16)
    ranks = jnp.dot(before, onehot.astype(jnp.bfloat16), preferred_element_type=jnp.float32)
    slot = jnp.sum(jnp.where(onehot, ranks, 0.0), axis=-1).astype(jnp.int32)
    place = target * capacity + slot
    inbox = route(place, mixed, group_count, capacity)
    return inbox[None]


def plane_shards(tokens, norm_gain, w_qkv, qk_gain, w_out, layer_scale, request, owner):
    count = lax.axis_size("group")
    capacity = max(2, 2 * tokens.shape[0] // count)
    return plane_call(
        tokens.T, jnp.stack([norm_gain.astype(F32), layer_scale]), w_qkv.transpose(1, 0, 2), qk_gain, w_out.T,
        request[None, :], owner.T, count, capacity,
    )[None]


def shards(*arrays):
    w_qkv = arrays[2]
    count, tp = lax.axis_size("group"), lax.axis_size("tp")
    whole_tiles = 2 * w_qkv.shape[0] % 16 == 0 and w_qkv.shape[2] % (2 * HD) == 0
    if tp == 2 and count == 16 and whole_tiles:
        return plane_shards(*arrays)
    return spread_shards(*arrays)


def solution(mesh):
    in_specs = (
        P("group", "tp"),
        P("tp"),
        P("group", None, "tp"),
        P(None, "tp"),
        P("tp", "group"),
        P("tp"),
        P("group"),
        P("group", None),
    )
    out_specs = P("group", None, None, "tp")
    return jax.shard_map(shards, mesh=mesh, in_specs=in_specs, out_specs=out_specs, check_vma=False)
```

```python
import functools
import math

import jax
import jax.numpy as jnp
from jax import lax
from jax.experimental import pallas as pl
from jax.experimental.pallas import tpu as pltpu
from jax.sharding import PartitionSpec as P

HD = 128
SHARE = 128


MESH = pl.DeviceIdType.MESH
BF16 = jnp.bfloat16
F32 = jnp.float32


def to_row(column):
    spread = jnp.broadcast_to(column, (column.shape[0], 128))
    return jnp.transpose(spread)[:8]


def to_column(row):
    spread = jnp.broadcast_to(row, (128, row.shape[1]))
    return jnp.transpose(spread)[:, :1]


def plane_kernel(
    levels, turned_ref, vectors_ref, w_ref, qk_gain_ref, wo_ref, request_ref, owner_ref, out_ref,
    tokens_ref, ids_ref, w_send, w_got, w_all, n_send, n_all, ids_all, sum_mine, sum_got, qk_mine, qk_got,
    qk_wide, qn, kn, vb, probs, att, wo_send, wo_got, wo_line, wo_all, att_all,
    ws_sem, wr_sem, is_sem, ir_sem, ss_sem, sr_sem, ns_sem, nr_sem, nf_sem, nfr_sem,
    right_sem, left_sem, chain_sem, core_s_sem, core_r_sem, qs_sem, qr_sem,
    wos_sem, wor_sem, uright_sem, uleft_sem, uchain_sem, uhere_sem, ux_sem, uxr_sem, uy_sem, uyr_sem, uc_sem, ucr_sem,
    as_sem, ar_sem, send_sem, recv_sem, keep_sem,
):
    group, t = lax.axis_index("group"), lax.axis_index("tp")
    z, y, c = group // 4, lax.rem(group // 2, 2), lax.rem(group, 2)
    rows, feat = tokens_ref.shape
    count, capacity = out_ref.shape[:2]
    slab = w_all.shape[1] // (2 * levels)
    depth = w_ref.shape[1]
    cols = w_all.shape[2]
    heads = cols // HD
    sub = rows // 2
    part = sub * 5 // 16
    half_cols = cols // 2
    edge_r, edge_l = z < levels - 1, z > 0

    def at(zz, yy, cc):
        return (zz * 2 + yy) * 2 + cc

    def remote(src, dst, send, recv, place, tt):
        return pltpu.make_async_remote_copy(
            src_ref=src, dst_ref=dst, send_sem=send, recv_sem=recv,
            device_id={"group": place, "tp": tt}, device_id_type=MESH,
        )

    barrier = pltpu.get_barrier_semaphore()

    @pl.loop(1, count)
    def _(step):
        pl.semaphore_signal(
            barrier, inc=1, device_id={"group": lax.rem(group + step, count), "tp": t}, device_id_type=MESH
        )

    for k in range(4):
        pl.semaphore_signal(
            barrier, inc=1, device_id={"group": z * 4 + k, "tp": lax.rem(t + 1, 2)}, device_id_type=MESH
        )

    for yy in range(2):
        w_send[yy, :, :depth, :] = w_ref[:, :, yy * cols : (yy + 1) * cols]

    half_out = wo_ref.shape[1] // 2
    for cc in range(2):
        wo_send[cc, :depth, :] = wo_ref[:, cc * half_out : (cc + 1) * half_out]
    ids_ref[...] = jnp.broadcast_to(request_ref[...].astype(F32), (8, rows))
    pl.semaphore_wait(barrier, count + 3)

    def pieces(yy):
        place = at(z, yy, y)
        copies = [
            remote(w_send.at[yy, j], w_got.at[c, j], ws_sem.at[yy, j], wr_sem.at[c, j], place, t) for j in range(3)
        ]
        return copies[:2] + [remote(ids_ref, ids_all.at[c], is_sem.at[yy], ir_sem.at[c], place, t)] + copies[2:]

    def kept(yy):
        copies = [pltpu.make_async_copy(w_send.at[yy, j], w_got.at[c, j], wr_sem.at[c, j]) for j in range(3)]
        return copies[:2] + [pltpu.make_async_copy(ids_ref, ids_all.at[c], ir_sem.at[c])] + copies[2:]

    def is_me(yy):
        return jnp.logical_and(y == yy, c == y)

    def start_pieces(which):
        for yy in range(2):
            @pl.when(is_me(yy))
            def _():
                for copy in kept(yy)[which]:
                    copy.start()

            @pl.when(jnp.logical_not(is_me(yy)))
            def _():
                for copy in pieces(yy)[which]:
                    copy.start()

    start_pieces(slice(0, 3))
    wo_swap = remote(wo_send.at[1 - c], wo_got, wos_sem, wor_sem, at(z, y, 1 - c), t)
    wo_swap.start()

    wide = turned_ref[...].astype(F32)
    sum_mine[...] = jnp.broadcast_to(jnp.sum(wide * wide, axis=0, keepdims=True), (8, rows))
    swap = remote(sum_mine, sum_got, ss_sem, sr_sem, group, lax.rem(t + 1, 2))
    swap.start()

    def rows_of(zz, cc):
        return pl.ds(pl.multiple_of((zz * 2 + cc) * slab, 16), slab)

    def piece(j, zz, cc):
        if j < 2:
            return w_all.at[j, rows_of(zz, cc), :]
        return w_all.at[2, rows_of(zz, cc), (j - 2) * half_cols : (j - 1) * half_cols]

    def go_right(j, zz):
        return remote(piece(j, zz, c), piece(j, zz, c), right_sem.at[j, zz], chain_sem.at[j, zz], group + 4, t)

    def go_left(j, zz):
        return remote(piece(j, zz, c), piece(j, zz, c), left_sem.at[j, zz], chain_sem.at[j, zz], group - 4, t)

    def go_core(j, zz):
        return remote(
            piece(j, zz, c), piece(j, zz, c), core_s_sem.at[j, zz], core_r_sem.at[j, zz],
            at(z, y, 1 - c), t,
        )

    def build(j):
        for cc in range(2):
            pltpu.make_async_copy(w_send.at[0, j], w_got.at[cc, j], wr_sem.at[cc, j]).wait()
        both = jnp.concatenate(
            [w_got[0, j].astype(F32)[:depth], w_got[1, j].astype(F32)[:depth]], axis=0
        )
        w_all[j, rows_of(z, c), :] = both.astype(BF16)

    def send_own(j):
        @pl.when(edge_r)
        def _():
            go_right(j, z).start()

        @pl.when(edge_l)
        def _():
            go_left(j, z).start()

        go_core(j, z).start()

    def arrive(j, d):
        @pl.when(z - d >= 0)
        def _():
            go_right(j, z - d).wait_recv()

            @pl.when(edge_r)
            def _():
                go_right(j, z - d).start()

            go_core(j, z - d).start()

        @pl.when(z + d < levels)
        def _():
            go_left(j, z + d).wait_recv()

            @pl.when(edge_l)
            def _():
                go_left(j, z + d).start()

            go_core(j, z + d).start()

    other_t = lax.rem(t + 1, 2)
    half_levels = levels // 2
    lanes_out = wo_all.shape[2] // 2

    def u_at(tt, i, yy, cc):
        return wo_all.at[
            tt, pl.ds(pl.multiple_of((i * 2 + yy) * slab, 16), slab),
            pl.ds(pl.multiple_of(cc * lanes_out, 128), lanes_out),
        ]

    def u_right(zz):
        return remote(wo_line.at[zz], wo_line.at[zz], uright_sem.at[zz], uchain_sem.at[zz], group + 4, t)

    def u_left(zz):
        return remote(wo_line.at[zz], wo_line.at[zz], uleft_sem.at[zz], uchain_sem.at[zz], group - 4, t)

    def u_here(i):
        return pltpu.make_async_copy(wo_line.at[t * half_levels + i], u_at(t, i, y, c), uhere_sem.at[i])

    def u_across(i):
        zz = other_t * half_levels + i
        return remote(wo_line.at[zz], u_at(t, i, y, c), ux_sem.at[i], uxr_sem.at[i], group, other_t)

    def u_over(tt, i, line):
        src = wo_line.at[t * half_levels + i] if line else u_at(tt, i, y, c)
        return remote(src, u_at(tt, i, y, c), uy_sem.at[tt, i], uyr_sem.at[tt, i], at(z, 1 - y, c), t)

    def u_core(tt, i, yy, line):
        src = wo_line.at[t * half_levels + i] if line else u_at(tt, i, yy, c)
        return remote(
            src, u_at(tt, i, yy, c), uc_sem.at[tt, i, yy], ucr_sem.at[tt, i, yy], at(z, y, 1 - c), t
        )

    def u_hops(zz):
        i = lax.rem(zz, half_levels)
        wanted = zz // half_levels == t

        @pl.when(wanted)
        def _():
            u_here(i).start()
            u_over(t, i, True).start()
            u_core(t, i, y, True).start()

        @pl.when(jnp.logical_not(wanted))
        def _():
            u_across(i).start()

    def u_own():
        wo_swap.wait()
        mine, theirs = wo_send[c].astype(F32)[:depth], wo_got[...].astype(F32)[:depth]
        low, high = jnp.where(c == 0, mine, theirs), jnp.where(c == 0, theirs, mine)
        wo_line[z] = jnp.concatenate([low, high], axis=0).astype(BF16)

        @pl.when(edge_r)
        def _():
            u_right(z).start()

        @pl.when(edge_l)
        def _():
            u_left(z).start()

    def u_arrive(d):
        @pl.when(z - d >= 0)
        def _():
            u_right(z - d).wait_recv()

            @pl.when(edge_r)
            def _():
                u_right(z - d).start()

        @pl.when(z + d < levels)
        def _():
            u_left(z + d).wait_recv()

            @pl.when(edge_l)
            def _():
                u_left(z + d).start()

    def u_hops_of(d):
        @pl.when(z - d >= 0)
        def _():
            u_hops(z - d)

        @pl.when(z + d < levels)
        def _():
            u_hops(z + d)

    def ux_take(d):
        for zz in ((z - d, z + d) if d else (z,)):
            here = jnp.logical_and(jnp.logical_and(zz >= 0, zz < levels), (zz + levels) // half_levels == t + 2)

            @pl.when(here)
            def _():
                i = lax.rem(zz, half_levels)
                ref = u_at(other_t, i, y, c)
                pltpu.make_async_copy(ref, ref, uxr_sem.at[i]).wait()
                u_over(other_t, i, False).start()
                u_core(other_t, i, y, False).start()

    inner = jnp.logical_and(edge_l, edge_r)
    outer = jnp.logical_not(inner)
    def own_first():
        for j in range(2):
            build(j)
            send_own(j)

    pl.when(c == y)(own_first)

    swap.wait()
    whole = sum_mine[...] + sum_got[...]
    factor = to_column(lax.rsqrt(whole[:1] / (2 * feat) + 1e-06))

    def n_rows(cc, start, size):
        return pl.ds(pl.multiple_of(cc * rows + start, 16), size)

    def n_copies(s):
        src = n_send.at[s * sub : (s + 1) * sub, :]
        dst = n_all.at[t, n_rows(c, s * sub, sub), :]
        recv = nr_sem.at[t, c, s]
        return (
            remote(src, dst, ns_sem.at[0, s], recv, at(z, y, y), lax.rem(t + 1, 2)),
            remote(src, dst, ns_sem.at[1, s], recv, at(z, 1 - y, y), t),
            remote(src, dst, ns_sem.at[2, s], recv, at(z, y, y), t),
            pltpu.make_async_copy(src, dst, recv),
        )

    start_pieces(slice(3, 4))
    for s in range(2):
        span = slice(s * sub, (s + 1) * sub)
        tokens_ref[span, :] = jnp.transpose(turned_ref[:, span].astype(F32)).astype(BF16)
        n_send[span, :] = (
            tokens_ref[span, :].astype(F32) * factor[span] * vectors_ref[:1, :]
        ).astype(BF16)
        n_x, n_y, n_core, n_here = n_copies(s)
        n_x.start()
        n_y.start()

        @pl.when(c == y)
        def _():
            n_here.start()

        @pl.when(c != y)
        def _():
            n_core.start()

    def n_wait(tt, cc, s):
        ref = n_all.at[tt, n_rows(cc, s * sub, sub), :]
        pltpu.make_async_copy(ref, ref, nr_sem.at[tt, cc, s]).wait()


    def forward_y(cc, s):
        ref = n_all.at[other_t, n_rows(cc, s * sub, part), :]
        return remote(ref, ref, nf_sem.at[cc, s], nfr_sem.at[0, cc, s], at(z, 1 - y, c), t)

    def forward_x(cc, s):
        ref = n_all.at[t, n_rows(cc, s * sub + part, sub - part), :]
        return remote(ref, ref, nf_sem.at[cc, s], nfr_sem.at[1, cc, s], group, other_t)

    def n_forward(s):
        for cc in range(2):
            @pl.when(c == y)
            def _():
                n_wait(other_t, cc, s)
                forward_y(cc, s).start()

            @pl.when(c != y)
            def _():
                n_wait(t, cc, s)
                forward_x(cc, s).start()

    pl.when(c != y)(own_first)
    arrive(0, 1)
    arrive(1, 1)
    u_own()
    build(2)

    @pl.when(outer)
    def _():
        send_own(2)
        send_own(3)

    n_forward(0)
    arrive(0, 2)
    arrive(1, 2)

    @pl.when(inner)
    def _():
        u_arrive(1)

    n_forward(1)
    u_hops(z)

    @pl.when(inner)
    def _():
        send_own(2)
        send_own(3)

    def n_rest(s):
        for cc in range(2):
            @pl.when(c == y)
            def _():
                n_wait(t, cc, s)

            @pl.when(c != y)
            def _():
                for way, (start, size) in enumerate(((0, part), (part, sub - part))):
                    ref = n_all.at[other_t, n_rows(cc, s * sub + start, size), :]
                    pltpu.make_async_copy(ref, ref, nfr_sem.at[way, cc, s]).wait()

    def core_wait(j):
        for zz in range(levels):
            remote(
                piece(j, zz, 1 - c), piece(j, zz, 1 - c), core_s_sem.at[j, zz], core_r_sem.at[j, zz],
                at(z, y, 1 - c), t,
            ).wait_recv()

    def project(j, start, size, lanes):
        return jnp.dot(
            n_all[0, pl.ds(start, size), :], w_all[j, :feat, lanes], preferred_element_type=F32
        ) + jnp.dot(n_all[1, pl.ds(start, size), :], w_all[j, feat:, lanes], preferred_element_type=F32)

    arrive(0, 3)
    arrive(1, 3)
    core_wait(0)
    core_wait(1)
    for s in range(2):
        n_rest(s)
        if s:
            @pl.when(inner)
            def _():
                u_hops_of(1)
                arrive(2, 1)
                arrive(3, 1)

        @pl.loop(0, 2)
        def _(cc):
            start = pl.multiple_of(cc * rows + s * sub, sub)
            for j in range(2):
                out = project(j, start, sub, slice(None))
                qk_wide[j, pl.ds(start, sub), :] = out
                qk_mine[j, :, pl.ds(start, sub)] = to_row(jnp.sum(out * out, axis=-1, keepdims=True))

    def stat_swap(k):
        return remote(
            qk_mine, qk_got.at[k - 1], qs_sem.at[k - 1], qr_sem.at[k - 1],
            at(z, lax.rem(y + k % 2, 2), c), lax.rem(t + k // 2, 2),
        )

    for k in range(1, 4):
        stat_swap(k).start()
    ux_take(0)

    @pl.when(inner)
    def _():
        arrive(2, 2)

    @pl.when(outer)
    def _():
        u_arrive(1)
        u_hops_of(1)

    for k in range(1, 4):
        stat_swap(k).wait()
    stats = qk_mine[...] + qk_got[0] + qk_got[1] + qk_got[2]
    factors = lax.rsqrt(stats / (4 * cols) + 1e-06)
    for j, ref in ((0, qn), (1, kn)):
        column = to_column(factors[j, :1])
        near = qk_gain_ref[j : j + 1, :cols]
        far = qk_gain_ref[j : j + 1, cols:]
        gains = jnp.where(y == 0, near, far)
        ref[...] = (qk_wide[j] * column * gains).astype(BF16)

    for cc in range(2):
        pltpu.make_async_copy(ids_ref, ids_all.at[cc], ir_sem.at[cc]).wait()
    seam = rows + SHARE
    scale = 1.0 / math.sqrt(HD)
    ids = jnp.concatenate([ids_all[0, :1], ids_all[1, :1]], axis=1)
    for half in range(2):
        first = half * (rows - SHARE)
        same = to_column(ids[:, half * rows : (half + 1) * rows]) == ids[:, first : first + seam]

        @pl.loop(0, heads)
        def _(h):
            lanes = pl.ds(pl.multiple_of(h * HD, HD), HD)
            scores = lax.dot_general(
                qn[half * rows : (half + 1) * rows, lanes], kn[first : first + seam, lanes],
                (((1,), (1,)), ((), ())), preferred_element_type=F32,
            ) * scale
            scores = jnp.where(same, scores, -jnp.inf)
            expo = jnp.exp(scores - jnp.max(scores, axis=-1, keepdims=True))
            share = 1.0 / jnp.sum(expo, axis=-1, keepdims=True)
            probs[half, h] = (expo * share).astype(BF16)

        if half == 0:
            @pl.when(inner)
            def _():
                arrive(3, 2)
                u_arrive(2)

            @pl.when(outer)
            def _():
                u_arrive(2)
                u_hops_of(2)

            ux_take(1)
        else:
            @pl.when(outer)
            def _():
                ux_take(2)

    def att_copy(dt, half, j):
        src = att.at[half * rows : (half + 1) * rows, j * half_cols : (j + 1) * half_cols]
        dst = att_all.at[t, :, pl.ds(pl.multiple_of(y * cols + j * half_cols, 128), half_cols)]
        mine = jnp.logical_and(y == c, c == half)
        recv = ar_sem.at[t, y, j]
        away = remote(src, dst, as_sem.at[dt, half, j], recv, at(z, c, half), lax.rem(t + dt, 2))
        return mine, away, pltpu.make_async_copy(src, dst, recv)

    def uy_take(i):
        for tt in range(2):
            ref = u_at(tt, i, 1 - y, c)
            pltpu.make_async_copy(ref, ref, uyr_sem.at[tt, i]).wait()
            u_core(tt, i, 1 - y, False).start()

    def u_ready(i):
        u_here(i).wait()
        for tt in range(2):
            for yy in range(2):
                ref = u_at(tt, i, yy, 1 - c)
                pltpu.make_async_copy(ref, ref, ucr_sem.at[tt, i, yy]).wait()

    upper = z // half_levels
    for j in range(2):
        @pl.when(outer)
        def _():
            for d in range(1, levels):
                arrive(2 + j, d)

        core_wait(2 + j)
        span = slice(j * half_cols, (j + 1) * half_cols)

        @pl.loop(0, 2)
        def _(i):
            start = pl.multiple_of(i * rows, rows)
            vb[pl.ds(start, rows), span] = project(2, start, rows, span).astype(BF16)

        for half in range(2):
            first = half * (rows - SHARE)
            for h in range(j * heads // 2, (j + 1) * heads // 2):
                lanes = slice(h * HD, (h + 1) * HD)
                att[half * rows : (half + 1) * rows, lanes] = jnp.dot(
                    probs[half, h], vb[first : first + seam, lanes], preferred_element_type=F32
                ).astype(BF16)

            att_copy(1, half, j)[1].start()
            mine, away, here = att_copy(0, half, j)

            @pl.when(mine)
            def _():
                here.start()

            @pl.when(jnp.logical_not(mine))
            def _():
                away.start()

        if j == 0:
            uy_take(upper)
        else:
            @pl.when(inner)
            def _():
                u_hops_of(2)

            @pl.when(outer)
            def _():
                u_arrive(3)
                u_hops_of(3)

    target = owner_ref[...]
    named = lax.broadcasted_iota(jnp.int32, (count, rows), 0) == target
    earlier = lax.broadcasted_iota(jnp.int32, (rows, rows), 0) < lax.broadcasted_iota(jnp.int32, (rows, rows), 1)
    ranks = jnp.dot(
        named.astype(F32).astype(BF16), earlier.astype(F32).astype(BF16), preferred_element_type=F32
    )
    slot = jnp.sum(jnp.where(named, ranks, 0.0), axis=0, keepdims=True).astype(jnp.int32)
    place = target * capacity + slot

    for tt in range(2):
        for yy in range(2):
            for j in range(2):
                ref = att_all.at[tt, :, yy * cols + j * half_cols : yy * cols + (j + 1) * half_cols]
                pltpu.make_async_copy(ref, ref, ar_sem.at[tt, yy, j]).wait()

    u_ready(upper)

    for s in range(2):
        n_x, n_y, n_core, n_here = n_copies(s)
        n_x.wait_send()
        n_y.wait_send()

        @pl.when(c != y)
        def _():
            n_core.wait_send()

        for cc in range(2):
            @pl.when(c == y)
            def _():
                forward_y(cc, s).wait_send()

            @pl.when(c != y)
            def _():
                forward_x(cc, s).wait_send()

    mixed = n_send

    def slots_of(owner_group, lanes):
        return n_all.at[0, pl.ds(pl.multiple_of(owner_group * capacity, 16), capacity), lanes]

    def sending(f, lanes, owner_group):
        return pltpu.make_async_remote_copy(
            src_ref=slots_of(owner_group, lanes), dst_ref=out_ref.at[group, :, lanes],
            send_sem=send_sem.at[f, owner_group], recv_sem=recv_sem.at[group],
            device_id={"group": owner_group, "tp": t}, device_id_type=MESH,
        )

    def keeping(f, lanes):
        return pltpu.make_async_copy(slots_of(group, lanes), out_ref.at[group, :, lanes], keep_sem.at[f])

    middle = feat // 2
    below, above = middle // 128 * 128, -(-middle // 128) * 128
    spans = (
        (slice(0, below), slice(below, feat)),
        (slice(above, feat), slice(0, above)),
    )
    planes = (3 - z, lax.rem(z + 2, 4), z + 1 - 2 * lax.rem(z, 2), z)

    def finish(f, lanes):
        total = jnp.zeros((rows, lanes.stop - lanes.start), F32)
        for tt in range(2):
            term = lax.dot_general(
                att_all[tt], wo_all[tt, lanes, :], (((1,), (1,)), ((), ())), preferred_element_type=F32
            )
            total += term.astype(BF16).astype(F32)
        mixed[:, lanes] = (tokens_ref[:, lanes].astype(F32) + vectors_ref[1:, lanes] * total).astype(BF16)
        for plane in planes:
            slots = lax.broadcasted_iota(jnp.int32, (4 * capacity, rows), 0) + plane * 4 * capacity
            chosen = (slots == place).astype(F32).astype(BF16)
            picked = jnp.dot(chosen, mixed[:, lanes], preferred_element_type=F32).astype(BF16)
            n_all[0, pl.ds(pl.multiple_of(plane * 4 * capacity, 16), 4 * capacity), lanes] = picked
            for k in range(4):
                peer = plane * 4 + lax.rem(k + group, 4)

                @pl.when(peer == group)
                def _():
                    keeping(f, lanes).start()

                @pl.when(peer != group)
                def _():
                    sending(f, lanes, peer).start()

    def left(f, lanes):
        @pl.loop(1, count)
        def _(step):
            sending(f, lanes, lax.rem(group + step, count)).wait_send()

        keeping(f, lanes).wait()

    for f in range(2):
        if f:
            @pl.when(inner)
            def _():
                ux_take(2)

            ux_take(3)
            uy_take(1 - upper)
            u_ready(1 - upper)

        for which in range(2):
            @pl.when(upper == which)
            def _():
                finish(f, spans[which][f])

    for f in range(2):
        for which in range(2):
            @pl.when(upper == which)
            def _():
                left(f, spans[which][f])

    @pl.loop(1, count)
    def _(step):
        ref = out_ref.at[lax.rem(group + step, count)]
        pltpu.make_async_copy(ref, ref, recv_sem.at[lax.rem(group + step, count)]).wait()

    for yy in range(2):
        @pl.when(jnp.logical_not(is_me(yy)))
        def _():
            for copy in pieces(yy):
                copy.wait_send()

    for half in range(2):
        for j in range(2):
            att_copy(1, half, j)[1].wait_send()
            mine, away, here = att_copy(0, half, j)

            @pl.when(jnp.logical_not(mine))
            def _():
                away.wait_send()

    for zz in range(levels):
        @pl.when(jnp.logical_and(zz <= z, edge_r))
        def _():
            u_right(zz).wait_send()

        @pl.when(jnp.logical_and(zz >= z, edge_l))
        def _():
            u_left(zz).wait_send()

    for i in range(half_levels):
        u_across(i).wait_send()
        for tt in range(2):
            u_over(tt, i, False).wait_send()
            for yy in range(2):
                u_core(tt, i, yy, False).wait_send()

    for j in range(4):
        for zz in range(levels):
            @pl.when(jnp.logical_and(zz <= z, edge_r))
            def _():
                go_right(j, zz).wait_send()

            @pl.when(jnp.logical_and(zz >= z, edge_l))
            def _():
                go_left(j, zz).wait_send()

            go_core(j, zz).wait_send()


def plane_call(turned, vectors, w, qk_gain, wo, request, owner, count, capacity):
    feat, rows = turned.shape
    depth, width = w.shape[1], w.shape[2]
    levels, cols = count // 4, width // 2
    heads = cols // HD
    padded = -(-depth // 16) * 16
    seam = rows + SHARE
    dma = pltpu.SemaphoreType.DMA
    vmem = pl.BlockSpec(memory_space=pltpu.VMEM)
    return pl.pallas_call(
        functools.partial(plane_kernel, levels),
        name="plane",
        out_shape=jax.ShapeDtypeStruct((count, capacity, feat), BF16),
        in_specs=[vmem] * 7,
        out_specs=pl.BlockSpec(memory_space=pl.ANY),
        scratch_shapes=[
            pltpu.VMEM((rows, feat), BF16),
            pltpu.VMEM((8, rows), F32),
            pltpu.VMEM((2, 3, padded, cols), BF16),
            pltpu.VMEM((2, 3, padded, cols), BF16),
            pltpu.VMEM((3, 2 * feat, cols), BF16),
            pltpu.VMEM((rows, feat), BF16),
            pltpu.VMEM((2, 2 * rows, feat), BF16),
            pltpu.VMEM((2, 8, rows), F32),
            pltpu.VMEM((8, rows), F32),
            pltpu.VMEM((8, rows), F32),
            pltpu.VMEM((2, 8, 2 * rows), F32),
            pltpu.VMEM((3, 2, 8, 2 * rows), F32),
            pltpu.VMEM((2, 2 * rows, cols), F32),
            pltpu.VMEM((2 * rows, cols), BF16),
            pltpu.VMEM((2 * rows, cols), BF16),
            pltpu.VMEM((2 * rows, cols), BF16),
            pltpu.VMEM((2, heads, rows, seam), BF16),
            pltpu.VMEM((2 * rows, cols), BF16),
            pltpu.VMEM((2, padded, width // 2), BF16),
            pltpu.VMEM((padded, width // 2), BF16),
            pltpu.VMEM((levels, 2 * depth, width // 2), BF16),
            pltpu.VMEM((2, feat, width), BF16),
            pltpu.VMEM((2, rows, width), BF16),
            dma((2, 3)), dma((2, 3)), dma((2,)), dma((2,)), dma, dma,
            dma((3, 2)), dma((2, 2, 2)), dma((2, 2)), dma((2, 2, 2)),
            dma((4, levels)), dma((4, levels)), dma((4, levels)), dma((4, levels)), dma((4, levels)),
            dma((3,)), dma((3,)),
            dma, dma, dma((levels,)), dma((levels,)), dma((levels,)), dma((2,)), dma((2,)), dma((2,)),
            dma((2, 2)), dma((2, 2)), dma((2, 2, 2)), dma((2, 2, 2)),
            dma((2, 2, 2)), dma((2, 2, 2)), dma((2, count)), dma((count,)), dma((2,)),
        ],
        compiler_params=pltpu.CompilerParams(
            collective_id=1, has_side_effects=True, vmem_limit_bytes=60 * 2**20
        ),
        cost_estimate=pl.CostEstimate(
            flops=20 * rows * feat * width, transcendentals=2 * heads * rows * seam,
            bytes_accessed=8 * 2**20,
        ),
    )(turned, vectors, w, qk_gain, wo, request, owner)


def swapped(value, axis, apart):
    mask = 2**apart
    pairs = [(source, source ^ mask) for source in range(lax.axis_size(axis))]
    return lax.ppermute(value, axis, pairs)


def from_next(value, axis):
    count = lax.axis_size(axis)
    return lax.ppermute(value, axis, [((i + 1) % count, i) for i in range(count)])


def attend_kernel(q_ref, k_ref, v_ref, kp_ref, vp_ref, row_ref, own_ref, pair_ref, out_ref):
    query = q_ref[...]
    over = (((1,), (1,)), ((), ()))
    scale = 1.0 / math.sqrt(HD)
    near = lax.dot_general(query, k_ref[...], over, preferred_element_type=jnp.float32) * scale
    far = lax.dot_general(query, kp_ref[...], over, preferred_element_type=jnp.float32) * scale
    near = jnp.where(row_ref[...] == own_ref[...], near, -jnp.inf)
    far = jnp.where(row_ref[...] == pair_ref[...], far, -jnp.inf)
    top = jnp.maximum(
        jnp.max(near, axis=-1, keepdims=True), jnp.max(far, axis=-1, keepdims=True)
    )
    near, far = jnp.exp(near - top), jnp.exp(far - top)
    share = 1.0 / (jnp.sum(near, axis=-1, keepdims=True) + jnp.sum(far, axis=-1, keepdims=True))
    near, far = (near * share).astype(jnp.bfloat16), (far * share).astype(jnp.bfloat16)
    total = jnp.dot(near, v_ref[...], preferred_element_type=jnp.float32)
    total += jnp.dot(far, vp_ref[...], preferred_element_type=jnp.float32)
    out_ref[...] = total.astype(jnp.bfloat16)


def attend(query, keys, values, paired_keys, paired_values, ids, paired_ids):
    rows, width = query.shape
    seam = paired_keys.shape[0]
    block = pl.BlockSpec((rows, HD), lambda h: (0, h))
    seam_block = pl.BlockSpec((seam, HD), lambda h: (0, h))
    fixed = lambda shape: pl.BlockSpec(shape, lambda h: (0, 0))
    return pl.pallas_call(
        attend_kernel,
        grid=(width // HD,),
        out_shape=jax.ShapeDtypeStruct((rows, width), jnp.bfloat16),
        in_specs=[
            block, block, block, seam_block, seam_block,
            fixed((rows, 1)), fixed((1, rows)), fixed((1, seam)),
        ],
        out_specs=block,
        compiler_params=pltpu.CompilerParams(vmem_limit_bytes=32 * 2**20),
        cost_estimate=pl.CostEstimate(
            flops=4 * rows * (rows + seam) * width,
            transcendentals=rows * (rows + seam) * width // HD,
            bytes_accessed=8 * rows * width,
        ),
    )(
        query, keys, values, paired_keys, paired_values,
        ids[:, None], ids[None, :], paired_ids[None, :],
    )


def route_kernel(count, place_ref, mixed_ref, out_ref, outbox, send_sem, recv_sem, keep_sem):
    me = lax.axis_index("group")
    capacity = outbox.shape[1]
    rows = mixed_ref.shape[0]
    barrier = pltpu.get_barrier_semaphore()

    @pl.loop(1, count)
    def _(step):
        pl.semaphore_signal(
            barrier, inc=1, device_id={"group": lax.rem(me + step, count)},
            device_id_type=pl.DeviceIdType.MESH,
        )

    pl.semaphore_wait(barrier, count - 1)

    def pick(owner):
        slots = lax.broadcasted_iota(jnp.int32, (capacity, rows), 0) + owner * capacity
        select = (slots == place_ref[...]).astype(jnp.float32).astype(jnp.bfloat16)
        return jnp.dot(select, mixed_ref[...], preferred_element_type=jnp.float32).astype(
            jnp.bfloat16
        )

    def sending(step):
        ahead = 1 + lax.rem(step - 1 + count // 2 - 1, count - 1)
        peer = lax.rem(me + ahead, count)
        return peer, pltpu.make_async_remote_copy(
            src_ref=outbox.at[step],
            dst_ref=out_ref.at[me],
            send_sem=send_sem.at[step],
            recv_sem=recv_sem.at[me],
            device_id={"group": peer},
            device_id_type=pl.DeviceIdType.MESH,
        )

    @pl.loop(1, count)
    def _(step):
        peer, copy = sending(step)
        outbox[step] = pick(peer)
        copy.start()

    outbox[0] = pick(me)
    keep = pltpu.make_async_copy(outbox.at[0], out_ref.at[me], keep_sem)
    keep.start()

    @pl.loop(1, count)
    def _(step):
        source = lax.rem(me + step, count)
        pltpu.make_async_remote_copy(
            src_ref=outbox.at[step],
            dst_ref=out_ref.at[source],
            send_sem=send_sem.at[step],
            recv_sem=recv_sem.at[source],
            device_id={"group": source},
            device_id_type=pl.DeviceIdType.MESH,
        ).wait()

    keep.wait()


def route(place, mixed, count, capacity):
    rows, feat = mixed.shape
    return pl.pallas_call(
        lambda *refs: route_kernel(count, *refs),
        name="route",
        out_shape=jax.ShapeDtypeStruct((count, capacity, feat), jnp.bfloat16),
        in_specs=[pl.BlockSpec(memory_space=pltpu.VMEM)] * 2,
        out_specs=pl.BlockSpec(memory_space=pl.ANY),
        scratch_shapes=[
            pltpu.VMEM((count, capacity, feat), jnp.bfloat16),
            pltpu.SemaphoreType.DMA((count,)),
            pltpu.SemaphoreType.DMA((count,)),
            pltpu.SemaphoreType.DMA,
        ],
        compiler_params=pltpu.CompilerParams(
            collective_id=0, has_side_effects=True, vmem_limit_bytes=32 * 2**20
        ),
        cost_estimate=pl.CostEstimate(
            flops=2 * count * capacity * rows * feat,
            transcendentals=0,
            bytes_accessed=4 * count * capacity * feat,
        ),
    )(place[None, :], mixed)


def spread_shards(tokens, norm_gain, w_qkv, qk_gain, w_out, layer_scale, request, owner):
    rows, feat_local = tokens.shape
    tp_count = lax.axis_size("tp")
    group_count = lax.axis_size("group")
    local_width = w_qkv.shape[2]
    head_count = local_width // HD
    me_tp = lax.axis_index("tp")
    w_all = lax.all_gather(
        w_qkv.reshape(w_qkv.shape[0], 3 * local_width), "group", axis=0, tiled=True
    )
    whole = jnp.zeros((rows, feat_local * tp_count), jnp.bfloat16)
    gain_all = jnp.zeros((1, feat_local * tp_count), jnp.bfloat16)
    piece, gain = tokens, norm_gain.reshape(1, feat_local)
    for step in range(tp_count):
        at = ((me_tp + step) % tp_count) * feat_local
        whole = lax.dynamic_update_slice(whole, piece, (0, at))
        gain_all = lax.dynamic_update_slice(gain_all, gain, (0, at))
        if step < tp_count - 1:
            piece, gain = from_next(piece, "tp"), from_next(gain, "tp")
    whole, late_out = lax.optimization_barrier((whole, w_out))
    per = group_count // tp_count
    pairs = []
    for g in range(group_count):
        for b in range(tp_count):
            t, j = g // per, g % per
            to_g = b * per + j
            pairs.append((g * tp_count + b, to_g * tp_count + t))
    w_piece = lax.ppermute(late_out.T, ("group", "tp"), pairs)
    w_o = lax.all_gather(w_piece, "group", axis=0, tiled=True)
    w_o = w_o.reshape(tp_count, feat_local, local_width)
    xwide = whole.astype(jnp.float32)
    stat = jnp.mean(xwide * xwide, axis=-1, keepdims=True)
    normed = (xwide * lax.rsqrt(stat + 1e-06) * gain_all.astype(jnp.float32)).astype(jnp.bfloat16)
    qkv = jnp.dot(normed, w_all, preferred_element_type=jnp.float32)
    query = qkv[:, :local_width]
    key_rows = qkv[:, local_width : 2 * local_width]
    value = qkv[:, 2 * local_width :].astype(jnp.bfloat16)
    qsum, ksum = lax.psum(
        (jnp.sum(query * query, axis=-1), jnp.sum(key_rows * key_rows, axis=-1)), "tp"
    )
    total_width = local_width * tp_count
    qnorm = (query * lax.rsqrt(qsum / total_width + 1e-06)[:, None] * qk_gain[0]).astype(
        jnp.bfloat16
    )
    knorm = (key_rows * lax.rsqrt(ksum / total_width + 1e-06)[:, None] * qk_gain[1]).astype(
        jnp.bfloat16
    )
    parity = lax.axis_index("group") % 2
    seam = jnp.where(parity == 0, rows - SHARE, 0).astype(jnp.int32)
    key_window = lax.dynamic_slice_in_dim(knorm, seam, SHARE, 0)
    id_window = lax.dynamic_slice_in_dim(request, seam, SHARE, 0)
    paired_keys, paired_ids = swapped((key_window, id_window), "group", 0)
    value_window = lax.dynamic_slice_in_dim(value, seam, SHARE, 0)
    paired_values = swapped(value_window, "group", 0)
    attended = attend(qnorm, knorm, value, paired_keys, paired_values, request, paired_ids)

    branch = jnp.zeros((rows, feat_local), jnp.float32)
    for step in range(tp_count):
        onward = from_next(attended, "tp") if step < tp_count - 1 else None
        part = lax.dot_general(
            attended,
            lax.dynamic_index_in_dim(w_o, (me_tp + step) % tp_count, 0, keepdims=False),
            (((1,), (1,)), ((), ())),
            preferred_element_type=jnp.float32,
        )
        branch = branch + part.astype(jnp.bfloat16).astype(jnp.float32)
        attended = onward
    mixed = (tokens.astype(jnp.float32) + layer_scale * branch).astype(jnp.bfloat16)

    capacity = max(2, 2 * rows // group_count)
    target = owner[:, 0]
    onehot = target[:, None] == jnp.arange(group_count, dtype=jnp.int32)[None, :]
    order = jnp.arange(rows, dtype=jnp.int32)
    before = (order[:, None] > order[None, :]).astype(jnp.bfloat16)
    ranks = jnp.dot(before, onehot.astype(jnp.bfloat16), preferred_element_type=jnp.float32)
    slot = jnp.sum(jnp.where(onehot, ranks, 0.0), axis=-1).astype(jnp.int32)
    place = target * capacity + slot
    inbox = route(place, mixed, group_count, capacity)
    return inbox[None]


def plane_shards(tokens, norm_gain, w_qkv, qk_gain, w_out, layer_scale, request, owner):
    count = lax.axis_size("group")
    capacity = max(2, 2 * tokens.shape[0] // count)
    return plane_call(
        tokens.T, jnp.stack([norm_gain.astype(F32), layer_scale]), w_qkv.transpose(1, 0, 2), qk_gain, w_out.T,
        request[None, :], owner.T, count, capacity,
    )[None]


def shards(*arrays):
    w_qkv = arrays[2]
    count, tp = lax.axis_size("group"), lax.axis_size("tp")
    whole_tiles = 2 * w_qkv.shape[0] % 16 == 0 and w_qkv.shape[2] % (2 * HD) == 0
    if tp == 2 and count == 16 and whole_tiles:
        return plane_shards(*arrays)
    return spread_shards(*arrays)


def solution(mesh):
    in_specs = (
        P("group", "tp"),
        P("tp"),
        P("group", None, "tp"),
        P(None, "tp"),
        P("tp", "group"),
        P("tp"),
        P("group"),
        P("group", None),
    )
    out_specs = P("group", None, None, "tp")
    return jax.shard_map(shards, mesh=mesh, in_specs=in_specs, out_specs=out_specs, check_vma=False)
```
